128 devices in a mesh: ctx: 16 (over z, x), tp: 8 (over y, core).
Axes of the slice: x: 4, y: 4, z: 4, core: 2. Of those that a mesh axis runs over, the one named last changes fastest.
Arguments:
- x_in: bfloat16 [8192, 8192], P('ctx', 'tp'), may hold values from -6 to 6
- bc_in: bfloat16 [8192, 256], P('ctx'), may hold values from -6 to 6
- z_in: bfloat16 [8192, 8192], P('ctx', 'tp'), may hold values from -6 to 6
- codes: int32 [8192, 64], P('ctx', 'tp'), may hold values from 0 to 63
- head_rate: float32 [64], P('tp'), may hold values from 0.25 to 1
- conv_x: float32 [4, 8192], P(None, 'tp'), may hold values from -3 to 3
- conv_bc: float32 [4, 256], replicated, may hold values from -3 to 3
- bias_x: float32 [8192], P('tp'), may hold values from -2 to 2
- bias_bc: float32 [256], replicated, may hold values from -2 to 2
- skip: float32 [64], P('tp'), may hold values from 0.5 to 1.5
- norm_gain: float32 [8192], P('tp'), may hold values from 0.5 to 1.5
- w_out: bfloat16 [8192, 8192], P('tp'), may hold values from -0.09375 to 0.09375
Outputs:
- mixed: bfloat16 [8192, 8192], P('ctx', 'tp')
The draws below stay inside these ranges and needn't reach their ends.
All inputs are finite; a program needn't handle non-finite values.
Results may differ from the reference program's by a relative error of at most 0.019.
Values may be sent and summed in bfloat16 or wider, within the bound.
No kernel may reach another device: no remote copies, remote signals or barrier semaphores. Data moves between devices by JAX's collectives and lax.ppermute only.
A program may use at most 128 MiB of HBM per device.

```python
import math
import jax
import jax.numpy as jnp
from jax import lax

DM = 8192
P_SIZE = 128
N = 128
TOK_DEV = 512
HEADS = 64
SEQ = 8192
N_TP = 8


def draw_codes(key, part):
    key_cap, key_raw = jax.random.split(jax.random.fold_in(key, 7))
    shard_count = SEQ // TOK_DEV
    caps = jax.random.randint(key_cap, (shard_count, 1, HEADS), 0, 64)
    raw = jax.random.randint(key_raw, (shard_count, TOK_DEV, HEADS), 0, 1048576)
    values = (raw % (caps + 1)).reshape(SEQ, HEADS)
    values = values.at[0].set(63)
    values = values.at[1].set(0)
    return values.astype(jnp.int32)


def strengthened(result, stream_key, source, target, blocks, factor):
    owner, partner = [(jnp.arange(result.shape[axis_at]) // (result.shape[axis_at] // blocks)).reshape([-1 if axis == axis_at else 1 for axis in range(result.ndim)]) for axis_at in (source, target)]
    chosen = jax.random.permutation(stream_key, blocks)[partner]
    strong = (owner == chosen) | (owner == (partner + blocks // 2) % blocks)
    return jnp.where(strong, factor * result, result)


def levels(rng, dims, cuts, low, top_value):
    gain = 1.0
    for position, shards_of in cuts:
        steps = jax.random.uniform(jax.random.fold_in(jax.random.fold_in(rng, 6), position), (shards_of,), jnp.float32, low / len(cuts), top_value / len(cuts))
        gain = gain * jnp.repeat(jnp.exp(steps), dims[position] // shards_of).reshape((-1,) + (1,) * (len(dims) - 1 - position))
    return gain


def normal_values(key, extent, deviation, reach, cuts=(), kind=jnp.bfloat16):
    entries = jax.random.normal(key, extent, jnp.float32) * deviation
    if len(cuts) > 0:
        entries = levels(key, extent, cuts, -0.22, 0.18) * entries
    return jnp.clip(entries, min=-reach, max=reach).astype(kind)


def heavy_noise(key, extent, width, bound, shards, heavy, kind=jnp.bfloat16):
    values = width * jax.random.normal(key, extent, jnp.float32)
    if shards:
        values = values * levels(key, extent, shards, -0.22, 0.18)
    return jnp.clip(strengthened(values, jax.random.fold_in(key, 3), *heavy), -bound, bound).astype(kind)


def setup_inputs(seed: int = 0) -> dict:
    arg_keys = jax.random.split(jax.random.key(seed), 13)
    x_in = normal_values(arg_keys[0], (SEQ, HEADS * P_SIZE), 1.0, 6.0, ((0, 16), (1, 8)))
    bc_in = normal_values(arg_keys[1], (SEQ, 2 * N), 1.0, 6.0, ((0, 16),))
    z_in = normal_values(arg_keys[2], (SEQ, HEADS * P_SIZE), 1.0, 6.0, ((0, 16), (1, 8)))
    codes = draw_codes(jax.random.fold_in(arg_keys[12], 71), 0)
    head_rate = jnp.clip(jnp.exp(math.log(1.0) - 1.3862944 * jax.random.uniform(arg_keys[4], (HEADS,), jnp.float32) ** levels(arg_keys[4], (HEADS,), ((0, 8),), -0.2, 0.2)), 0.25, 1.0)
    conv_x = normal_values(arg_keys[5], (4, HEADS * P_SIZE), 0.5, 3.0, ((1, 8),), jnp.float32)
    conv_bc = normal_values(arg_keys[6], (4, 2 * N), 0.5, 3.0, (), jnp.float32)
    bias_x = normal_values(arg_keys[7], (HEADS * P_SIZE,), 0.3, 2.0, ((0, 8),), jnp.float32)
    bias_bc = normal_values(arg_keys[8], (2 * N,), 0.3, 2.0, (), jnp.float32)
    skip = jnp.clip(0.5 + 1.0 * jax.random.uniform(arg_keys[9], (HEADS,), jnp.float32) ** levels(arg_keys[9], (HEADS,), ((0, 8),), -0.2, 0.2), 0.5, 1.5)
    norm_gain = jnp.clip(1.0 + 0.1 * jax.random.normal(arg_keys[10], (HEADS * P_SIZE,), jnp.float32), 0.5, 1.5)
    w_out = heavy_noise(arg_keys[11], (HEADS * P_SIZE, DM), (HEADS * P_SIZE) ** -0.5, 0.09375, ((0, 8),), (0, 1, 8, 2.0))
    return dict(x_in=x_in, bc_in=bc_in, z_in=z_in, codes=codes, head_rate=head_rate, conv_x=conv_x, conv_bc=conv_bc, bias_x=bias_x, bias_bc=bias_bc, skip=skip, norm_gain=norm_gain, w_out=w_out)


def causal_conv(signal, weight, shift_bias):
    tok_count = signal.shape[0]
    padded = jnp.pad(signal.astype(jnp.float32), ((3, 0), (0, 0)))
    total = shift_bias[None, :]
    for k in range(4):
        total = total + weight[k][None, :] * padded[k:k + tok_count]
    return jax.nn.silu(total).astype(jnp.bfloat16)

def reference(x_in, bc_in, z_in, codes, head_rate, conv_x, conv_bc, bias_x, bias_bc, skip, norm_gain, w_out):
    high = lax.Precision.HIGHEST
    wide = lax.Precision.HIGH
    xc = causal_conv(x_in, conv_x, bias_x).reshape(SEQ, HEADS, P_SIZE)
    bcc = causal_conv(bc_in, conv_bc, bias_bc)
    in_maps = bcc[:, :N]
    out_maps = bcc[:, N:]
    log_decay = -12.288 / SEQ * head_rate[None, :] * codes.astype(jnp.float32) / 63.0
    cum = jnp.cumsum(log_decay, axis=0)
    block_len = math.gcd(TOK_DEV, 128)
    block_count = SEQ // block_len
    x_blocks = xc.reshape(block_count, block_len, HEADS, P_SIZE)
    in_blocks = in_maps.reshape(block_count, block_len, N)
    out_blocks = out_maps.reshape(block_count, block_len, N)
    cum_blocks = cum.reshape(block_count, block_len, HEADS)
    starts = jnp.concatenate([jnp.zeros((1, HEADS), jnp.float32), cum_blocks[:-1, -1]], axis=0)
    causal = jnp.tril(jnp.ones((block_len, block_len), dtype=bool))

    def advance(running_state, inputs):
        x_block, in_block, out_block, cum_block, block_start = inputs
        scores = jnp.dot(out_block, in_block.T, preferred_element_type=jnp.float32)
        log_gap = cum_block[:, None, :] - cum_block[None, :, :]
        mask3 = causal[:, :, None]
        weights = jnp.where(mask3, jnp.exp(jnp.where(mask3, log_gap, 0.0)), 0.0) * scores[:, :, None]
        weights = weights.astype(jnp.bfloat16)
        inside = jnp.einsum('tsh,shp->thp', weights, x_block, preferred_element_type=jnp.float32)
        carried = jnp.einsum('tn,hnp->thp', out_block.astype(jnp.float32), running_state, precision=wide)
        carried = carried * jnp.exp(cum_block - block_start[None, :])[:, :, None]
        block_end = cum_block[-1]
        factors = jnp.exp(block_end[None, :] - cum_block)
        sent = (x_block.astype(jnp.float32) * factors[:, :, None]).astype(jnp.bfloat16)
        added = jnp.einsum('sn,shp->hnp', in_block, sent, preferred_element_type=jnp.float32)
        next_state = jnp.exp(block_end - block_start)[:, None, None] * running_state + added
        return (next_state, inside + carried)
    _, outputs = lax.scan(advance, jnp.zeros((HEADS, N, P_SIZE), jnp.float32), (x_blocks, in_blocks, out_blocks, cum_blocks, starts))
    scanned = outputs.reshape(SEQ, HEADS, P_SIZE)
    ssd_scale = 1.0 / math.sqrt(N * SEQ)
    ssd = scanned * ssd_scale + skip[None, :, None] * xc.astype(jnp.float32)
    gated_out = ssd * jax.nn.silu(z_in.astype(jnp.float32).reshape(SEQ, HEADS, P_SIZE))
    mean_square = lax.optimization_barrier(jnp.mean(gated_out * gated_out, axis=-1, keepdims=True))
    normed = gated_out * lax.rsqrt(mean_square + 1e-05) * norm_gain.reshape(HEADS, P_SIZE)[None]
    normed = normed.astype(jnp.bfloat16).reshape(SEQ, HEADS * P_SIZE)
    group_width = HEADS * P_SIZE // N_TP
    normed_groups = jnp.transpose(normed.reshape(SEQ, N_TP, group_width), (1, 0, 2))
    weight_groups = w_out.reshape(N_TP, group_width, DM)

    def add_group(total, pair):
        group_rows, group_weight = pair
        partial_value = jnp.dot(group_rows.astype(jnp.float32), group_weight.astype(jnp.float32), precision=high)
        partial_value = lax.optimization_barrier(partial_value.astype(jnp.bfloat16)).astype(jnp.float32)
        return (total + partial_value, None)
    total, _ = lax.scan(add_group, jnp.zeros((SEQ, DM), jnp.float32), (normed_groups, weight_groups))
    return total.astype(jnp.bfloat16)
```

```python
import functools

import jax
import jax.numpy as jnp
from jax import lax
from jax.experimental import pallas as pl
from jax.experimental.pallas import tpu as pltpu
from jax.sharding import PartitionSpec as P

BF = jnp.bfloat16
F32 = jnp.float32
TOK = 512
WID = 1024
HEADS = 8
HW = 128
ST = 128
CTX = 16
CB = 256
NB = WID // CB
HB = CB // HW
SEQ = TOK * CTX
DECAY = 12.288 / SEQ / 63.0
SCALE = 1.0 / (ST * SEQ) ** 0.5
ROWS = 64


def silu(v):
    half = 0.5 * v
    return half + half * jnp.tanh(half)


def mm(a, b):
    return jnp.dot(a, b, preferred_element_type=F32)


def lanes(ref, first, count, factor):
    rows = [jnp.full((1, HW), ref[first + k] * factor, F32) for k in range(count)]
    return jnp.concatenate(rows, axis=1)


def fill_tri(tri):
    for r in range(0, TOK, HW):
        row = lax.broadcasted_iota(jnp.int32, (HW, TOK), 0) + r
        col = lax.broadcasted_iota(jnp.int32, (HW, TOK), 1)
        tri[r : r + HW, :] = jnp.where(row >= col, 1.0, 0.0).astype(BF)


def code_sums(codes_ref, tri, block):
    head = lax.broadcasted_iota(jnp.int32, (HEADS, CB), 0)
    lane = lax.broadcasted_iota(jnp.int32, (HEADS, CB), 1) // HW + HB * block
    spread = jnp.where(head == lane, 1.0, 0.0).astype(BF)
    wide = mm(codes_ref[...].astype(F32).astype(BF), spread).astype(BF)
    return mm(tri[...], wide)


def conv_rows(xe, w_ref, bias_ref, r):
    total = bias_ref[...]
    for k in range(4):
        total = total + w_ref[k : k + 1, :] * xe[5 + k + r : 5 + k + r + ROWS, :]
    return silu(total)


def scan_in_body(
    rate_ref, x_ref, rim_ref, bc_ref, rimbc_ref, codes_ref, cx_ref, bx_ref, cbc_ref, bbc_ref,
    xc_ref, xt_ref, b_ref, c_ref, msg_ref, xe, tri, bt, sums,
):
    block = pl.program_id(0)

    @pl.when(block == 0)
    def _():
        fill_tri(tri)
        xe[0:8, :] = rimbc_ref[...].astype(F32)
        xe[8 : 8 + TOK, :] = bc_ref[...].astype(F32)
        for r in range(0, TOK, ROWS):
            out = conv_rows(xe, cbc_ref, bbc_ref, r)
            b_ref[r : r + ROWS, :] = out[:, :ST].astype(BF)
            c_ref[r : r + ROWS, :] = out[:, ST:].astype(BF)
        bt[...] = b_ref[...].astype(F32).T.astype(BF)

    xe[0:8, :] = rim_ref[...].astype(F32)
    xe[8 : 8 + TOK, :] = x_ref[...].astype(F32)
    sums[...] = code_sums(codes_ref, tri, block)
    rate = lanes(rate_ref, block * HB, HB, DECAY)
    for r in range(0, TOK, ROWS):
        xc = conv_rows(xe, cx_ref, bx_ref, r).astype(BF)
        xc_ref[r : r + ROWS, :] = xc
        xt_ref[r : r + ROWS, :] = (xc.astype(F32) * jnp.exp(rate * sums[r : r + ROWS, :])).astype(BF)
    state = mm(bt[...], xt_ref[...])
    total = sums[TOK - 1 : TOK, :]
    high = jnp.floor(total * (1.0 / 256.0))
    low = total - 256.0 * high
    row = lax.broadcasted_iota(jnp.int32, (8, CB), 0)
    extra = jnp.where(row == 0, high, jnp.where(row == 1, low, 0.0))
    for j in range(CTX):
        part = jnp.concatenate([state[8 * j : 8 * j + 8, :], extra], axis=0)
        msg_ref[j] = part.astype(BF)


def local_body(
    rate_ref, skip_ref, xt_ref, xc_ref, z_ref, codes_ref, b_ref, c_ref, a1_ref, a2_ref, tri, gram, sums, prod,
):
    block = pl.program_id(0)

    @pl.when(block == 0)
    def _():
        fill_tri(tri)
        for r in range(0, TOK, HW):
            part = lax.dot_general(
                c_ref[r : r + HW, :], b_ref[...], (((1,), (1,)), ((), ())), preferred_element_type=F32
            )
            row = lax.broadcasted_iota(jnp.int32, (HW, TOK), 0) + r
            col = lax.broadcasted_iota(jnp.int32, (HW, TOK), 1)
            gram[r : r + HW, :] = jnp.where(row >= col, part, 0.0).astype(BF)

    sums[...] = code_sums(codes_ref, tri, block)
    prod[...] = mm(gram[...], xt_ref[...])
    rate = lanes(rate_ref, block * HB, HB, -DECAY)
    skip = lanes(skip_ref, block * HB, HB, 1.0)
    for r in range(0, TOK, ROWS):
        gate = silu(z_ref[r : r + ROWS, :].astype(F32))
        fade = SCALE * jnp.exp(rate * sums[r : r + ROWS, :])
        xc = xc_ref[r : r + ROWS, :].astype(F32)
        a1_ref[r : r + ROWS, :] = (prod[r : r + ROWS, :] * fade + skip * xc) * gate
        a2_ref[r : r + ROWS, :] = fade * gate


def prefix_body(rate_ref, r_ref, q_ref):
    rate = lanes(rate_ref, 0, HEADS, -DECAY)
    state = jnp.zeros((8, WID), F32)
    for c in range(CTX):
        q_ref[c] = state.astype(BF)
        got = r_ref[c].astype(F32)
        total = 256.0 * got[8:9, :] + got[9:10, :]
        state = jnp.exp(rate * total) * (state + got[0:8, :])


def norm_body(q_ref, a1_ref, a2_ref, c_ref, gain_ref, n_ref, prod):
    state = q_ref[...].astype(F32).reshape(ST, CB).astype(BF)
    prod[...] = mm(c_ref[...], state)
    for r in range(0, TOK, ROWS):
        for h in range(0, CB, HW):
            rs, hs = slice(r, r + ROWS), slice(h, h + HW)
            gated = a1_ref[rs, hs] + a2_ref[rs, hs] * prod[rs, hs]
            power = jnp.mean(gated * gated, axis=-1, keepdims=True)
            n_ref[rs, hs] = (gated * lax.rsqrt(power + 1e-05) * gain_ref[:, hs]).astype(BF)


def pick_body(index_ref, w_ref, gate_ref, o_ref):
    o_ref[0] = w_ref[...]


def proj_body(adds, index_ref, own_ref, sib_ref, w_ref, ws_ref, *refs):
    step = pl.program_id(0)
    outs = refs[-2:]
    value = mm(own_ref[...], w_ref[...]) + mm(sib_ref[...], ws_ref[0])
    for k in range(2):

        @pl.when(step == k)
        def _():
            total = value
            for a in range(adds):
                total = total + refs[2 * a + k][...].astype(F32)
            outs[k][...] = total.astype(outs[k].dtype)


def final_body(m0_ref, m1_ref, a_ref, b_ref, o_ref):
    half = m0_ref.shape[1]
    o_ref[:, :half] = (m0_ref[...] + a_ref[...].astype(F32)).astype(BF)
    o_ref[:, half:] = (m1_ref[...] + b_ref[...].astype(F32)).astype(BF)


def params(**kw):
    return pltpu.CompilerParams(dimension_semantics=("arbitrary",), vmem_limit_bytes=48 << 20, **kw)


SMEM = pl.BlockSpec(memory_space=pltpu.SMEM)


def whole(*shape):
    return pl.BlockSpec(shape, lambda i: (0,) * len(shape))


def cols(rows):
    return pl.BlockSpec((rows, CB), lambda i: (0, i))


def project(index, own, sib, w, ws, addends, kind):
    half = WID // 2
    flat = [a for pair in addends for a in pair]
    const = pl.BlockSpec((TOK, half), lambda i, ix: (0, 0))
    full = pl.BlockSpec((TOK, WID), lambda i, ix: (0, 0))
    return pl.pallas_call(
        functools.partial(proj_body, len(addends)),
        out_shape=[jax.ShapeDtypeStruct((TOK, half), kind)] * 2,
        grid_spec=pltpu.PrefetchScalarGridSpec(
            num_scalar_prefetch=1,
            grid=(2,),
            in_specs=[
                full,
                full,
                pl.BlockSpec((WID, half), lambda i, ix: (0, ix[i])),
                pl.BlockSpec((1, WID, half), lambda i, ix: (ix[2 + i], 0, ix[4 + i])),
            ]
            + [const] * len(flat),
            out_specs=[const, const],
        ),
        compiler_params=params(),
        name="project",
    )(index, own, sib, w, ws, *flat)


def body(
    x_in, bc_in, z_in, codes, head_rate, conv_x, conv_bc, bias_x, bias_bc, skip, norm_gain, w_out
):
    place = lax.axis_index("tp")
    row, core = place // 2, place % 2
    rim = jnp.concatenate([x_in[TOK - 8 :], bc_in[TOK - 8 :]], axis=1)
    rim = lax.ppermute(rim, "ctx", [(s, s + 1) for s in range(CTX - 1)])

    sd = jax.ShapeDtypeStruct
    xc, xt, b_map, c_map, msg = pl.pallas_call(
        scan_in_body,
        grid=(NB,),
        in_specs=[
            SMEM, cols(TOK), cols(8), whole(TOK, 2 * ST),
            pl.BlockSpec((8, CB), lambda i: (0, NB)), whole(TOK, HEADS), cols(4), cols(1),
            whole(4, 2 * ST), whole(1, 2 * ST),
        ],
        out_specs=[
            cols(TOK), cols(TOK), whole(TOK, ST), whole(TOK, ST),
            pl.BlockSpec((CTX, 16, CB), lambda i: (0, 0, i)),
        ],
        out_shape=[
            sd((TOK, WID), BF), sd((TOK, WID), BF), sd((TOK, ST), BF), sd((TOK, ST), BF),
            sd((CTX, 16, WID), BF),
        ],
        scratch_shapes=[
            pltpu.VMEM((TOK + 8, CB), F32), pltpu.VMEM((TOK, TOK), BF), pltpu.VMEM((ST, TOK), BF),
            pltpu.VMEM((TOK, CB), F32),
        ],
        compiler_params=params(),
        name="scan_in",
    )(
        head_rate, x_in, rim, bc_in, rim, codes, conv_x, bias_x[None, :], conv_bc, bias_bc[None, :]
    )

    got = lax.all_to_all(msg, "ctx", 0, 0, tiled=True)

    order = jnp.stack([2 * r + 1 - core for r in range(4)]).astype(jnp.int32)
    picked = pl.pallas_call(
        pick_body,
        out_shape=sd((4, WID, WID), BF),
        grid_spec=pltpu.PrefetchScalarGridSpec(
            num_scalar_prefetch=1,
            grid=(4,),
            in_specs=[
                pl.BlockSpec((WID, WID), lambda i, ix: (0, ix[i])),
                pl.BlockSpec(memory_space=pl.ANY),
            ],
            out_specs=pl.BlockSpec((1, WID, WID), lambda i, ix: (i, 0, 0)),
        ),
        compiler_params=params(),
        name="pick",
    )(order, w_out, c_map)
    swap = [(s, s ^ 1) for s in range(8)]
    w_sib = lax.ppermute(picked, "tp", swap)

    a1, a2 = pl.pallas_call(
        local_body,
        grid=(NB,),
        in_specs=[
            SMEM, SMEM, cols(TOK), cols(TOK), cols(TOK), whole(TOK, HEADS), whole(TOK, ST),
            whole(TOK, ST),
        ],
        out_specs=[cols(TOK), cols(TOK)],
        out_shape=[sd((TOK, WID), F32)] * 2,
        scratch_shapes=[
            pltpu.VMEM((TOK, TOK), BF), pltpu.VMEM((TOK, TOK), BF), pltpu.VMEM((TOK, CB), F32),
            pltpu.VMEM((TOK, CB), F32),
        ],
        compiler_params=params(),
        name="local",
    )(head_rate, skip, xt, xc, z_in, codes, b_map, c_map)

    prefix = pl.pallas_call(
        prefix_body,
        in_specs=[SMEM, pl.BlockSpec(memory_space=pltpu.VMEM)],
        out_specs=pl.BlockSpec(memory_space=pltpu.VMEM),
        out_shape=sd((CTX, 8, WID), BF),
        compiler_params=pltpu.CompilerParams(vmem_limit_bytes=48 << 20),
        name="prefix",
    )(head_rate, got)
    incoming = lax.all_to_all(prefix, "ctx", 0, 0, tiled=True)

    normed = pl.pallas_call(
        norm_body,
        grid=(NB,),
        in_specs=[
            pl.BlockSpec((CTX, 8, CB), lambda i: (0, 0, i)), cols(TOK), cols(TOK), whole(TOK, ST),
            cols(1),
        ],
        out_specs=cols(TOK),
        out_shape=sd((TOK, WID), BF),
        scratch_shapes=[pltpu.VMEM((TOK, CB), F32)],
        compiler_params=params(),
        name="norm",
    )(incoming, a1, a2, c_map, norm_gain[None, :])
    sibling = lax.ppermute(normed, "tp", swap)

    up = [(s, (s + 2) % 8) for s in range(8)]
    down = [(s, (s + 6) % 8) for s in range(8)]

    def target(far0, half0, far1, half1):
        d0, d1 = (row + far0) % 4, (row + far1) % 4
        return jnp.stack(
            [(2 * d0 + core) * 2 + half0, (2 * d1 + core) * 2 + half1, d0, d1,
             jnp.int32(half0), jnp.int32(half1)]
        ).astype(jnp.int32)

    def run(index, addends, kind):
        return project(index, normed, sibling, w_out, w_sib, addends, kind)

    far_l, far_r = run(target(2, 0, 2, 1), [], BF)
    far_l = lax.ppermute(far_l, "tp", up)
    far_r = lax.ppermute(far_r, "tp", down)
    above_r, below_l = run(target(1, 1, 3, 0), [], BF)
    above_r = lax.ppermute(above_r, "tp", up)
    below_l = lax.ppermute(below_l, "tp", down)
    above_l, below_r = run(target(1, 0, 3, 1), [(far_l, far_r)], BF)
    above_l = lax.ppermute(above_l, "tp", up)
    below_r = lax.ppermute(below_r, "tp", down)
    here_l, here_r = run(target(0, 0, 0, 1), [(below_l, above_r)], F32)
    return pl.pallas_call(
        final_body,
        in_specs=[pl.BlockSpec(memory_space=pltpu.VMEM)] * 4,
        out_specs=pl.BlockSpec(memory_space=pltpu.VMEM),
        out_shape=sd((TOK, WID), BF),
        compiler_params=pltpu.CompilerParams(vmem_limit_bytes=48 << 20),
        name="final",
    )(here_l, here_r, above_l, below_r)


def solution(mesh):
    in_specs = (
        P("ctx", "tp"),
        P("ctx", None),
        P("ctx", "tp"),
        P("ctx", "tp"),
        P("tp"),
        P(None, "tp"),
        P(),
        P("tp"),
        P(),
        P("tp"),
        P("tp"),
        P("tp", None),
    )
    out_specs = P("ctx", "tp")
    return jax.shard_map(body, mesh=mesh, in_specs=in_specs, out_specs=out_specs, check_vma=False)
```

```python
import functools

import jax
import jax.numpy as jnp
from jax import lax
from jax.experimental import pallas as pl
from jax.experimental.pallas import tpu as pltpu
from jax.sharding import PartitionSpec as P

BF = jnp.bfloat16
F32 = jnp.float32
TOK = 512
HT = TOK // 2
WID = 1024
HALF = WID // 2
HEADS = 8
HW = 128
ST = 128
CTX = 16
CB = 256
NB = WID // CB
HB = CB // HW
SEQ = TOK * CTX
DECAY = 12.288 / SEQ / 63.0
SCALE = 1.0 / (ST * SEQ) ** 0.5
ROWS = 64
SD = jax.ShapeDtypeStruct


def silu(v):
    half = 0.5 * v
    return half + half * jnp.tanh(half)


def mm(a, b):
    return jnp.dot(a, b, preferred_element_type=F32)


def lanes(ref, first, count, factor):
    rows = [jnp.full((1, HW), ref[first + k] * factor, F32) for k in range(count)]
    return jnp.concatenate(rows, axis=1)


def fill_tri(tri, first, count):
    for r in range(0, count, HW):
        row = lax.broadcasted_iota(jnp.int32, (HW, TOK), 0) + (r + first)
        col = lax.broadcasted_iota(jnp.int32, (HW, TOK), 1)
        tri[r : r + HW, :] = jnp.where(row >= col, 1.0, 0.0).astype(BF)


def fill_codes(codes_ref, codes):
    padded = jnp.concatenate([codes_ref[...].astype(F32), jnp.zeros((HW - HEADS, TOK), F32)], axis=0)
    codes[...] = padded.T.astype(BF)


def code_sums(codes, tri, block):
    head = lax.broadcasted_iota(jnp.int32, (HW, CB), 0)
    lane = lax.broadcasted_iota(jnp.int32, (HW, CB), 1) // HW + HB * block
    spread = jnp.where(head == lane, 1.0, 0.0).astype(BF)
    return mm(tri[...], mm(codes[...], spread).astype(BF))


def conv_rows(xe, w_ref, bias_ref, r):
    total = bias_ref[...]
    for k in range(4):
        total = total + w_ref[k : k + 1, :] * xe[5 + k + r : 5 + k + r + ROWS, :]
    return silu(total)


def rim_body(x_ref, bc_ref, o_ref):
    o_ref[:, :WID] = x_ref[...]
    o_ref[:, WID:] = bc_ref[...]


def scan_in_body(
    last, rate_ref, x_ref, rim_ref, bc_ref, rimbc_ref, codes_ref, cx_ref, bx_ref, cbc_ref, bbc_ref, *refs
):
    if last:
        xc_ref, xt_ref, b_ref, c_ref, state_ref, total_ref, xe, tri, bt, sums, codes = refs
    else:
        earlier_ref, whole_ref, xc_ref, xt_ref, b_ref, c_ref, msg_ref, xe, tri, bt, sums, codes = refs
    block = pl.program_id(0)

    @pl.when(block == 0)
    def _():
        fill_tri(tri, HT if last else 0, HT)
        fill_codes(codes_ref, codes)
        xe[0:8, :] = rimbc_ref[...].astype(F32)[-8:, :]
        xe[8 : 8 + HT, :] = bc_ref[...].astype(F32)
        for r in range(0, HT, ROWS):
            out = conv_rows(xe, cbc_ref, bbc_ref, r)
            b_ref[r : r + ROWS, :] = out[:, :ST].astype(BF)
            c_ref[r : r + ROWS, :] = out[:, ST:].astype(BF)
        bt[...] = b_ref[...].astype(F32).T.astype(BF)

    xe[0:8, :] = rim_ref[...].astype(F32)[-8:, :]
    xe[8 : 8 + HT, :] = x_ref[...].astype(F32)
    sums[...] = code_sums(codes, tri, block)
    rate = lanes(rate_ref, block * HB, HB, DECAY)
    for r in range(0, HT, ROWS):
        xc = conv_rows(xe, cx_ref, bx_ref, r).astype(BF)
        xc_ref[r : r + ROWS, :] = xc
        xt_ref[r : r + ROWS, :] = (xc.astype(F32) * jnp.exp(rate * sums[r : r + ROWS, :])).astype(BF)
    state = mm(bt[...], xt_ref[...])
    if last:
        state_ref[...] = state
        total_ref[...] = sums[HT - 8 : HT, :]
        return
    state = state + earlier_ref[...]
    total = whole_ref[7:8, :]
    high = jnp.floor(total * (1.0 / 256.0))
    low = total - 256.0 * high
    row = lax.broadcasted_iota(jnp.int32, (8, CB), 0)
    extra = jnp.where(row == 0, high, jnp.where(row == 1, low, 0.0))
    for j in range(CTX):
        part = jnp.concatenate([state[8 * j : 8 * j + 8, :], extra], axis=0)
        msg_ref[j] = part.astype(BF)


def local_body(
    rate_ref, skip_ref, xt0_ref, xt1_ref, xc0_ref, xc1_ref, z_ref, codes_ref, b0_ref, b1_ref, c0_ref, c1_ref,
    a1_ref, a2_ref, tri, gram, sums, prod, codes,
):
    block = pl.program_id(0)

    @pl.when(block == 0)
    def _():
        fill_tri(tri, 0, TOK)
        fill_codes(codes_ref, codes)
        for r in range(0, TOK, HW):
            c_ref = c0_ref if r < HT else c1_ref
            rows = c_ref[r % HT : r % HT + HW, :]
            row = lax.broadcasted_iota(jnp.int32, (HW, HT), 0) + r
            col = lax.broadcasted_iota(jnp.int32, (HW, HT), 1)
            for k, b_ref in enumerate((b0_ref, b1_ref)):
                part = lax.dot_general(
                    rows, b_ref[...], (((1,), (1,)), ((), ())), preferred_element_type=F32
                )
                gram[r : r + HW, k * HT : (k + 1) * HT] = jnp.where(
                    row >= col + k * HT, part, 0.0
                ).astype(BF)

    sums[...] = code_sums(codes, tri, block)
    prod[0:HT, :] = mm(gram[0:HT, 0:HT], xt0_ref[...])
    prod[HT:TOK, :] = mm(gram[HT:TOK, 0:HT], xt0_ref[...]) + mm(gram[HT:TOK, HT:TOK], xt1_ref[...])
    rate = lanes(rate_ref, block * HB, HB, -DECAY)
    skip = lanes(skip_ref, block * HB, HB, 1.0)
    for r in range(0, TOK, ROWS):
        gate = silu(z_ref[r : r + ROWS, :].astype(F32))
        fade = SCALE * jnp.exp(rate * sums[r : r + ROWS, :])
        xc_ref = xc0_ref if r < HT else xc1_ref
        xc = xc_ref[r % HT : r % HT + ROWS, :].astype(F32)
        a1_ref[r : r + ROWS, :] = (prod[r : r + ROWS, :] * fade + skip * xc) * gate
        a2_ref[r : r + ROWS, :] = fade * gate


def prefix_body(rate_ref, r_ref, after_ref, q_ref):
    rate = lanes(rate_ref, 0, HEADS, -DECAY)
    state = jnp.zeros((8, WID), F32)
    for c in range(CTX):
        q_ref[c] = state.astype(BF)
        got = r_ref[c].astype(F32)
        total = 256.0 * got[8:9, :] + got[9:10, :]
        state = jnp.exp(rate * total) * (state + got[0:8, :])


def norm_body(q_ref, a1_ref, a2_ref, c0_ref, c1_ref, gain_ref, n_ref, prod):
    state = q_ref[...].astype(F32).reshape(ST, CB).astype(BF)
    prod[0:HT, :] = mm(c0_ref[...], state)
    prod[HT:TOK, :] = mm(c1_ref[...], state)
    for r in range(0, TOK, ROWS):
        for h in range(0, CB, HW):
            rs, hs = slice(r, r + ROWS), slice(h, h + HW)
            gated = a1_ref[rs, hs] + a2_ref[rs, hs] * prod[rs, hs]
            power = jnp.mean(gated * gated, axis=-1, keepdims=True)
            n_ref[rs, hs] = (gated * lax.rsqrt(power + 1e-05) * gain_ref[:, hs]).astype(BF)


def partial_body(index_ref, n_ref, w_ref, after_ref, o_ref):
    o_ref[...] = mm(n_ref[...], w_ref[...]).astype(o_ref.dtype)


def summed_body(adds, index_ref, n_ref, w_ref, r_ref, after_ref, *refs):
    step = pl.program_id(0)
    outs = refs[-2:]
    for k in range(2):

        @pl.when(step == k)
        def _():
            total = mm(n_ref[...], w_ref[...]) + r_ref[...].astype(F32)
            for a in range(adds):
                total = total + refs[2 * a + k][...].astype(F32)
            outs[k][...] = total.astype(outs[k].dtype)


def final_body(m0_ref, m1_ref, a_ref, b_ref, o_ref):
    o_ref[:, :HALF] = (m0_ref[...] + a_ref[...].astype(F32)).astype(BF)
    o_ref[:, HALF:] = (m1_ref[...] + b_ref[...].astype(F32)).astype(BF)


def params(dims=1):
    return pltpu.CompilerParams(
        dimension_semantics=("arbitrary",) * dims if dims else None, vmem_limit_bytes=20 << 20
    )


SMEM = pl.BlockSpec(memory_space=pltpu.SMEM)
VMEM = pl.BlockSpec(memory_space=pltpu.VMEM)


def whole(*shape):
    return pl.BlockSpec(shape, lambda i: (0,) * len(shape))


def cols(rows, at=0):
    return pl.BlockSpec((rows, CB), lambda i: (at, i))


def in_hbm(a):
    return pltpu.with_memory_space_constraint(a, pltpu.HBM)


STEPS = ((2, 0), (2, 1), (1, 1), (3, 0), (1, 0), (3, 1), (0, 0), (0, 1))


def column_block(first, flip):
    def index(i, place_ref):
        place = place_ref[0]
        far, side = jnp.int32(0), jnp.int32(0)
        for k, (f, s) in enumerate(STEPS[first:]):
            far = jnp.where(i == k, f, far)
            side = jnp.where(i == k, s, side)
        core = (place & 1) ^ flip
        return 0, ((((place >> 1) + far) & 3) * 2 + core) * 2 + side

    return pl.BlockSpec((WID, HALF), index)


def whole2(*shape):
    return pl.BlockSpec(shape, lambda i, ix: (0,) * len(shape))


ANY = pl.BlockSpec(memory_space=pl.ANY)


def partial(place, normed, w, first, count, after):
    return pl.pallas_call(
        partial_body,
        out_shape=SD((TOK, count * HALF), BF),
        grid_spec=pltpu.PrefetchScalarGridSpec(
            num_scalar_prefetch=1,
            grid=(count,),
            in_specs=[whole2(TOK, WID), column_block(first, 1), ANY],
            out_specs=pl.BlockSpec((TOK, HALF), lambda i, ix: (0, i)),
        ),
        compiler_params=params(),
        name="partial",
    )(place, normed, w, after)


def summed(place, normed, w, first, got, at, addends, kind, after):
    flat = [a for pair in addends for a in pair]
    const = whole2(TOK, HALF)
    return pl.pallas_call(
        functools.partial(summed_body, len(addends)),
        out_shape=[SD((TOK, HALF), kind)] * 2,
        grid_spec=pltpu.PrefetchScalarGridSpec(
            num_scalar_prefetch=1,
            grid=(2,),
            in_specs=[
                whole2(TOK, WID),
                column_block(first, 0),
                pl.BlockSpec((TOK, HALF), lambda i, ix: (0, at + i)),
                ANY,
            ]
            + [const] * len(flat),
            out_specs=[const, const],
        ),
        compiler_params=params(),
        name="summed",
    )(place, normed, w, got, after, *flat)


def scan_in(last, rate, x_in, rim, bc_in, codes, conv_x, bias_x, conv_bc, bias_bc, *carry):
    at = 1 if last else 0
    if last:
        rims = [pl.BlockSpec((16, CB), lambda i: (15, i)), pl.BlockSpec((16, 2 * ST), lambda i: (15, 0))]
        rim_args = (x_in, bc_in)
        extra_out = [SD((ST, WID), F32), SD((8, WID), F32)]
        extra_spec = [cols(ST), cols(8)]
    else:
        rims = [cols(8), pl.BlockSpec((8, 2 * ST), lambda i: (0, NB))]
        rim_args = (rim, rim)
        extra_out = [SD((CTX, 16, WID), BF)]
        extra_spec = [pl.BlockSpec((CTX, 16, CB), lambda i: (0, 0, i))]
    return pl.pallas_call(
        functools.partial(scan_in_body, last),
        grid=(NB,),
        in_specs=[
            SMEM, cols(HT, at), rims[0], pl.BlockSpec((HT, 2 * ST), lambda i: (at, 0)), rims[1],
            whole(HEADS, TOK), cols(4), cols(1), whole(4, 2 * ST), whole(1, 2 * ST),
        ]
        + ([] if last else [cols(ST), cols(8)]),
        out_specs=[cols(HT), cols(HT), whole(HT, ST), whole(HT, ST)] + extra_spec,
        out_shape=[pltpu.HBM((HT, WID), BF), pltpu.HBM((HT, WID), BF), SD((HT, ST), BF), SD((HT, ST), BF)]
        + extra_out,
        scratch_shapes=[
            pltpu.VMEM((HT + 8, CB), F32), pltpu.VMEM((HT, TOK), BF), pltpu.VMEM((ST, HT), BF),
            pltpu.VMEM((HT, CB), F32), pltpu.VMEM((TOK, HW), BF),
        ],
        compiler_params=params(),
        name="scan_in",
    )(rate, x_in, rim_args[0], bc_in, rim_args[1], codes, conv_x, bias_x, conv_bc, bias_bc, *carry)


def body(
    x_in, bc_in, z_in, codes, head_rate, conv_x, conv_bc, bias_x, bias_bc, skip, norm_gain, w_out
):
    place = lax.axis_index("tp")
    where = jnp.full((1,), place, jnp.int32)
    x_in, bc_in, z_in, w_out = in_hbm(x_in), in_hbm(bc_in), in_hbm(z_in), in_hbm(w_out)
    codes, conv_x, conv_bc = in_hbm(codes.T), in_hbm(conv_x), in_hbm(conv_bc)
    head_rate, skip = in_hbm(head_rate), in_hbm(skip)
    bias_x, bias_bc, gain = in_hbm(bias_x[None, :]), in_hbm(bias_bc[None, :]), in_hbm(norm_gain[None, :])

    rim = pl.pallas_call(
        rim_body,
        grid=(1,),
        in_specs=[
            pl.BlockSpec((8, WID), lambda i: (TOK // 8 - 1, 0)),
            pl.BlockSpec((8, 2 * ST), lambda i: (TOK // 8 - 1, 0)),
        ],
        out_specs=whole(8, WID + 2 * ST),
        out_shape=SD((8, WID + 2 * ST), BF),
        compiler_params=params(),
        name="rim",
    )(x_in, bc_in)
    rim = lax.ppermute(rim, "ctx", [(s, s + 1) for s in range(CTX - 1)])

    shared = (codes, conv_x, bias_x, conv_bc, bias_bc)
    xc1, xt1, b1, c1, state1, total = scan_in(True, head_rate, x_in, None, bc_in, *shared)
    xc0, xt0, b0, c0, msg = scan_in(False, head_rate, x_in, rim, bc_in, *shared, state1, total)

    got = lax.all_to_all(msg, "ctx", 0, 0, tiled=True)

    a1, a2 = pl.pallas_call(
        local_body,
        grid=(NB,),
        in_specs=[
            SMEM, SMEM, cols(HT), cols(HT), cols(HT), cols(HT), cols(TOK), whole(HEADS, TOK),
            whole(HT, ST), whole(HT, ST), whole(HT, ST), whole(HT, ST),
        ],
        out_specs=[cols(TOK), cols(TOK)],
        out_shape=[pltpu.HBM((TOK, WID), F32)] * 2,
        scratch_shapes=[
            pltpu.VMEM((TOK, TOK), BF), pltpu.VMEM((TOK, TOK), BF), pltpu.VMEM((TOK, CB), F32),
            pltpu.VMEM((TOK, CB), F32), pltpu.VMEM((TOK, HW), BF),
        ],
        compiler_params=params(),
        cost_estimate=pl.CostEstimate(flops=2 << 30, transcendentals=1 << 20, bytes_accessed=8 << 20),
        name="local",
    )(head_rate, skip, *map(in_hbm, (xt0, xt1, xc0, xc1)), z_in, codes, b0, b1, c0, c1)
    a1, a2 = in_hbm(a1), in_hbm(a2)

    prefix = pl.pallas_call(
        prefix_body,
        in_specs=[SMEM, VMEM, ANY],
        out_specs=VMEM,
        out_shape=SD((CTX, 8, WID), BF),
        compiler_params=params(0),
        name="prefix",
    )(head_rate, got, a1)
    incoming = lax.all_to_all(prefix, "ctx", 0, 0, tiled=True)

    normed = pl.pallas_call(
        norm_body,
        grid=(NB,),
        in_specs=[
            pl.BlockSpec((CTX, 8, CB), lambda i: (0, 0, i)), cols(TOK), cols(TOK), whole(HT, ST),
            whole(HT, ST), cols(1),
        ],
        out_specs=cols(TOK),
        out_shape=SD((TOK, WID), BF),
        scratch_shapes=[pltpu.VMEM((TOK, CB), F32)],
        compiler_params=params(),
        name="norm",
    )(incoming, a1, a2, c0, c1, gain)

    swap = [(s, s ^ 1) for s in range(8)]
    up = [(s, (s + 2) % 8) for s in range(8)]
    down = [(s, (s + 6) % 8) for s in range(8)]
    args = (where, normed, w_out)
    s1 = partial(*args, 0, 2, where)
    r1 = lax.ppermute(s1, "tp", swap)
    s2 = partial(*args, 2, 2, s1)
    r2 = lax.ppermute(s2, "tp", swap)
    far_l, far_r = summed(*args, 0, r1, 0, [], BF, s2)
    got_l = lax.ppermute(far_l, "tp", up)
    got_r = lax.ppermute(far_r, "tp", down)
    above_r, below_l = summed(*args, 2, r2, 0, [], BF, far_l)
    from_r = lax.ppermute(above_r, "tp", up)
    from_l = lax.ppermute(below_l, "tp", down)
    r3 = lax.ppermute(partial(*args, 4, 4, above_r), "tp", swap)
    above_l, below_r = summed(*args, 4, r3, 0, [(got_l, got_r)], BF, where)
    last_l = lax.ppermute(above_l, "tp", up)
    last_r = lax.ppermute(below_r, "tp", down)
    here_l, here_r = summed(*args, 6, r3, 2, [(from_l, from_r)], F32, above_l)
    return pl.pallas_call(
        final_body,
        in_specs=[VMEM] * 4,
        out_specs=VMEM,
        out_shape=SD((TOK, WID), BF),
        compiler_params=params(0),
        name="final",
    )(here_l, here_r, last_l, last_r)


def solution(mesh):
    in_specs = (
        P("ctx", "tp"),
        P("ctx", None),
        P("ctx", "tp"),
        P("ctx", "tp"),
        P("tp"),
        P(None, "tp"),
        P(),
        P("tp"),
        P(),
        P("tp"),
        P("tp"),
        P("tp", None),
    )
    out_specs = P("ctx", "tp")
    return jax.shard_map(body, mesh=mesh, in_specs=in_specs, out_specs=out_specs, check_vma=False)
```

```python
import functools

import jax
import jax.numpy as jnp
from jax import lax
from jax.experimental import pallas as pl
from jax.experimental.pallas import tpu as pltpu
from jax.sharding import PartitionSpec as P

BF = jnp.bfloat16
F32 = jnp.float32
TOK = 512
HT = TOK // 2
WID = 1024
HALF = WID // 2
HEADS = 8
HW = 128
ST = 128
CTX = 16
CB = 512
NB = WID // CB
SEQ = TOK * CTX
DECAY = 12.288 / SEQ / 63.0
SCALE = 1.0 / (ST * SEQ) ** 0.5
ROWS = 32
SD = jax.ShapeDtypeStruct


def silu(v):
    half = 0.5 * v
    return half + half * jnp.tanh(half)


def mm(a, b):
    return jnp.dot(a, b, preferred_element_type=F32)


def triangle(first, rows, count):
    row = lax.broadcasted_iota(jnp.int32, (rows, count), 0) + first
    col = lax.broadcasted_iota(jnp.int32, (rows, count), 1)
    return jnp.where(row >= col, 1.0, 0.0).astype(BF)


def head_row(ref, factor):
    lane = lax.broadcasted_iota(jnp.int32, (1, HW), 1)
    row = jnp.zeros((1, HW), F32)
    for h in range(HEADS):
        row = jnp.where(lane == h, ref[h] * factor, row)
    return row


def spread(compact, head, rows=None):
    column = compact[:, head : head + 1]
    return jnp.broadcast_to(column, (compact.shape[0], HW))


def conv_part(xe, w_ref, bias_ref, r, lo, hi):
    total = bias_ref[:, lo:hi]
    for k in range(4):
        total = total + w_ref[k : k + 1, lo:hi] * xe[5 + k + r : 5 + k + r + ROWS, lo:hi]
    return silu(total)


def rim_body(x_ref, bc_ref, o_ref):
    o_ref[:, :WID] = x_ref[...]
    o_ref[:, WID:] = bc_ref[...]


def scan_in_body(
    last, rate_ref, x_ref, rim_ref, bc_ref, rimbc_ref, codes_ref, cx_ref, bx_ref, cbc_ref, bbc_ref, *refs
):
    if last:
        xc_ref, xt_ref, b_ref, c_ref, cum_ref, state_ref, xe, be = refs
    else:
        earlier_ref, later_ref, xc_ref, xt_ref, b_ref, c_ref, cum_ref, msg_ref, xe, be = refs
    be[0:8, :] = rimbc_ref[...].astype(F32)[-8:, :]
    be[8 : 8 + HT, :] = bc_ref[...].astype(F32)
    xe[0:8, :] = rim_ref[...].astype(F32)[-8:, :]
    xe[8 : 8 + HT, :] = x_ref[...].astype(F32)
    codes = jnp.concatenate([codes_ref[...].astype(F32), jnp.zeros((HW - HEADS, TOK), F32)], axis=0)
    first = HT if last else 0
    cum = lax.dot_general(
        triangle(first, HT, TOK), codes.astype(BF), (((1,), (1,)), ((), ())), preferred_element_type=F32
    )
    cum_ref[...] = cum
    grow = jnp.exp(head_row(rate_ref, DECAY) * cum)
    for r in range(0, HT, ROWS):
        b_ref[r : r + ROWS, :] = conv_part(be, cbc_ref, bbc_ref, r, 0, ST).astype(BF)
        c_ref[r : r + ROWS, :] = conv_part(be, cbc_ref, bbc_ref, r, ST, 2 * ST).astype(BF)
    bt = b_ref[...].astype(F32).T.astype(BF)
    for r in range(0, HT, ROWS):
        for h in range(HEADS):
            lo, hi = h * HW, (h + 1) * HW
            xc = conv_part(xe, cx_ref, bx_ref, r, lo, hi).astype(BF)
            xc_ref[r : r + ROWS, lo:hi] = xc
            scaled = xc.astype(F32) * spread(grow[r : r + ROWS, :], h)
            xt_ref[r : r + ROWS, lo:hi] = scaled.astype(BF)
    if last:
        state_ref[...] = mm(bt, xt_ref[...])
        return
    state = mm(bt, xt_ref[...]) + earlier_ref[...]
    total = later_ref[7:8, :]
    high = jnp.floor(total * (1.0 / 256.0))
    low = total - 256.0 * high
    row = lax.broadcasted_iota(jnp.int32, (8, HW), 0)
    pair = jnp.where(row == 0, high, jnp.where(row == 1, low, 0.0))
    extra = jnp.concatenate([spread(pair, h) for h in range(HEADS)], axis=1)
    for j in range(CTX):
        part = jnp.concatenate([state[8 * j : 8 * j + 8, :], extra], axis=0)
        msg_ref[j] = part.astype(BF)


def local_body(
    rate_ref, skip_ref, xt0_ref, xt1_ref, xc0_ref, xc1_ref, z_ref, cum0_ref, cum1_ref, b0_ref, b1_ref, c0_ref,
    c1_ref, a1_ref, a2_ref, gram, prod,
):
    for r in range(0, TOK, HW):
        c_ref = c0_ref if r < HT else c1_ref
        rows = c_ref[r % HT : r % HT + HW, :]
        row = lax.broadcasted_iota(jnp.int32, (HW, HT), 0) + r
        col = lax.broadcasted_iota(jnp.int32, (HW, HT), 1)
        for k, b_ref in enumerate((b0_ref, b1_ref)):
            part = lax.dot_general(rows, b_ref[...], (((1,), (1,)), ((), ())), preferred_element_type=F32)
            gram[r : r + HW, k * HT : (k + 1) * HT] = jnp.where(row >= col + k * HT, part, 0.0).astype(BF)
    prod[0:HT, :] = mm(gram[0:HT, 0:HT], xt0_ref[...])
    prod[HT:TOK, :] = mm(gram[HT:TOK, 0:HT], xt0_ref[...]) + mm(gram[HT:TOK, HT:TOK], xt1_ref[...])
    rate = head_row(rate_ref, -DECAY)
    for r in range(0, TOK, ROWS):
        cum_ref, xc_ref, p = (cum0_ref, xc0_ref, r) if r < HT else (cum1_ref, xc1_ref, r - HT)
        fades = SCALE * jnp.exp(rate * cum_ref[p : p + ROWS, :])
        for h in range(HEADS):
            lo, hi = h * HW, (h + 1) * HW
            gate = silu(z_ref[r : r + ROWS, lo:hi].astype(F32))
            fade = spread(fades, h)
            xc = xc_ref[p : p + ROWS, lo:hi].astype(F32)
            both = (prod[r : r + ROWS, lo:hi] * fade + skip_ref[h] * xc) * gate
            a1_ref[r : r + ROWS, lo:hi] = both.astype(BF)
            a2_ref[r : r + ROWS, lo:hi] = (fade * gate).astype(BF)


def prefix_body(rate_ref, r_ref, after_ref, q_ref):
    rate = jnp.concatenate([jnp.full((1, HW), rate_ref[h] * -DECAY, F32) for h in range(HEADS)], axis=1)
    state = jnp.zeros((8, WID), F32)
    for c in range(CTX):
        q_ref[c] = state.astype(BF)
        got = r_ref[c].astype(F32)
        total = 256.0 * got[8:9, :] + got[9:10, :]
        state = jnp.exp(rate * total) * (state + got[0:8, :])


def norm_body(q_ref, a1_ref, a2_ref, c0_ref, c1_ref, gain_ref, n_ref, prod):
    state = q_ref[...].astype(F32).reshape(ST, CB).astype(BF)
    prod[0:HT, :] = mm(c0_ref[...], state)
    prod[HT:TOK, :] = mm(c1_ref[...], state)
    for r in range(0, TOK, ROWS):
        for h in range(0, CB, HW):
            rs, hs = slice(r, r + ROWS), slice(h, h + HW)
            gated = a1_ref[rs, hs].astype(F32) + a2_ref[rs, hs].astype(F32) * prod[rs, hs]
            power = jnp.mean(gated * gated, axis=-1, keepdims=True)
            n_ref[rs, hs] = (gated * lax.rsqrt(power + 1e-05) * gain_ref[:, hs]).astype(BF)


def project_body(adds, place_ref, own_ref, sib_ref, w_ref, ws_ref, *refs):
    step = pl.program_id(0)
    outs = refs[-2:]
    for k in range(2):

        @pl.when(step // 2 == k)
        def _():
            total = mm(own_ref[...], w_ref[...]) + mm(sib_ref[...], ws_ref[...])
            for ref in refs[adds * k : adds * (k + 1)]:
                total = total + ref[...].astype(F32)
            outs[k][...] = total.astype(outs[k].dtype)


def final_body(m0_ref, m1_ref, a_ref, b_ref, o_ref):
    o_ref[:, :HALF] = (m0_ref[...] + a_ref[...].astype(F32)).astype(BF)
    o_ref[:, HALF:] = (m1_ref[...] + b_ref[...].astype(F32)).astype(BF)


def params(dims=1):
    return pltpu.CompilerParams(
        dimension_semantics=("arbitrary",) * dims if dims else None, vmem_limit_bytes=20 << 20
    )


SMEM = pl.BlockSpec(memory_space=pltpu.SMEM)
VMEM = pl.BlockSpec(memory_space=pltpu.VMEM)
ANY = pl.BlockSpec(memory_space=pl.ANY)


def whole(*shape):
    return pl.BlockSpec(shape, lambda i: (0,) * len(shape))


def cols(rows, at=0):
    return pl.BlockSpec((rows, CB), lambda i: (at, i))


def in_hbm(a):
    return pltpu.with_memory_space_constraint(a, pltpu.HBM)


QUART = HALF // 2


def project(place, normed, sibling, w, w_sib, targets, addends, kind):
    def column(i, place_ref):
        index = place_ref[0]
        far = jnp.where(i < 2, targets[0][0], targets[1][0])
        side = jnp.where(i < 2, targets[0][1], targets[1][1])
        return 0, ((((index >> 1) + far) & 3) * 2 + (index & 1)) * 4 + side * 2 + (i & 1)

    whole2 = pl.BlockSpec((TOK, WID), lambda i, ix: (0, 0))
    weight = pl.BlockSpec((WID, QUART), column)
    halves = [
        pl.BlockSpec((TOK, QUART), lambda i, ix: (0, jnp.minimum(i, 1))),
        pl.BlockSpec((TOK, QUART), lambda i, ix: (0, jnp.maximum(i - 2, 0))),
    ]
    count = len(addends[0])
    return pl.pallas_call(
        functools.partial(project_body, count),
        out_shape=[SD((TOK, HALF), kind)] * 2,
        grid_spec=pltpu.PrefetchScalarGridSpec(
            num_scalar_prefetch=1,
            grid=(4,),
            in_specs=[whole2, whole2, weight, weight] + [halves[0]] * count + [halves[1]] * count,
            out_specs=halves,
        ),
        compiler_params=params(),
        name="project",
    )(place, normed, sibling, w, w_sib, *addends[0], *addends[1])


def scan_in(last, rate, x_in, rim, bc_in, codes, conv_x, bias_x, conv_bc, bias_bc, *carry):
    at = 1 if last else 0
    if last:
        rims = [pl.BlockSpec((16, WID), lambda i: (15, 0)), pl.BlockSpec((16, 2 * ST), lambda i: (15, 0))]
        rim_args = (x_in, bc_in)
        extra_out = [SD((ST, WID), F32)]
    else:
        rims = [whole(8, WID), pl.BlockSpec((8, 2 * ST), lambda i: (0, WID // (2 * ST)))]
        rim_args = (rim, rim)
        extra_out = [SD((CTX, 16, WID), BF)]
    V = pltpu.HBM
    outs = [V((HT, WID), BF), V((HT, WID), BF), V((HT, ST), BF), V((HT, ST), BF), V((HT, HW), F32)]
    outs = outs + extra_out
    return pl.pallas_call(
        functools.partial(scan_in_body, last),
        grid=(1,),
        in_specs=[
            SMEM, pl.BlockSpec((HT, WID), lambda i: (at, 0)), rims[0],
            pl.BlockSpec((HT, 2 * ST), lambda i: (at, 0)), rims[1],
            whole(HEADS, TOK), whole(4, WID), whole(1, WID), whole(4, 2 * ST), whole(1, 2 * ST),
        ]
        + ([] if last else [whole(ST, WID), pl.BlockSpec((8, HW), lambda i: (HT // 8 - 1, 0))]),
        out_specs=[whole(*o.shape) for o in outs],
        out_shape=outs,
        scratch_shapes=[pltpu.VMEM((HT + 8, WID), F32), pltpu.VMEM((HT + 8, 2 * ST), F32)],
        compiler_params=params(),
        name="scan_in",
    )(rate, x_in, rim_args[0], bc_in, rim_args[1], codes, conv_x, bias_x, conv_bc, bias_bc, *carry)


def body(
    x_in, bc_in, z_in, codes, head_rate, conv_x, conv_bc, bias_x, bias_bc, skip, norm_gain, w_out
):
    place = lax.axis_index("tp")
    where = jnp.full((1,), place, jnp.int32)
    x_in, bc_in, z_in, w_out = in_hbm(x_in), in_hbm(bc_in), in_hbm(z_in), in_hbm(w_out)
    codes, conv_x, conv_bc = in_hbm(codes.T), in_hbm(conv_x), in_hbm(conv_bc)
    head_rate, skip = in_hbm(head_rate), in_hbm(skip)
    bias_x, bias_bc, gain = in_hbm(bias_x[None, :]), in_hbm(bias_bc[None, :]), in_hbm(norm_gain[None, :])

    swap = [(s, s ^ 1) for s in range(8)]
    w_sib = in_hbm(lax.ppermute(w_out, "tp", swap))
    rim = pl.pallas_call(
        rim_body,
        grid=(1,),
        in_specs=[
            pl.BlockSpec((8, WID), lambda i: (TOK // 8 - 1, 0)),
            pl.BlockSpec((8, 2 * ST), lambda i: (TOK // 8 - 1, 0)),
        ],
        out_specs=whole(8, WID + 2 * ST),
        out_shape=SD((8, WID + 2 * ST), BF),
        compiler_params=params(),
        name="rim",
    )(x_in, bc_in)
    rim = lax.ppermute(rim, "ctx", [(s, s + 1) for s in range(CTX - 1)])

    shared = (codes, conv_x, bias_x, conv_bc, bias_bc)
    xc1, xt1, b1, c1, cum1, state1 = scan_in(True, head_rate, x_in, None, bc_in, *shared)
    xc0, xt0, b0, c0, cum0, msg = scan_in(False, head_rate, x_in, rim, bc_in, *shared, state1, in_hbm(cum1))

    xt0, xt1, xc0, xc1, cum0, cum1, b0, b1, c0, c1 = map(
        in_hbm, (xt0, xt1, xc0, xc1, cum0, cum1, b0, b1, c0, c1)
    )
    got = lax.all_to_all(msg, "ctx", 0, 0, tiled=True)

    a1, a2 = pl.pallas_call(
        local_body,
        grid=(1,),
        in_specs=[
            SMEM, SMEM, whole(HT, WID), whole(HT, WID), whole(HT, WID), whole(HT, WID), whole(TOK, WID),
            whole(HT, HW), whole(HT, HW), whole(HT, ST), whole(HT, ST), whole(HT, ST), whole(HT, ST),
        ],
        out_specs=[whole(TOK, WID), whole(TOK, WID)],
        out_shape=[pltpu.HBM((TOK, WID), BF)] * 2,
        scratch_shapes=[pltpu.VMEM((TOK, TOK), BF), pltpu.VMEM((TOK, WID), F32)],
        compiler_params=params(),
        cost_estimate=pl.CostEstimate(flops=2 << 30, transcendentals=1 << 20, bytes_accessed=8 << 20),
        name="local",
    )(head_rate, skip, xt0, xt1, xc0, xc1, z_in, cum0, cum1, b0, b1, c0, c1)
    a1, a2 = in_hbm(a1), in_hbm(a2)

    prefix = pl.pallas_call(
        prefix_body,
        in_specs=[SMEM, VMEM, ANY],
        out_specs=VMEM,
        out_shape=SD((CTX, 8, WID), BF),
        compiler_params=params(0),
        name="prefix",
    )(head_rate, got, a1)
    incoming = lax.all_to_all(prefix, "ctx", 0, 0, tiled=True)

    normed = pl.pallas_call(
        norm_body,
        grid=(NB,),
        in_specs=[
            pl.BlockSpec((CTX, 8, CB), lambda i: (0, 0, i)), cols(TOK), cols(TOK), whole(HT, ST),
            whole(HT, ST), cols(1),
        ],
        out_specs=cols(TOK),
        out_shape=SD((TOK, WID), BF),
        scratch_shapes=[pltpu.VMEM((TOK, CB), F32)],
        compiler_params=params(),
        name="norm",
    )(incoming, a1, a2, c0, c1, gain)

    up = [(s, (s + 2) % 8) for s in range(8)]
    down = [(s, (s + 6) % 8) for s in range(8)]
    sibling = lax.ppermute(normed, "tp", swap)
    run = functools.partial(project, where, normed, sibling, w_out, w_sib)
    far_l, far_r = run(((2, 0), (2, 1)), ((), ()), BF)
    far_l, far_r = lax.ppermute(far_l, "tp", up), lax.ppermute(far_r, "tp", down)
    above_r, below_l = run(((1, 1), (3, 0)), ((), ()), BF)
    from_r, from_l = lax.ppermute(above_r, "tp", up), lax.ppermute(below_l, "tp", down)
    above_l, below_r = run(((1, 0), (3, 1)), ((far_l,), (far_r,)), BF)
    last_l, last_r = lax.ppermute(above_l, "tp", up), lax.ppermute(below_r, "tp", down)
    here_l, here_r = run(((0, 0), (0, 1)), ((from_l,), (from_r,)), F32)
    return pl.pallas_call(
        final_body,
        in_specs=[VMEM] * 4,
        out_specs=VMEM,
        out_shape=SD((TOK, WID), BF),
        compiler_params=params(0),
        name="final",
    )(here_l, here_r, last_l, last_r)


def solution(mesh):
    in_specs = (
        P("ctx", "tp"),
        P("ctx", None),
        P("ctx", "tp"),
        P("ctx", "tp"),
        P("tp"),
        P(None, "tp"),
        P(),
        P("tp"),
        P(),
        P("tp"),
        P("tp"),
        P("tp", None),
    )
    out_specs = P("ctx", "tp")
    return jax.shard_map(body, mesh=mesh, in_specs=in_specs, out_specs=out_specs, check_vma=False)
```

```python
import functools

import jax
import jax.numpy as jnp
from jax import lax
from jax.experimental import pallas as pl
from jax.experimental.pallas import tpu as pltpu
from jax.sharding import PartitionSpec as P

BF = jnp.bfloat16
F32 = jnp.float32
TOK = 512
HT = TOK // 2
BT = 128
EDGE = 3
MSG = 1152
WID = 1024
HALF = WID // 2
HEADS = 8
HW = 128
ST = 128
CTX = 16
CB = 512
NB = WID // CB
SEQ = TOK * CTX
DECAY = 12.288 / SEQ / 63.0
SCALE = 1.0 / (ST * SEQ) ** 0.5
ROWS = 32
SD = jax.ShapeDtypeStruct


def silu(v):
    half = 0.5 * v
    return half + half * jnp.tanh(half)


def mm(a, b):
    return jnp.dot(a, b, preferred_element_type=F32)


def triangle():
    row = lax.broadcasted_iota(jnp.int32, (BT, BT), 0)
    col = lax.broadcasted_iota(jnp.int32, (BT, BT), 1)
    return jnp.where(row >= col, 1.0, 0.0).astype(BF)


def head_row(ref, factor, at=0):
    lane = lax.broadcasted_iota(jnp.int32, (1, HW), 1)
    row = jnp.zeros((1, HW), F32)
    for h in range(HEADS):
        row = jnp.where(lane == at + h, ref[h] * factor, row)
    return row


def spread(compact, lane, rows=None):
    column = compact[:, lane : lane + 1]
    return jnp.broadcast_to(column, (rows or compact.shape[0], HW))


def row_ids(rows, width):
    return lax.broadcasted_iota(jnp.int32, (rows, width), 0)


def conv_part(source, w_ref, bias, r, rows, lo, hi):
    total = bias
    for k in range(4):
        total = total + w_ref[k : k + 1, lo:hi] * source[5 + k + r : 5 + k + r + rows, lo:hi]
    return total


def scan_in_body(
    rate_ref, x_ref, bc_ref, codes_ref, cx_ref, bx_ref, cbc_ref, bbc_ref,
    xc_ref, xt_ref, b_ref, c_ref, cum_ref, msg_ref, xe, be, acc, run, first, cum_first, b_first,
):
    step = pl.program_id(0)

    @pl.when(step == 0)
    def _():
        xe[0:8, :] = jnp.zeros((8, WID), F32)
        be[0:8, :] = jnp.zeros((8, 2 * ST), F32)
        be[8 + BT : 16 + BT, :] = jnp.zeros((8, 2 * ST), F32)
        run[...] = jnp.zeros((8, HW), F32)

    @pl.when(step > 0)
    def _():
        xe[0:8, :] = xe[BT : BT + 8, :]
        be[0:8, :] = be[BT : BT + 8, :]

    be[8 : 8 + BT, :] = bc_ref[...].astype(F32)
    xe[8 : 8 + BT, :] = x_ref[...].astype(F32)
    codes = jnp.concatenate([codes_ref[...].astype(F32), jnp.zeros((HW - HEADS, BT), F32)], axis=0)
    cum = lax.dot_general(
        triangle(), codes.astype(BF), (((1,), (1,)), ((), ())), preferred_element_type=F32
    )
    cum = cum + run[0:1, :]
    cum_ref[...] = cum
    run[...] = jnp.broadcast_to(cum[BT - 1 : BT, :], (8, HW))
    grow = jnp.exp(head_row(rate_ref, DECAY) * cum)

    @pl.when(step == 0)
    def _():
        first[...] = xe[8:16, :]
        cum_first[...] = cum_ref[0:8, :]
        b_first[...] = conv_part(be, cbc_ref, bbc_ref[:, :ST], 0, 8, 0, ST)

    for r in range(0, BT, ROWS):
        for ref, lo in ((b_ref, 0), (c_ref, ST)):
            part = conv_part(be, cbc_ref, bbc_ref[:, lo : lo + ST], r, ROWS, lo, lo + ST)
            ref[r : r + ROWS, :] = silu(part).astype(BF)
    for r in range(0, BT, ROWS):
        for h in range(HEADS):
            lo, hi = h * HW, (h + 1) * HW
            xc = silu(conv_part(xe, cx_ref, bx_ref[:, lo:hi], r, ROWS, lo, hi)).astype(BF)
            xc_ref[r : r + ROWS, lo:hi] = xc
            scaled = xc.astype(F32) * spread(grow[r : r + ROWS, :], h)
            xt_ref[r : r + ROWS, lo:hi] = scaled.astype(BF)

    @pl.when(step == 0)
    def _():
        head = xt_ref[0:16, :].astype(F32)
        xt_ref[0:16, :] = jnp.where(row_ids(16, WID) < EDGE, 0.0, head).astype(BF)
        acc[...] = jnp.zeros((ST, WID), F32)

    bt = b_ref[...].astype(F32).T.astype(BF)
    acc[...] += mm(bt, xt_ref[...])

    @pl.when(step == TOK // BT - 1)
    def _():
        row = row_ids(8, WID)
        last = pltpu.roll(xe[BT : BT + 8, :], EDGE, 0)
        bc_rows = [be[BT + 8 - EDGE + k : BT + 9 - EDGE + k, :] for k in range(EDGE)]
        bc_row = jnp.concatenate(bc_rows + [jnp.zeros((1, WID - EDGE * 2 * ST), F32)], axis=1)
        rows = jnp.where(row < EDGE, last, jnp.where(row < 2 * EDGE, pltpu.roll(first[...], EDGE, 0), 0.0))
        rows = jnp.where(row == 2 * EDGE, jnp.broadcast_to(bc_row, (8, WID)), rows)
        row = row_ids(8, HW)
        total = run[0:1, :]
        high = jnp.floor(total * (1.0 / 256.0))
        low = total - 256.0 * high
        heads = jnp.where(row < 5, pltpu.roll(cum_first[...], 2, 0), 0.0)
        heads = jnp.where(row == 0, high, jnp.where(row == 1, low, heads))
        heads = pltpu.roll(heads, HW // 2, 1)
        pad = jnp.zeros((HW - 8, HW), F32)
        b_last = conv_part(be, cbc_ref, jnp.zeros((1, ST), F32), BT, 8, 0, ST)
        b_last = jnp.concatenate([b_last, pad], axis=0).T
        b_head = jnp.concatenate([b_first[...], pad], axis=0).T
        for j in range(CTX):
            at = slice(8 * j, 8 * j + 8)
            msg_ref[j, :, 0:WID] = jnp.concatenate([acc[at, :], rows], axis=0).astype(BF)
            side = jnp.concatenate([b_last[at, :] + heads, b_head[at, :]], axis=0)
            msg_ref[j, :, WID:MSG] = side.astype(BF)


def prefix_body(rate_ref, cx_ref, bx_ref, r_ref, q_ref):
    rate = head_row(rate_ref, DECAY, HW // 2)
    state = jnp.zeros((8, WID), F32)
    before = jnp.zeros((8, WID), F32)
    side_before = jnp.zeros((8, HW), F32)
    edge_row = row_ids(8, WID) < EDGE
    for c in range(CTX):
        q_ref[c] = state.astype(BF)
        main = r_ref[c, :, 0:WID].astype(F32)
        side = r_ref[c, :, WID:MSG].astype(F32)
        rows = jnp.where(edge_row, before, main[8:16, :])
        before = main[8:16, :]
        pre = bx_ref[...] + cx_ref[0:1, :] * rows
        for k in range(1, 4):
            pre = pre + cx_ref[k : k + 1, :] * pltpu.roll(rows, 8 - k, 0)
        edge = silu(pre).astype(BF).astype(F32)
        heads = side[0:8, :]
        grow = jnp.exp(rate * pltpu.roll(heads, 6, 0))
        fade = jnp.exp(-rate * (256.0 * heads[0:1, :] + heads[1:2, :]))
        b_edge = silu(side_before + side[8:16, :]).astype(BF).astype(F32)
        side_before = heads
        parts = []
        for h in range(HEADS):
            lo, hi = h * HW, (h + 1) * HW
            scaled = (edge[:, lo:hi] * spread(grow, HW // 2 + h)).astype(BF).astype(F32)
            part = state[:, lo:hi] + main[0:8, lo:hi]
            for k in range(EDGE):
                part = part + spread(b_edge, k) * jnp.broadcast_to(scaled[k : k + 1, :], (8, HW))
            parts.append(spread(fade, HW // 2 + h, 8) * part)
        state = jnp.concatenate(parts, axis=1)


def local_body(
    place_ref, rate_ref, skip_ref, xt_ref, xc_ref, z_ref, cum_ref, b_ref, c_ref, got_ref, x_ref, bc_ref, cx_ref,
    bx_ref, cbc_ref, bbc_ref, after_ref, a1_ref, a2_ref, cm_ref, gram, prod, xe, be, bm, xt_first, xc_first,
):
    rim = pltpu.roll(got_ref[0, 8:16, 0:WID].astype(F32), 8 - EDGE, 0)
    live = place_ref[0] > 0
    xe[0:8, :] = jnp.where(live, rim, 0.0)
    xe[8:24, :] = x_ref[...].astype(F32)
    bc_row = got_ref[0, 8:16, 0 : EDGE * 2 * ST].astype(F32)[2 * EDGE : 2 * EDGE + 1, :]
    for k in range(EDGE):
        part = bc_row[:, k * 2 * ST : (k + 1) * 2 * ST]
        be[8 - EDGE + k : 9 - EDGE + k, :] = jnp.where(live, part, 0.0)
    be[8:24, :] = bc_ref[...].astype(F32)
    bm[...] = b_ref[...]
    cm_ref[...] = c_ref[...]
    bm[0:16, :] = silu(conv_part(be, cbc_ref, bbc_ref[:, :ST], 0, 16, 0, ST)).astype(BF)
    cm_ref[0:16, :] = silu(conv_part(be, cbc_ref, bbc_ref[:, ST:], 0, 16, ST, 2 * ST)).astype(BF)
    xt_first[...] = xt_ref[0:BT, :]
    xc_first[...] = xc_ref[0:ROWS, :]
    grow = jnp.exp(head_row(rate_ref, DECAY) * cum_ref[0:16, :])
    for h in range(HEADS):
        lo, hi = h * HW, (h + 1) * HW
        xc = silu(conv_part(xe, cx_ref, bx_ref[:, lo:hi], 0, 16, lo, hi)).astype(BF)
        xc_first[0:16, lo:hi] = xc
        xt_first[0:16, lo:hi] = (xc.astype(F32) * spread(grow, h)).astype(BF)
    for r in range(0, TOK, BT):
        size = r + BT
        part = lax.dot_general(
            cm_ref[r:size, :], bm[0:size, :], (((1,), (1,)), ((), ())), preferred_element_type=F32
        )
        row = lax.broadcasted_iota(jnp.int32, (BT, size), 0) + r
        col = lax.broadcasted_iota(jnp.int32, (BT, size), 1)
        gram[r:size, 0:size] = jnp.where(row >= col, part, 0.0).astype(BF)
        total = mm(gram[r:size, 0:BT], xt_first[...])
        if r:
            total = total + mm(gram[r:size, BT:size], xt_ref[BT:size, :])
        prod[r:size, :] = total
    rate = head_row(rate_ref, -DECAY)
    for r in range(0, TOK, ROWS):
        rs = slice(r, r + ROWS)
        fades = SCALE * jnp.exp(rate * cum_ref[rs, :])
        for h in range(HEADS):
            lo, hi = h * HW, (h + 1) * HW
            gate = silu(z_ref[rs, lo:hi].astype(F32))
            fade = spread(fades, h)
            xc = (xc_ref[rs, lo:hi] if r else xc_first[:, lo:hi]).astype(F32)
            both = (prod[rs, lo:hi] * fade + skip_ref[h] * xc) * gate
            a1_ref[rs, lo:hi] = both.astype(BF)
            a2_ref[rs, lo:hi] = (fade * gate).astype(BF)


def norm_body(q_ref, a1_ref, a2_ref, c_ref, gain_ref, n_ref, prod):
    state = q_ref[...].astype(F32).reshape(ST, CB).astype(BF)
    prod[...] = mm(c_ref[...], state)
    for r in range(0, TOK, ROWS):
        for h in range(0, CB, HW):
            rs, hs = slice(r, r + ROWS), slice(h, h + HW)
            gated = a1_ref[rs, hs].astype(F32) + a2_ref[rs, hs].astype(F32) * prod[rs, hs]
            power = jnp.mean(gated * gated, axis=-1, keepdims=True)
            n_ref[rs, hs] = (gated * lax.rsqrt(power + 1e-05) * gain_ref[:, hs]).astype(BF)


def project_body(adds, place_ref, own_ref, sib_ref, w_ref, ws_ref, *refs):
    step = pl.program_id(0)
    outs = refs[-2:]
    for k in range(2):

        @pl.when(step // 2 == k)
        def _():
            total = mm(own_ref[...], w_ref[...]) + mm(sib_ref[...], ws_ref[...])
            for ref in refs[adds * k : adds * (k + 1)]:
                total = total + ref[...].astype(F32)
            outs[k][...] = total.astype(outs[k].dtype)


def final_body(m0_ref, m1_ref, a_ref, b_ref, o_ref):
    o_ref[:, :HALF] = (m0_ref[...] + a_ref[...].astype(F32)).astype(BF)
    o_ref[:, HALF:] = (m1_ref[...] + b_ref[...].astype(F32)).astype(BF)


def params(dims=1):
    return pltpu.CompilerParams(
        dimension_semantics=("arbitrary",) * dims if dims else None, vmem_limit_bytes=20 << 20
    )


SMEM = pl.BlockSpec(memory_space=pltpu.SMEM)
VMEM = pl.BlockSpec(memory_space=pltpu.VMEM)
ANY = pl.BlockSpec(memory_space=pl.ANY)


def whole(*shape):
    return pl.BlockSpec(shape, lambda i: (0,) * len(shape))


def cols(rows, at=0):
    return pl.BlockSpec((rows, CB), lambda i: (at, i))


def in_hbm(a):
    return pltpu.with_memory_space_constraint(a, pltpu.HBM)


QUART = HALF // 2


def project(place, normed, sibling, w, w_sib, targets, addends, kind):
    def column(i, place_ref):
        index = place_ref[0]
        far = jnp.where(i < 2, targets[0][0], targets[1][0])
        side = jnp.where(i < 2, targets[0][1], targets[1][1])
        return 0, ((((index >> 1) + far) & 3) * 2 + (index & 1)) * 4 + side * 2 + (i & 1)

    whole2 = pl.BlockSpec((TOK, WID), lambda i, ix: (0, 0))
    weight = pl.BlockSpec((WID, QUART), column)
    halves = [
        pl.BlockSpec((TOK, QUART), lambda i, ix: (0, jnp.minimum(i, 1))),
        pl.BlockSpec((TOK, QUART), lambda i, ix: (0, jnp.maximum(i - 2, 0))),
    ]
    count = len(addends[0])
    return pl.pallas_call(
        functools.partial(project_body, count),
        out_shape=[SD((TOK, HALF), kind)] * 2,
        grid_spec=pltpu.PrefetchScalarGridSpec(
            num_scalar_prefetch=1,
            grid=(4,),
            in_specs=[whole2, whole2, weight, weight] + [halves[0]] * count + [halves[1]] * count,
            out_specs=halves,
        ),
        compiler_params=params(),
        name="project",
    )(place, normed, sibling, w, w_sib, *addends[0], *addends[1])


def body(
    x_in, bc_in, z_in, codes, head_rate, conv_x, conv_bc, bias_x, bias_bc, skip, norm_gain, w_out
):
    place = lax.axis_index("tp")
    where = jnp.full((1,), place, jnp.int32)
    x_in, bc_in, z_in, w_out = in_hbm(x_in), in_hbm(bc_in), in_hbm(z_in), in_hbm(w_out)
    codes, conv_x, conv_bc = in_hbm(codes.T), in_hbm(conv_x), in_hbm(conv_bc)
    head_rate, skip = in_hbm(head_rate), in_hbm(skip)
    bias_x, bias_bc, gain = in_hbm(bias_x[None, :]), in_hbm(bias_bc[None, :]), in_hbm(norm_gain[None, :])

    swap = [(s, s ^ 1) for s in range(8)]
    w_sib = in_hbm(lax.ppermute(w_out, "tp", swap))
    taps = (conv_x, bias_x, conv_bc, bias_bc)
    taps_specs = [whole(4, WID), whole(1, WID), whole(4, 2 * ST), whole(1, 2 * ST)]

    def tokens(width):
        return pl.BlockSpec((BT, width), lambda i: (i, 0))

    xc, xt, b_map, c_map, cum, msg = pl.pallas_call(
        scan_in_body,
        grid=(TOK // BT,),
        in_specs=[
            SMEM, tokens(WID), tokens(2 * ST), pl.BlockSpec((HEADS, BT), lambda i: (0, i)), *taps_specs,
        ],
        out_specs=[tokens(WID), tokens(WID), tokens(ST), tokens(ST), tokens(HW), whole(CTX, 16, MSG)],
        out_shape=[
            pltpu.HBM((TOK, WID), BF), pltpu.HBM((TOK, WID), BF), pltpu.HBM((TOK, ST), BF),
            pltpu.HBM((TOK, ST), BF), pltpu.HBM((TOK, HW), F32), SD((CTX, 16, MSG), BF),
        ],
        scratch_shapes=[
            pltpu.VMEM((BT + 8, WID), F32), pltpu.VMEM((BT + 16, 2 * ST), F32), pltpu.VMEM((ST, WID), F32),
            pltpu.VMEM((8, HW), F32), pltpu.VMEM((8, WID), F32), pltpu.VMEM((8, HW), F32),
            pltpu.VMEM((8, ST), F32),
        ],
        compiler_params=params(),
        name="scan_in",
    )(head_rate, x_in, bc_in, codes, *taps)
    got = lax.all_to_all(msg, "ctx", 0, 0, tiled=True)

    prefix = pl.pallas_call(
        prefix_body,
        in_specs=[SMEM, VMEM, VMEM, VMEM],
        out_specs=VMEM,
        out_shape=SD((CTX, 8, WID), BF),
        compiler_params=params(0),
        name="prefix",
    )(head_rate, conv_x, bias_x, got)
    incoming = lax.all_to_all(prefix, "ctx", 0, 0, tiled=True)

    def fixed(*shape):
        return pl.BlockSpec(shape, lambda i, ix: (0,) * len(shape))

    ctx = jnp.full((1,), lax.axis_index("ctx"), jnp.int32)
    a1, a2, c_map = pl.pallas_call(
        local_body,
        out_shape=[pltpu.HBM((TOK, WID), BF)] * 2 + [SD((TOK, ST), BF)],
        grid_spec=pltpu.PrefetchScalarGridSpec(
            num_scalar_prefetch=1,
            grid=(1,),
            in_specs=[
                SMEM, SMEM, fixed(TOK, WID), fixed(TOK, WID), fixed(TOK, WID), fixed(TOK, HW), fixed(TOK, ST),
                fixed(TOK, ST), pl.BlockSpec((1, 16, MSG), lambda i, ix: (jnp.maximum(ix[0] - 1, 0), 0, 0)),
                fixed(16, WID), fixed(16, 2 * ST), fixed(4, WID), fixed(1, WID), fixed(4, 2 * ST),
                fixed(1, 2 * ST), ANY,
            ],
            out_specs=[fixed(TOK, WID), fixed(TOK, WID), fixed(TOK, ST)],
            scratch_shapes=[
                pltpu.VMEM((TOK, TOK), BF), pltpu.VMEM((TOK, WID), F32), pltpu.VMEM((24, WID), F32),
                pltpu.VMEM((24, 2 * ST), F32), pltpu.VMEM((TOK, ST), BF), pltpu.VMEM((BT, WID), BF),
                pltpu.VMEM((ROWS, WID), BF),
            ],
        ),
        compiler_params=params(),
        name="local",
    )(ctx, head_rate, skip, *map(in_hbm, (xt, xc)), z_in, *map(in_hbm, (cum, b_map, c_map)), got, x_in, bc_in,
      *taps, prefix)
    a1, a2 = in_hbm(a1), in_hbm(a2)

    normed = pl.pallas_call(
        norm_body,
        grid=(NB,),
        in_specs=[
            pl.BlockSpec((CTX, 8, CB), lambda i: (0, 0, i)), cols(TOK), cols(TOK), whole(TOK, ST), cols(1),
        ],
        out_specs=cols(TOK),
        out_shape=SD((TOK, WID), BF),
        scratch_shapes=[pltpu.VMEM((TOK, CB), F32)],
        compiler_params=params(),
        name="norm",
    )(incoming, a1, a2, c_map, gain)

    up = [(s, (s + 2) % 8) for s in range(8)]
    down = [(s, (s + 6) % 8) for s in range(8)]
    sibling = lax.ppermute(normed, "tp", swap)
    run = functools.partial(project, where, normed, sibling, w_out, w_sib)
    far_l, far_r = run(((2, 0), (2, 1)), ((), ()), BF)
    far_l, far_r = lax.ppermute(far_l, "tp", up), lax.ppermute(far_r, "tp", down)
    above_r, below_l = run(((1, 1), (3, 0)), ((), ()), BF)
    from_r, from_l = lax.ppermute(above_r, "tp", up), lax.ppermute(below_l, "tp", down)
    above_l, below_r = run(((1, 0), (3, 1)), ((far_l,), (far_r,)), BF)
    last_l, last_r = lax.ppermute(above_l, "tp", up), lax.ppermute(below_r, "tp", down)
    here_l, here_r = run(((0, 0), (0, 1)), ((from_l,), (from_r,)), F32)
    return pl.pallas_call(
        final_body,
        in_specs=[VMEM] * 4,
        out_specs=VMEM,
        out_shape=SD((TOK, WID), BF),
        compiler_params=params(0),
        name="final",
    )(here_l, here_r, last_l, last_r)


def solution(mesh):
    in_specs = (
        P("ctx", "tp"),
        P("ctx", None),
        P("ctx", "tp"),
        P("ctx", "tp"),
        P("tp"),
        P(None, "tp"),
        P(),
        P("tp"),
        P(),
        P("tp"),
        P("tp"),
        P("tp", None),
    )
    out_specs = P("ctx", "tp")
    return jax.shard_map(body, mesh=mesh, in_specs=in_specs, out_specs=out_specs, check_vma=False)
```

```python
import functools

import jax
import jax.numpy as jnp
from jax import lax
from jax.experimental import pallas as pl
from jax.experimental.pallas import tpu as pltpu
from jax.sharding import PartitionSpec as P

BF = jnp.bfloat16
F32 = jnp.float32
TOK = 512
HT = TOK // 2
BT = 128
EDGE = 3
MSG = 1152
WID = 1024
HALF = WID // 2
HEADS = 8
HW = 128
ST = 128
CTX = 16
SEQ = TOK * CTX
DECAY = 12.288 / SEQ / 63.0
SCALE = 1.0 / (ST * SEQ) ** 0.5
ROWS = 64
SD = jax.ShapeDtypeStruct


def silu(v):
    half = 0.5 * v
    return half + half * jnp.tanh(half)


def mm(a, b):
    return jnp.dot(a, b, preferred_element_type=F32)


def head_row(ref, factor, at=0):
    lane = lax.broadcasted_iota(jnp.int32, (1, HW), 1)
    row = jnp.zeros((1, HW), F32)
    for h in range(HEADS):
        row = jnp.where(lane == at + h, ref[h] * factor, row)
    return row


def spread(compact, lane, rows=None):
    column = compact[:, lane : lane + 1]
    return jnp.broadcast_to(column, (rows or compact.shape[0], HW))


def row_ids(rows, width):
    return lax.broadcasted_iota(jnp.int32, (rows, width), 0)


def conv_part(big, w_ref, bias, lo, hi):
    count = big.shape[0] // 8
    row = row_ids(8, hi - lo)
    total = bias + w_ref[3:4, lo:hi] * big[8:]
    for k in range(1, 4):
        rolled = [pltpu.roll(big[8 * t : 8 * t + 8], k, 0) for t in range(count)]
        moved = [jnp.where(row < k, rolled[t], rolled[t + 1]) for t in range(count - 1)]
        total = total + w_ref[3 - k : 4 - k, lo:hi] * jnp.concatenate(moved, axis=0)
    return total


def with_rim(ref, r, rows, lo, hi):
    body = ref[r : r + rows, lo:hi].astype(F32)
    if r == 0:
        return jnp.concatenate([jnp.zeros((8, hi - lo), F32), body], axis=0)
    return jnp.concatenate([ref[r - 16 : r, lo:hi].astype(F32)[8:], body], axis=0)


def code_sums(codes_ref, count=TOK):
    codes = jnp.concatenate([codes_ref[...].astype(F32), jnp.zeros((HW - HEADS, count), F32)], axis=0)
    row = lax.broadcasted_iota(jnp.int32, (count, count), 0)
    col = lax.broadcasted_iota(jnp.int32, (count, count), 1)
    return lax.dot_general(
        jnp.where(row >= col, 1.0, 0.0).astype(BF), codes.astype(BF), (((1,), (1,)), ((), ())),
        preferred_element_type=F32,
    )


def scan_in_body(
    rate_ref, x_hbm, bc_hbm, codes_hbm, cx_hbm, bx_hbm, cbc_hbm, bbc_hbm, xt_hbm, msg_ref,
    x_ref, bc_ref, codes_ref, cx_ref, bx_ref, cbc_ref, bbc_ref, xt_ref, b_ref, sems,
):
    chunks = [slice(r, r + BT) for r in range(0, TOK, BT)]
    pairs = [
        (codes_hbm, codes_ref), (bc_hbm, bc_ref), (cbc_hbm, cbc_ref), (bbc_hbm, bbc_ref), (cx_hbm, cx_ref),
        (bx_hbm, bx_ref),
    ]
    loads = [pltpu.make_async_copy(src, dst, sems.at[2, k]) for k, (src, dst) in enumerate(pairs)]

    def copy(src, dst, k, i):
        return pltpu.make_async_copy(src.at[chunks[i]], dst.at[chunks[i]], sems.at[k, i])

    for load in loads:
        load.start()
    for i in range(len(chunks)):
        copy(x_hbm, x_ref, 0, i).start()
    for load in loads[:4]:
        load.wait()
    cum = code_sums(codes_ref)
    grow = jnp.exp(head_row(rate_ref, DECAY) * cum)
    for r in range(0, TOK, ROWS):
        part = conv_part(with_rim(bc_ref, r, ROWS, 0, ST), cbc_ref, bbc_ref[:, :ST], 0, ST)
        b_ref[r : r + ROWS, :] = silu(part)
    bt = b_ref[...].T.astype(BF)
    for load in loads[4:]:
        load.wait()
    for i in range(len(chunks)):
        copy(x_hbm, x_ref, 0, i).wait()
        for r in range(i * BT, (i + 1) * BT, ROWS):
            for h in range(HEADS):
                lo, hi = h * HW, (h + 1) * HW
                part = conv_part(with_rim(x_ref, r, ROWS, lo, hi), cx_ref, bx_ref[:, lo:hi], lo, hi)
                xc = silu(part).astype(BF)
                scaled = xc.astype(F32) * spread(grow[r : r + ROWS, :], h)
                if r == 0:
                    scaled = jnp.where(row_ids(ROWS, HW) < EDGE, 0.0, scaled)
                xt_ref[r : r + ROWS, lo:hi] = scaled.astype(BF)
        copy(xt_ref, xt_hbm, 1, i).start()
    state = mm(bt, xt_ref[...])
    row = row_ids(8, WID)
    last = pltpu.roll(x_ref[TOK - 16 : TOK, :].astype(F32)[8:], EDGE, 0)
    head = pltpu.roll(x_ref[0:16, :].astype(F32)[0:8], EDGE, 0)
    bc_last = bc_ref[TOK - 16 : TOK, :].astype(F32)[8:]
    bc_head = bc_ref[0:16, :].astype(F32)[0:8]
    bc_rows = [bc_last[8 - EDGE + k : 9 - EDGE + k, :] for k in range(EDGE)]
    bc_row = jnp.concatenate(bc_rows + [jnp.zeros((1, WID - EDGE * 2 * ST), F32)], axis=1)
    rows = jnp.where(row < EDGE, last, jnp.where(row < 2 * EDGE, head, 0.0))
    rows = jnp.where(row == 2 * EDGE, jnp.broadcast_to(bc_row, (8, WID)), rows)
    row = row_ids(8, HW)
    total = cum[TOK - 1 : TOK, :]
    high = jnp.floor(total * (1.0 / 256.0))
    low = total - 256.0 * high
    heads = jnp.where(row < 5, pltpu.roll(cum[0:8, :], 2, 0), 0.0)
    heads = jnp.where(row == 0, high, jnp.where(row == 1, low, heads))
    heads = pltpu.roll(heads, HW // 2, 1)
    pad = jnp.zeros((HW - 8, HW), F32)
    none = jnp.zeros((8, ST), F32)
    b_last = conv_part(jnp.concatenate([bc_last[:, :ST], none], axis=0), cbc_ref, none[0:1], 0, ST)
    b_head = conv_part(jnp.concatenate([none, bc_head[:, :ST]], axis=0), cbc_ref, bbc_ref[:, :ST], 0, ST)
    b_last = jnp.concatenate([b_last, pad], axis=0).T
    b_head = jnp.concatenate([b_head, pad], axis=0).T
    for j in range(CTX):
        at = slice(8 * j, 8 * j + 8)
        msg_ref[j, :, 0:WID] = jnp.concatenate([state[at, :], rows], axis=0).astype(BF)
        side = jnp.concatenate([b_last[at, :] + heads, b_head[at, :]], axis=0)
        msg_ref[j, :, WID:MSG] = side.astype(BF)
    for i in range(len(chunks)):
        copy(xt_ref, xt_hbm, 1, i).wait()


def prefix_body(rate_ref, cx_ref, bx_ref, r_ref, after_ref, q_ref):
    rate = head_row(rate_ref, DECAY, HW // 2)
    state = jnp.zeros((8, WID), F32)
    before = jnp.zeros((8, WID), F32)
    side_before = jnp.zeros((8, HW), F32)
    edge_row = row_ids(8, WID) < EDGE
    for c in range(CTX):
        main = r_ref[c, :, 0:WID].astype(F32)
        side = r_ref[c, :, WID:MSG].astype(F32)
        rows = jnp.where(edge_row, before, main[8:16, :])
        before = main[8:16, :]
        pre = bx_ref[...] + cx_ref[0:1, :] * rows
        for k in range(1, 4):
            pre = pre + cx_ref[k : k + 1, :] * pltpu.roll(rows, 8 - k, 0)
        edge = silu(pre).astype(BF).astype(F32)
        heads = side[0:8, :]
        grow = jnp.exp(rate * pltpu.roll(heads, 6, 0))
        fade = jnp.exp(-rate * (256.0 * heads[0:1, :] + heads[1:2, :]))
        b_edge = silu(side_before + side[8:16, :]).astype(BF).astype(F32)
        side_before = heads
        parts = []
        for h in range(HEADS):
            lo, hi = h * HW, (h + 1) * HW
            scaled = (edge[:, lo:hi] * spread(grow, HW // 2 + h)).astype(BF).astype(F32)
            part = state[:, lo:hi]
            for k in range(EDGE):
                part = part + spread(b_edge, k) * jnp.broadcast_to(scaled[k : k + 1, :], (8, HW))
            q_ref[c, :, lo:hi] = part.astype(BF)
            parts.append(spread(fade, HW // 2 + h, 8) * (part + main[0:8, lo:hi]))
        state = jnp.concatenate(parts, axis=1)


def local_body(
    rate_ref, skip_ref, xt_ref, z_ref, codes_ref, bc_ref, cbc_ref, bbc_ref, a1_ref, a2_ref, cm_ref, gram, prod, bm,
):
    cum = code_sums(codes_ref)
    for r in range(0, TOK, ROWS):
        for ref, lo in ((bm, 0), (cm_ref, ST)):
            hi = lo + ST
            part = conv_part(with_rim(bc_ref, r, ROWS, lo, hi), cbc_ref, bbc_ref[:, lo:hi], lo, hi)
            ref[r : r + ROWS, :] = silu(part).astype(BF)
    for r in range(0, TOK, BT):
        size = r + BT
        part = lax.dot_general(
            cm_ref[r:size, :], bm[0:size, :], (((1,), (1,)), ((), ())), preferred_element_type=F32
        )
        row = lax.broadcasted_iota(jnp.int32, (BT, size), 0) + r
        col = lax.broadcasted_iota(jnp.int32, (BT, size), 1)
        gram[r:size, 0:size] = jnp.where(row >= col, part, 0.0).astype(BF)
        prod[r:size, :] = mm(gram[r:size, 0:size], xt_ref[0:size, :])
    fades = jnp.exp(head_row(rate_ref, -DECAY) * cum)
    for r in range(0, TOK, ROWS):
        rs = slice(r, r + ROWS)
        for h in range(HEADS):
            lo, hi = h * HW, (h + 1) * HW
            gate = silu(z_ref[rs, lo:hi].astype(F32))
            fade = spread(fades[rs, :], h)
            total = prod[rs, lo:hi] * SCALE + skip_ref[h] * xt_ref[rs, lo:hi].astype(F32)
            fade = fade * gate
            a1_ref[rs, lo:hi] = (total * fade).astype(BF)
            a2_ref[rs, lo:hi] = (SCALE * fade).astype(BF)


def patch_body(
    place_ref, rate_ref, skip_ref, got_ref, x_ref, bc_ref, z_ref, codes_ref, cx_ref, bx_ref, cbc_ref, bbc_ref,
    after_ref, a1_ref, cm_ref, xe, be,
):
    live = place_ref[0] > 0
    rim = got_ref[0, 8:16, 0:WID].astype(F32)
    xe[0:8, :] = jnp.where(live, pltpu.roll(rim, 8 - EDGE, 0), 0.0)
    xe[8:24, :] = x_ref[...].astype(F32)
    for k in range(EDGE):
        part = rim[2 * EDGE : 2 * EDGE + 1, k * 2 * ST : (k + 1) * 2 * ST]
        be[8 - EDGE + k : 9 - EDGE + k, :] = jnp.where(live, part, 0.0)
    be[8:24, :] = bc_ref[...].astype(F32)
    cum = code_sums(codes_ref, HW)[0:16, :]
    grow = jnp.exp(head_row(rate_ref, DECAY) * cum)
    fades = jnp.exp(head_row(rate_ref, -DECAY) * cum)
    bm = silu(conv_part(be[:, :ST], cbc_ref, bbc_ref[:, :ST], 0, ST)).astype(BF)
    cm = silu(conv_part(be[:, ST:], cbc_ref, bbc_ref[:, ST:], ST, 2 * ST)).astype(BF)
    cm_ref[...] = cm
    part = lax.dot_general(cm, bm, (((1,), (1,)), ((), ())), preferred_element_type=F32)
    row = lax.broadcasted_iota(jnp.int32, (16, 16), 0)
    col = lax.broadcasted_iota(jnp.int32, (16, 16), 1)
    edge = jnp.where(row < col, -part, 0.0)
    gram = jnp.where(col < EDGE, edge, jnp.where(row >= col, part, 0.0)).astype(BF)
    for h in range(HEADS):
        lo, hi = h * HW, (h + 1) * HW
        xc = silu(conv_part(xe[:, lo:hi], cx_ref, bx_ref[:, lo:hi], lo, hi)).astype(BF).astype(F32)
        total = mm(gram, (xc * spread(grow, h)).astype(BF))
        gate = silu(z_ref[:, lo:hi].astype(F32))
        a1_ref[:, lo:hi] = ((total * (SCALE * spread(fades, h)) + skip_ref[h] * xc) * gate).astype(BF)


def norm_body(first, q_ref, a1_ref, a2_ref, c_ref, gain_ref, *refs):
    n_ref, prod = refs[-2:]
    state = q_ref[...].astype(F32).reshape(ST, WID).astype(BF)
    prod[...] = mm(c_ref[...], state)
    if first:
        prod[0:16, :] = mm(refs[1][...], state)
    for r in range(0, HT, ROWS):
        for h in range(HEADS):
            rs, hs = slice(r, r + ROWS), slice(h * HW, (h + 1) * HW)
            local = a1_ref[rs, hs]
            if first and r == 0:
                local = jnp.concatenate([refs[0][:, hs], local[16:, :]], axis=0)
            gated = local.astype(F32) + a2_ref[rs, hs].astype(F32) * prod[rs, hs]
            power = jnp.mean(gated * gated, axis=-1, keepdims=True)
            n_ref[rs, hs] = (gated * lax.rsqrt(power + 1e-05) * gain_ref[:, hs]).astype(BF)


def project_body(parts, adds, place_ref, *refs):
    step = pl.program_id(0)
    owns, sibs, (w_ref, ws_ref), rest = refs[:parts], refs[parts : 2 * parts], refs[2 * parts : 2 * parts + 2], refs[
        2 * parts + 2 :
    ]
    outs = rest[-2:]
    for k in range(2):

        @pl.when(step // 2 == k)
        def _():
            for p in range(parts):
                total = mm(owns[p][...], w_ref[...]) + mm(sibs[p][...], ws_ref[...])
                rows = slice(p * HT, (p + 1) * HT)
                mine = rest[adds * k : adds * (k + 1)]
                if adds == 2:
                    total = total + mine[p][...].astype(F32)
                elif adds == 1:
                    total = total + mine[0][rows, :].astype(F32)
                outs[k][rows, :] = total.astype(outs[k].dtype)


def final_body(m0_ref, m1_ref, a_ref, b_ref, o_ref):
    o_ref[:, :HALF] = (m0_ref[...] + a_ref[...].astype(F32)).astype(BF)
    o_ref[:, HALF:] = (m1_ref[...] + b_ref[...].astype(F32)).astype(BF)


def params(dims=1):
    return pltpu.CompilerParams(
        dimension_semantics=("arbitrary",) * dims if dims else None, vmem_limit_bytes=20 << 20
    )


SMEM = pl.BlockSpec(memory_space=pltpu.SMEM)
VMEM = pl.BlockSpec(memory_space=pltpu.VMEM)
ANY = pl.BlockSpec(memory_space=pl.ANY)


def whole(*shape):
    return pl.BlockSpec(shape, lambda i: (0,) * len(shape))


def in_hbm(a):
    return pltpu.with_memory_space_constraint(a, pltpu.HBM)


QUART = HALF // 2


def project(place, owns, sibs, w, w_sib, targets, addends, kind):
    def column(i, place_ref):
        index = place_ref[0]
        far = jnp.where(i < 2, targets[0][0], targets[1][0])
        side = jnp.where(i < 2, targets[0][1], targets[1][1])
        return 0, ((((index >> 1) + far) & 3) * 2 + (index & 1)) * 4 + side * 2 + (i & 1)

    parts = len(owns)
    tokens = pl.BlockSpec((HT, WID), lambda i, ix: (0, 0))
    weight = pl.BlockSpec((WID, QUART), column)

    def halves(rows):
        return [
            pl.BlockSpec((rows, QUART), lambda i, ix: (0, jnp.minimum(i, 1))),
            pl.BlockSpec((rows, QUART), lambda i, ix: (0, jnp.maximum(i - 2, 0))),
        ]

    count = len(addends[0])
    add_specs = [halves(a.shape[0])[k] for k in range(2) for a in addends[k]]
    return pl.pallas_call(
        functools.partial(project_body, parts, count),
        out_shape=[SD((parts * HT, HALF), kind)] * 2,
        grid_spec=pltpu.PrefetchScalarGridSpec(
            num_scalar_prefetch=1,
            grid=(4,),
            in_specs=[tokens] * (2 * parts) + [weight, weight] + add_specs,
            out_specs=halves(parts * HT),
        ),
        compiler_params=params(),
        name="project",
    )(place, *owns, *sibs, w, w_sib, *addends[0], *addends[1])


def body(
    x_in, bc_in, z_in, codes, head_rate, conv_x, conv_bc, bias_x, bias_bc, skip, norm_gain, w_out
):
    place = lax.axis_index("tp")
    where = jnp.full((1,), place, jnp.int32)
    x_in, bc_in, z_in, w_out = in_hbm(x_in), in_hbm(bc_in), in_hbm(z_in), in_hbm(w_out)
    codes, conv_x, conv_bc = in_hbm(codes.T), in_hbm(conv_x), in_hbm(conv_bc)
    head_rate, skip = in_hbm(head_rate), in_hbm(skip)
    bias_x, bias_bc, gain = in_hbm(bias_x[None, :]), in_hbm(bias_bc[None, :]), in_hbm(norm_gain[None, :])

    swap = [(s, s ^ 1) for s in range(8)]
    w_sib = in_hbm(lax.ppermute(w_out, "tp", swap))
    taps = (conv_x, bias_x, conv_bc, bias_bc)
    buf = pltpu.VMEM
    xt, msg = pl.pallas_call(
        scan_in_body,
        in_specs=[SMEM] + [ANY] * 7,
        out_specs=[ANY, VMEM],
        out_shape=[pltpu.HBM((TOK, WID), BF), SD((CTX, 16, MSG), BF)],
        scratch_shapes=[
            buf((TOK, WID), BF), buf((TOK, 2 * ST), BF), buf((HEADS, TOK), jnp.int32), buf((4, WID), F32),
            buf((1, WID), F32), buf((4, 2 * ST), F32), buf((1, 2 * ST), F32), buf((TOK, WID), BF), buf((TOK, ST), F32),
            pltpu.SemaphoreType.DMA((3, 8)),
        ],
        compiler_params=params(0),
        name="scan_in",
    )(head_rate, x_in, bc_in, codes, *taps)
    got = lax.all_to_all(msg, "ctx", 0, 0, tiled=True)

    a1, a2, c_map = pl.pallas_call(
        local_body,
        grid=(1,),
        in_specs=[
            SMEM, SMEM, whole(TOK, WID), whole(TOK, WID), whole(HEADS, TOK), whole(TOK, 2 * ST), whole(4, 2 * ST),
            whole(1, 2 * ST),
        ],
        out_specs=[whole(TOK, WID), whole(TOK, WID), whole(TOK, ST)],
        out_shape=[pltpu.HBM((TOK, WID), BF), pltpu.HBM((TOK, WID), BF), pltpu.HBM((TOK, ST), BF)],
        scratch_shapes=[buf((TOK, TOK), BF), buf((TOK, WID), F32), buf((TOK, ST), BF)],
        compiler_params=params(),
        name="local",
    )(head_rate, skip, in_hbm(xt), z_in, codes, bc_in, conv_bc, bias_bc)
    a1, a2, c_map = in_hbm(a1), in_hbm(a2), in_hbm(c_map)

    prefix = pl.pallas_call(
        prefix_body,
        in_specs=[SMEM, VMEM, VMEM, VMEM, ANY],
        out_specs=VMEM,
        out_shape=SD((CTX, 8, WID), BF),
        compiler_params=params(0),
        name="prefix",
    )(head_rate, conv_x, bias_x, got, a1)
    incoming = lax.all_to_all(prefix, "ctx", 0, 0, tiled=True)

    def fixed(*shape):
        return pl.BlockSpec(shape, lambda i, ix: (0,) * len(shape))

    ctx = jnp.full((1,), lax.axis_index("ctx"), jnp.int32)
    a_first, c_first = pl.pallas_call(
        patch_body,
        out_shape=[SD((16, WID), BF), SD((16, ST), BF)],
        grid_spec=pltpu.PrefetchScalarGridSpec(
            num_scalar_prefetch=1,
            grid=(1,),
            in_specs=[
                SMEM, SMEM, pl.BlockSpec((1, 16, MSG), lambda i, ix: (jnp.maximum(ix[0] - 1, 0), 0, 0)),
                fixed(16, WID), fixed(16, 2 * ST), fixed(16, WID), fixed(HEADS, HW), fixed(4, WID), fixed(1, WID),
                fixed(4, 2 * ST), fixed(1, 2 * ST), ANY,
            ],
            out_specs=[fixed(16, WID), fixed(16, ST)],
            scratch_shapes=[buf((24, WID), F32), buf((24, 2 * ST), F32)],
        ),
        compiler_params=params(),
        name="patch",
    )(ctx, head_rate, skip, got, x_in, bc_in, z_in, codes, *taps, prefix)

    def norm(half, first):
        rows = pl.BlockSpec((HT, WID), lambda i: (half, 0))
        return pl.pallas_call(
            functools.partial(norm_body, half == 0),
            grid=(1,),
            in_specs=[
                whole(CTX, 8, WID), rows, rows, pl.BlockSpec((HT, ST), lambda i: (half, 0)), whole(1, WID),
                *[ANY if half else whole(*a.shape) for a in first],
            ],
            out_specs=whole(HT, WID),
            out_shape=SD((HT, WID), BF),
            scratch_shapes=[buf((HT, WID), F32)],
            compiler_params=params(),
            name="norm",
        )(incoming, a1, a2, c_map, gain, *first)

    up = [(s, (s + 2) % 8) for s in range(8)]
    down = [(s, (s + 6) % 8) for s in range(8)]
    n0 = norm(0, (a_first, c_first))
    s0 = lax.ppermute(n0, "tp", swap)
    n1 = norm(1, (a_first,))
    s1 = lax.ppermute(n1, "tp", swap)
    far = ((2, 0), (2, 1))
    fl0, fr0 = project(where, (n0,), (s0,), w_out, w_sib, far, ((), ()), BF)
    fl0, fr0 = lax.ppermute(fl0, "tp", up), lax.ppermute(fr0, "tp", down)
    fl1, fr1 = project(where, (n1,), (s1,), w_out, w_sib, far, ((), ()), BF)
    fl1, fr1 = lax.ppermute(fl1, "tp", up), lax.ppermute(fr1, "tp", down)
    run = functools.partial(project, where, (n0, n1), (s0, s1), w_out, w_sib)
    above_r, below_l = run(((1, 1), (3, 0)), ((), ()), BF)
    from_r, from_l = lax.ppermute(above_r, "tp", up), lax.ppermute(below_l, "tp", down)
    above_l, below_r = run(((1, 0), (3, 1)), ((fl0, fl1), (fr0, fr1)), BF)
    last_l, last_r = lax.ppermute(above_l, "tp", up), lax.ppermute(below_r, "tp", down)
    here_l, here_r = run(((0, 0), (0, 1)), ((from_l,), (from_r,)), F32)
    return pl.pallas_call(
        final_body,
        in_specs=[VMEM] * 4,
        out_specs=VMEM,
        out_shape=SD((TOK, WID), BF),
        compiler_params=params(0),
        name="final",
    )(here_l, here_r, last_l, last_r)


def solution(mesh):
    in_specs = (
        P("ctx", "tp"),
        P("ctx", None),
        P("ctx", "tp"),
        P("ctx", "tp"),
        P("tp"),
        P(None, "tp"),
        P(),
        P("tp"),
        P(),
        P("tp"),
        P("tp"),
        P("tp", None),
    )
    out_specs = P("ctx", "tp")
    return jax.shard_map(body, mesh=mesh, in_specs=in_specs, out_specs=out_specs, check_vma=False)
```

```python
import functools

import jax
import jax.numpy as jnp
from jax import lax
from jax.experimental import pallas as pl
from jax.experimental.pallas import tpu as pltpu
from jax.sharding import PartitionSpec as P

BF = jnp.bfloat16
F32 = jnp.float32
TOK = 512
HT = TOK // 2
BT = 128
EDGE = 3
MSG = 1152
WID = 1024
HALF = WID // 2
HEADS = 8
HW = 128
ST = 128
CTX = 16
SEQ = TOK * CTX
DECAY = 12.288 / SEQ / 63.0
SCALE = 1.0 / (ST * SEQ) ** 0.5
ROWS = 64
SD = jax.ShapeDtypeStruct


def silu(v):
    half = 0.5 * v
    return half + half * jnp.tanh(half)


def mm(a, b):
    return jnp.dot(a, b, preferred_element_type=F32)


def head_row(ref, factor, at=0):
    lane = lax.broadcasted_iota(jnp.int32, (1, HW), 1)
    row = jnp.zeros((1, HW), F32)
    for h in range(HEADS):
        row = jnp.where(lane == at + h, ref[h] * factor, row)
    return row


def spread(compact, lane, rows=None):
    column = compact[:, lane : lane + 1]
    return jnp.broadcast_to(column, (rows or compact.shape[0], HW))


def row_ids(rows, width):
    return lax.broadcasted_iota(jnp.int32, (rows, width), 0)


def conv_part(big, w_ref, bias, lo, hi):
    count = big.shape[0] // 8
    row = row_ids(8, hi - lo)
    total = bias + w_ref[3:4, lo:hi] * big[8:]
    for k in range(1, 4):
        rolled = [pltpu.roll(big[8 * t : 8 * t + 8], k, 0) for t in range(count)]
        moved = [jnp.where(row < k, rolled[t], rolled[t + 1]) for t in range(count - 1)]
        total = total + w_ref[3 - k : 4 - k, lo:hi] * jnp.concatenate(moved, axis=0)
    return total


def with_rim(ref, r, rows, lo, hi):
    body = ref[r : r + rows, lo:hi].astype(F32)
    if r == 0:
        return jnp.concatenate([jnp.zeros((8, hi - lo), F32), body], axis=0)
    return jnp.concatenate([ref[r - 16 : r, lo:hi].astype(F32)[8:], body], axis=0)


def code_sums(codes_ref, count=TOK):
    codes = jnp.concatenate([codes_ref[...].astype(F32), jnp.zeros((HW - HEADS, count), F32)], axis=0)
    row = lax.broadcasted_iota(jnp.int32, (count, count), 0)
    col = lax.broadcasted_iota(jnp.int32, (count, count), 1)
    return lax.dot_general(
        jnp.where(row >= col, 1.0, 0.0).astype(BF), codes.astype(BF), (((1,), (1,)), ((), ())),
        preferred_element_type=F32,
    )


def scan_in_body(
    rate_ref, x_hbm, bc_hbm, codes_hbm, cx_hbm, bx_hbm, cbc_hbm, bbc_hbm, xt_hbm, msg_ref,
    x_ref, bc_ref, codes_ref, cx_ref, bx_ref, cbc_ref, bbc_ref, xt_ref, b_ref, sems,
):
    chunks = [slice(r, r + BT) for r in range(0, TOK, BT)]
    pairs = [
        (codes_hbm, codes_ref), (bc_hbm, bc_ref), (cbc_hbm, cbc_ref), (bbc_hbm, bbc_ref), (cx_hbm, cx_ref),
        (bx_hbm, bx_ref),
    ]
    loads = [pltpu.make_async_copy(src, dst, sems.at[2, k]) for k, (src, dst) in enumerate(pairs)]

    def copy(src, dst, k, i):
        return pltpu.make_async_copy(src.at[chunks[i]], dst.at[chunks[i]], sems.at[k, i])

    for load in loads:
        load.start()
    for i in range(len(chunks)):
        copy(x_hbm, x_ref, 0, i).start()
    for load in loads[:4]:
        load.wait()
    cum = code_sums(codes_ref)
    grow = jnp.exp(head_row(rate_ref, DECAY) * cum)
    for r in range(0, TOK, ROWS):
        part = conv_part(with_rim(bc_ref, r, ROWS, 0, ST), cbc_ref, bbc_ref[:, :ST], 0, ST)
        b_ref[r : r + ROWS, :] = silu(part)
    bt = b_ref[...].T.astype(BF)
    for load in loads[4:]:
        load.wait()
    for i in range(len(chunks)):
        copy(x_hbm, x_ref, 0, i).wait()
        for r in range(i * BT, (i + 1) * BT, ROWS):
            for h in range(HEADS):
                lo, hi = h * HW, (h + 1) * HW
                part = conv_part(with_rim(x_ref, r, ROWS, lo, hi), cx_ref, bx_ref[:, lo:hi], lo, hi)
                xc = silu(part).astype(BF)
                scaled = xc.astype(F32) * spread(grow[r : r + ROWS, :], h)
                if r == 0:
                    scaled = jnp.where(row_ids(ROWS, HW) < EDGE, 0.0, scaled)
                xt_ref[r : r + ROWS, lo:hi] = scaled.astype(BF)
        copy(xt_ref, xt_hbm, 1, i).start()
    state = mm(bt, xt_ref[...])
    row = row_ids(8, WID)
    last = pltpu.roll(x_ref[TOK - 16 : TOK, :].astype(F32)[8:], EDGE, 0)
    head = pltpu.roll(x_ref[0:16, :].astype(F32)[0:8], EDGE, 0)
    bc_last = bc_ref[TOK - 16 : TOK, :].astype(F32)[8:]
    bc_head = bc_ref[0:16, :].astype(F32)[0:8]
    bc_rows = [bc_last[8 - EDGE + k : 9 - EDGE + k, :] for k in range(EDGE)]
    bc_row = jnp.concatenate(bc_rows + [jnp.zeros((1, WID - EDGE * 2 * ST), F32)], axis=1)
    rows = jnp.where(row < EDGE, last, jnp.where(row < 2 * EDGE, head, 0.0))
    rows = jnp.where(row == 2 * EDGE, jnp.broadcast_to(bc_row, (8, WID)), rows)
    row = row_ids(8, HW)
    total = cum[TOK - 1 : TOK, :]
    high = jnp.floor(total * (1.0 / 256.0))
    low = total - 256.0 * high
    heads = jnp.where(row < 5, pltpu.roll(cum[0:8, :], 2, 0), 0.0)
    heads = jnp.where(row == 0, high, jnp.where(row == 1, low, heads))
    heads = pltpu.roll(heads, HW // 2, 1)
    pad = jnp.zeros((HW - 8, HW), F32)
    none = jnp.zeros((8, ST), F32)
    b_last = conv_part(jnp.concatenate([bc_last[:, :ST], none], axis=0), cbc_ref, none[0:1], 0, ST)
    b_head = conv_part(jnp.concatenate([none, bc_head[:, :ST]], axis=0), cbc_ref, bbc_ref[:, :ST], 0, ST)
    b_last = jnp.concatenate([b_last, pad], axis=0).T
    b_head = jnp.concatenate([b_head, pad], axis=0).T
    for j in range(CTX):
        at = slice(8 * j, 8 * j + 8)
        msg_ref[j, :, 0:WID] = jnp.concatenate([state[at, :], rows], axis=0).astype(BF)
        side = jnp.concatenate([b_last[at, :] + heads, b_head[at, :]], axis=0)
        msg_ref[j, :, WID:MSG] = side.astype(BF)
    for i in range(len(chunks)):
        copy(xt_ref, xt_hbm, 1, i).wait()


def prefix_body(rate_ref, cx_ref, bx_ref, r_ref, after_ref, q_ref):
    rate = head_row(rate_ref, DECAY, HW // 2)
    state = jnp.zeros((8, WID), F32)
    before = jnp.zeros((8, WID), F32)
    side_before = jnp.zeros((8, HW), F32)
    edge_row = row_ids(8, WID) < EDGE
    for c in range(CTX):
        main = r_ref[c, :, 0:WID].astype(F32)
        side = r_ref[c, :, WID:MSG].astype(F32)
        rows = jnp.where(edge_row, before, main[8:16, :])
        before = main[8:16, :]
        pre = bx_ref[...] + cx_ref[0:1, :] * rows
        for k in range(1, 4):
            pre = pre + cx_ref[k : k + 1, :] * pltpu.roll(rows, 8 - k, 0)
        edge = silu(pre).astype(BF).astype(F32)
        heads = side[0:8, :]
        grow = jnp.exp(rate * pltpu.roll(heads, 6, 0))
        fade = jnp.exp(-rate * (256.0 * heads[0:1, :] + heads[1:2, :]))
        b_edge = silu(side_before + side[8:16, :]).astype(BF).astype(F32)
        side_before = heads
        parts = []
        for h in range(HEADS):
            lo, hi = h * HW, (h + 1) * HW
            scaled = (edge[:, lo:hi] * spread(grow, HW // 2 + h)).astype(BF).astype(F32)
            part = state[:, lo:hi]
            for k in range(EDGE):
                part = part + spread(b_edge, k) * jnp.broadcast_to(scaled[k : k + 1, :], (8, HW))
            q_ref[c, :, lo:hi] = part.astype(BF)
            parts.append(spread(fade, HW // 2 + h, 8) * (part + main[0:8, lo:hi]))
        state = jnp.concatenate(parts, axis=1)


def local_body(
    rate_ref, skip_ref, xt_ref, z_ref, codes_ref, bc_ref, cbc_ref, bbc_ref, a1_ref, a2_ref, cm_ref, gram, prod, bm,
):
    cum = code_sums(codes_ref)
    for r in range(0, TOK, ROWS):
        for ref, lo in ((bm, 0), (cm_ref, ST)):
            hi = lo + ST
            part = conv_part(with_rim(bc_ref, r, ROWS, lo, hi), cbc_ref, bbc_ref[:, lo:hi], lo, hi)
            ref[r : r + ROWS, :] = silu(part).astype(BF)
    for r in range(0, TOK, BT):
        size = r + BT
        part = lax.dot_general(
            cm_ref[r:size, :], bm[0:size, :], (((1,), (1,)), ((), ())), preferred_element_type=F32
        )
        row = lax.broadcasted_iota(jnp.int32, (BT, size), 0) + r
        col = lax.broadcasted_iota(jnp.int32, (BT, size), 1)
        gram[r:size, 0:size] = jnp.where(row >= col, part, 0.0).astype(BF)
        prod[r:size, :] = mm(gram[r:size, 0:size], xt_ref[0:size, :])
    fades = jnp.exp(head_row(rate_ref, -DECAY) * cum)
    for r in range(0, TOK, ROWS):
        rs = slice(r, r + ROWS)
        for h in range(HEADS):
            lo, hi = h * HW, (h + 1) * HW
            gate = silu(z_ref[rs, lo:hi].astype(F32))
            fade = spread(fades[rs, :], h)
            total = prod[rs, lo:hi] * SCALE + skip_ref[h] * xt_ref[rs, lo:hi].astype(F32)
            fade = fade * gate
            a1_ref[rs, lo:hi] = (total * fade).astype(BF)
            a2_ref[rs, lo:hi] = (SCALE * fade).astype(BF)


def patch_body(
    place_ref, rate_ref, skip_ref, got_ref, x_ref, bc_ref, z_ref, codes_ref, cx_ref, bx_ref, cbc_ref, bbc_ref,
    after_ref, a1_ref, cm_ref, xe, be,
):
    live = place_ref[0] > 0
    rim = got_ref[0, 8:16, 0:WID].astype(F32)
    xe[0:8, :] = jnp.where(live, pltpu.roll(rim, 8 - EDGE, 0), 0.0)
    xe[8:24, :] = x_ref[...].astype(F32)
    for k in range(EDGE):
        part = rim[2 * EDGE : 2 * EDGE + 1, k * 2 * ST : (k + 1) * 2 * ST]
        be[8 - EDGE + k : 9 - EDGE + k, :] = jnp.where(live, part, 0.0)
    be[8:24, :] = bc_ref[...].astype(F32)
    cum = code_sums(codes_ref, HW)[0:16, :]
    grow = jnp.exp(head_row(rate_ref, DECAY) * cum)
    fades = jnp.exp(head_row(rate_ref, -DECAY) * cum)
    bm = silu(conv_part(be[:, :ST], cbc_ref, bbc_ref[:, :ST], 0, ST)).astype(BF)
    cm = silu(conv_part(be[:, ST:], cbc_ref, bbc_ref[:, ST:], ST, 2 * ST)).astype(BF)
    cm_ref[...] = cm
    part = lax.dot_general(cm, bm, (((1,), (1,)), ((), ())), preferred_element_type=F32)
    row = lax.broadcasted_iota(jnp.int32, (16, 16), 0)
    col = lax.broadcasted_iota(jnp.int32, (16, 16), 1)
    edge = jnp.where(row < col, -part, 0.0)
    gram = jnp.where(col < EDGE, edge, jnp.where(row >= col, part, 0.0)).astype(BF)
    for h in range(HEADS):
        lo, hi = h * HW, (h + 1) * HW
        xc = silu(conv_part(xe[:, lo:hi], cx_ref, bx_ref[:, lo:hi], lo, hi)).astype(BF).astype(F32)
        total = mm(gram, (xc * spread(grow, h)).astype(BF))
        gate = silu(z_ref[:, lo:hi].astype(F32))
        a1_ref[:, lo:hi] = ((total * (SCALE * spread(fades, h)) + skip_ref[h] * xc) * gate).astype(BF)


def norm_body(half, q_ref, a1_hbm, a2_hbm, c_hbm, gain_hbm, first_ref, cm_ref, n_ref, a1_ref, a2_ref, c_ref, gain_ref, prod, sems):
    tokens = pl.ds(half * HT, HT)
    pairs = [
        (c_hbm.at[tokens], c_ref), (a1_hbm.at[tokens], a1_ref), (a2_hbm.at[tokens], a2_ref), (gain_hbm, gain_ref),
    ]
    loads = [pltpu.make_async_copy(src, dst, sems.at[k]) for k, (src, dst) in enumerate(pairs)]
    for load in loads:
        load.start()
    state = q_ref[...].astype(F32).reshape(ST, WID).astype(BF)
    loads[0].wait()
    prod[...] = mm(c_ref[...], state)
    if half == 0:
        prod[0:16, :] = mm(cm_ref[...], state)
    for load in loads[1:]:
        load.wait()
    for r in range(0, HT, ROWS):
        for h in range(HEADS):
            rs, hs = slice(r, r + ROWS), slice(h * HW, (h + 1) * HW)
            local = a1_ref[rs, hs]
            if half == 0 and r == 0:
                local = jnp.concatenate([first_ref[:, hs], local[16:, :]], axis=0)
            gated = local.astype(F32) + a2_ref[rs, hs].astype(F32) * prod[rs, hs]
            power = jnp.mean(gated * gated, axis=-1, keepdims=True)
            n_ref[rs, hs] = (gated * lax.rsqrt(power + 1e-05) * gain_ref[:, hs]).astype(BF)


def target_column(place_ref, far, side):
    index = place_ref[0]
    column = ((((index >> 1) + far) & 3) * 2 + (index & 1)) * WID + side * HALF
    return pl.multiple_of(column, HALF)


def fetch_body(place_ref, w_hbm, ws_hbm, after_ref, own_ref, sib_ref, token_ref, sems):
    source = pl.ds(target_column(place_ref, 2, 0), WID)
    loads = [
        pltpu.make_async_copy(w_hbm.at[:, source], own_ref, sems.at[0]),
        pltpu.make_async_copy(ws_hbm.at[:, source], sib_ref, sems.at[1]),
    ]
    token_ref[...] = jnp.zeros((8, HW), F32)
    for load in loads:
        load.start()
    for load in loads:
        load.wait()


def project_far_body(own_ref, sib_ref, w_ref, ws_ref, l_ref, r_ref):
    for i in range(4):
        at = slice(i * QUART, (i + 1) * QUART)
        cols = slice((i & 1) * QUART, (i & 1) * QUART + QUART)
        total = mm(own_ref[...], w_ref[:, at]) + mm(sib_ref[...], ws_ref[:, at])
        (l_ref, r_ref)[i // 2][:, cols] = total.astype(BF)


def project_body(parts, adds, targets, place_ref, *refs):
    owns, sibs = refs[:parts], refs[parts : 2 * parts]
    weights = refs[2 * parts : 2 * parts + 2]
    addends = refs[2 * parts + 2 : 2 * parts + 2 + 2 * adds]
    outs = refs[-4:-2]
    blocks, sems = refs[-2:]

    def load(k, i):
        column = target_column(place_ref, *targets[i // 2]) + (i & 1) * QUART
        source = weights[k].at[:, pl.ds(pl.multiple_of(column, QUART), QUART)]
        return pltpu.make_async_copy(source, blocks.at[k, i], sems.at[k, i])

    for i in range(4):
        for k in range(2):
            load(k, i).start()
    for i in range(4):
        cols = slice((i & 1) * QUART, (i & 1) * QUART + QUART)
        mine = addends[adds * (i // 2) : adds * (i // 2 + 1)]
        for k in range(2):
            load(k, i).wait()
        for p in range(parts):
            rows = slice(p * HT, (p + 1) * HT)
            total = mm(owns[p][...], blocks[0, i]) + mm(sibs[p][...], blocks[1, i])
            if adds == 2:
                total = total + mine[p][:, cols].astype(F32)
            elif adds == 1:
                total = total + mine[0][rows, cols].astype(F32)
            outs[i // 2][rows, cols] = total.astype(outs[i // 2].dtype)


def final_body(m0_ref, m1_ref, a_ref, b_ref, o_ref):
    o_ref[:, :HALF] = (m0_ref[...] + a_ref[...].astype(F32)).astype(BF)
    o_ref[:, HALF:] = (m1_ref[...] + b_ref[...].astype(F32)).astype(BF)


def params(dims=1, room=20):
    return pltpu.CompilerParams(
        dimension_semantics=("arbitrary",) * dims if dims else None, vmem_limit_bytes=room << 20
    )


SMEM = pl.BlockSpec(memory_space=pltpu.SMEM)
VMEM = pl.BlockSpec(memory_space=pltpu.VMEM)
ANY = pl.BlockSpec(memory_space=pl.ANY)


def whole(*shape):
    return pl.BlockSpec(shape, lambda i: (0,) * len(shape))


def in_hbm(a):
    return pltpu.with_memory_space_constraint(a, pltpu.HBM)


QUART = HALF // 2


def project(place, owns, sibs, w, w_sib, targets, addends, kind):
    parts, count = len(owns), len(addends[0])
    return pl.pallas_call(
        functools.partial(project_body, parts, count, targets),
        out_shape=[SD((parts * HT, HALF), kind)] * 2,
        in_specs=[SMEM] + [VMEM] * (2 * parts) + [ANY, ANY] + [VMEM] * (2 * count),
        out_specs=[VMEM, VMEM],
        scratch_shapes=[pltpu.VMEM((2, 4, WID, QUART), BF), pltpu.SemaphoreType.DMA((2, 4))],
        compiler_params=params(0),
        name="project",
    )(place, *owns, *sibs, w, w_sib, *addends[0], *addends[1])


def body(
    x_in, bc_in, z_in, codes, head_rate, conv_x, conv_bc, bias_x, bias_bc, skip, norm_gain, w_out
):
    place = lax.axis_index("tp")
    where = jnp.full((1,), place, jnp.int32)
    x_in, bc_in, z_in, w_out = in_hbm(x_in), in_hbm(bc_in), in_hbm(z_in), in_hbm(w_out)
    codes, conv_x, conv_bc = in_hbm(codes.T), in_hbm(conv_x), in_hbm(conv_bc)
    head_rate, skip = in_hbm(head_rate), in_hbm(skip)
    bias_x, bias_bc, gain = in_hbm(bias_x[None, :]), in_hbm(bias_bc[None, :]), in_hbm(norm_gain[None, :])

    swap = [(s, s ^ 1) for s in range(8)]
    w_sib = in_hbm(lax.ppermute(w_out, "tp", swap))
    taps = (conv_x, bias_x, conv_bc, bias_bc)
    buf = pltpu.VMEM
    xt, msg = pl.pallas_call(
        scan_in_body,
        in_specs=[SMEM] + [ANY] * 7,
        out_specs=[ANY, VMEM],
        out_shape=[pltpu.HBM((TOK, WID), BF), SD((CTX, 16, MSG), BF)],
        scratch_shapes=[
            buf((TOK, WID), BF), buf((TOK, 2 * ST), BF), buf((HEADS, TOK), jnp.int32), buf((4, WID), F32),
            buf((1, WID), F32), buf((4, 2 * ST), F32), buf((1, 2 * ST), F32), buf((TOK, WID), BF), buf((TOK, ST), F32),
            pltpu.SemaphoreType.DMA((3, 8)),
        ],
        compiler_params=params(0),
        name="scan_in",
    )(head_rate, x_in, bc_in, codes, *taps)
    got = lax.all_to_all(msg, "ctx", 0, 0, tiled=True)

    a1, a2, c_map = pl.pallas_call(
        local_body,
        grid=(1,),
        in_specs=[
            SMEM, SMEM, whole(TOK, WID), whole(TOK, WID), whole(HEADS, TOK), whole(TOK, 2 * ST), whole(4, 2 * ST),
            whole(1, 2 * ST),
        ],
        out_specs=[whole(TOK, WID), whole(TOK, WID), whole(TOK, ST)],
        out_shape=[pltpu.HBM((TOK, WID), BF), pltpu.HBM((TOK, WID), BF), pltpu.HBM((TOK, ST), BF)],
        scratch_shapes=[buf((TOK, TOK), BF), buf((TOK, WID), F32), buf((TOK, ST), BF)],
        compiler_params=params(),
        name="local",
    )(head_rate, skip, in_hbm(xt), z_in, codes, bc_in, conv_bc, bias_bc)
    a1, a2, c_map = in_hbm(a1), in_hbm(a2), in_hbm(c_map)

    prefix = pl.pallas_call(
        prefix_body,
        in_specs=[SMEM, VMEM, VMEM, VMEM, ANY],
        out_specs=VMEM,
        out_shape=SD((CTX, 8, WID), BF),
        compiler_params=params(0),
        name="prefix",
    )(head_rate, conv_x, bias_x, got, a1)
    incoming = lax.all_to_all(prefix, "ctx", 0, 0, tiled=True)

    def fixed(*shape):
        return pl.BlockSpec(shape, lambda i, ix: (0,) * len(shape))

    far_own, far_sib, token = pl.pallas_call(
        fetch_body,
        in_specs=[SMEM, ANY, ANY, ANY],
        out_specs=[VMEM] * 3,
        out_shape=[SD((WID, WID), BF)] * 2 + [SD((8, HW), F32)],
        scratch_shapes=[pltpu.SemaphoreType.DMA((2,))],
        compiler_params=params(0, 2),
        name="fetch",
    )(where, w_out, w_sib, prefix)

    def project_far(own, sib):
        return pl.pallas_call(
            project_far_body,
            in_specs=[VMEM] * 4,
            out_specs=[VMEM, VMEM],
            out_shape=[SD((HT, HALF), BF)] * 2,
            compiler_params=params(0, 6),
            name="project_far",
        )(own, sib, far_own, far_sib)

    ctx = jnp.full((1,), lax.axis_index("ctx"), jnp.int32)
    a_first, c_first = pl.pallas_call(
        patch_body,
        out_shape=[SD((16, WID), BF), SD((16, ST), BF)],
        grid_spec=pltpu.PrefetchScalarGridSpec(
            num_scalar_prefetch=1,
            grid=(1,),
            in_specs=[
                SMEM, SMEM, pl.BlockSpec((1, 16, MSG), lambda i, ix: (jnp.maximum(ix[0] - 1, 0), 0, 0)),
                fixed(16, WID), fixed(16, 2 * ST), fixed(16, WID), fixed(HEADS, HW), fixed(4, WID), fixed(1, WID),
                fixed(4, 2 * ST), fixed(1, 2 * ST), ANY,
            ],
            out_specs=[fixed(16, WID), fixed(16, ST)],
            scratch_shapes=[buf((24, WID), F32), buf((24, 2 * ST), F32)],
        ),
        compiler_params=params(1, 6),
        name="patch",
    )(ctx, head_rate, skip, got, x_in, bc_in, z_in, codes, *taps, token)

    def norm(half):
        return pl.pallas_call(
            functools.partial(norm_body, half),
            in_specs=[VMEM] + [ANY] * 4 + [VMEM] * 2,
            out_specs=VMEM,
            out_shape=SD((HT, WID), BF),
            scratch_shapes=[
                buf((HT, WID), BF), buf((HT, WID), BF), buf((HT, ST), BF), buf((1, WID), F32), buf((HT, WID), F32),
                pltpu.SemaphoreType.DMA((4,)),
            ],
            compiler_params=params(0, 6),
            name="norm",
        )(incoming, a1, a2, c_map, gain, a_first, c_first)

    up = [(s, (s + 2) % 8) for s in range(8)]
    down = [(s, (s + 6) % 8) for s in range(8)]
    n0 = norm(0)
    s0 = lax.ppermute(n0, "tp", swap)
    n1 = norm(1)
    s1 = lax.ppermute(n1, "tp", swap)
    fl0, fr0 = project_far(n0, s0)
    fl0, fr0 = lax.ppermute(fl0, "tp", up), lax.ppermute(fr0, "tp", down)
    fl1, fr1 = project_far(n1, s1)
    fl1, fr1 = lax.ppermute(fl1, "tp", up), lax.ppermute(fr1, "tp", down)
    run = functools.partial(project, where, (n0, n1), (s0, s1), w_out, w_sib)
    above_r, below_l = run(((1, 1), (3, 0)), ((), ()), BF)
    from_r, from_l = lax.ppermute(above_r, "tp", up), lax.ppermute(below_l, "tp", down)
    above_l, below_r = run(((1, 0), (3, 1)), ((fl0, fl1), (fr0, fr1)), BF)
    last_l, last_r = lax.ppermute(above_l, "tp", up), lax.ppermute(below_r, "tp", down)
    here_l, here_r = run(((0, 0), (0, 1)), ((from_l,), (from_r,)), F32)
    return pl.pallas_call(
        final_body,
        in_specs=[VMEM] * 4,
        out_specs=VMEM,
        out_shape=SD((TOK, WID), BF),
        compiler_params=params(0),
        name="final",
    )(here_l, here_r, last_l, last_r)


def solution(mesh):
    in_specs = (
        P("ctx", "tp"),
        P("ctx", None),
        P("ctx", "tp"),
        P("ctx", "tp"),
        P("tp"),
        P(None, "tp"),
        P(),
        P("tp"),
        P(),
        P("tp"),
        P("tp"),
        P("tp", None),
    )
    out_specs = P("ctx", "tp")
    return jax.shard_map(body, mesh=mesh, in_specs=in_specs, out_specs=out_specs, check_vma=False)
```

```python
import functools

import jax
import jax.numpy as jnp
from jax import lax
from jax.experimental import pallas as pl
from jax.experimental.pallas import tpu as pltpu
from jax.sharding import PartitionSpec as P

BF = jnp.bfloat16
F32 = jnp.float32
TOK = 512
HT = TOK // 2
BT = 128
EDGE = 3
MSG = 1152
WID = 1024
HALF = WID // 2
HEADS = 8
HW = 128
ST = 128
CTX = 16
SEQ = TOK * CTX
DECAY = 12.288 / SEQ / 63.0
SCALE = 1.0 / (ST * SEQ) ** 0.5
ROWS = 64
SD = jax.ShapeDtypeStruct


def silu(v):
    half = 0.5 * v
    return half + half * jnp.tanh(half)


def mm(a, b):
    return jnp.dot(a, b, preferred_element_type=F32)


def head_row(ref, factor, at=0):
    lane = lax.broadcasted_iota(jnp.int32, (1, HW), 1)
    row = jnp.zeros((1, HW), F32)
    for h in range(HEADS):
        row = jnp.where(lane == at + h, ref[h] * factor, row)
    return row


def spread(compact, lane, rows=None):
    column = compact[:, lane : lane + 1]
    return jnp.broadcast_to(column, (rows or compact.shape[0], HW))


def row_ids(rows, width):
    return lax.broadcasted_iota(jnp.int32, (rows, width), 0)


def conv_part(big, w_ref, bias, lo, hi):
    count = big.shape[0] // 8
    row = row_ids(8, hi - lo)
    total = bias + w_ref[3:4, lo:hi] * big[8:]
    for k in range(1, 4):
        rolled = [pltpu.roll(big[8 * t : 8 * t + 8], k, 0) for t in range(count)]
        moved = [jnp.where(row < k, rolled[t], rolled[t + 1]) for t in range(count - 1)]
        total = total + w_ref[3 - k : 4 - k, lo:hi] * jnp.concatenate(moved, axis=0)
    return total


def with_rim(ref, r, rows, lo, hi):
    body = ref[r : r + rows, lo:hi].astype(F32)
    if r == 0:
        return jnp.concatenate([jnp.zeros((8, hi - lo), F32), body], axis=0)
    return jnp.concatenate([ref[r - 16 : r, lo:hi].astype(F32)[8:], body], axis=0)


def code_sums(codes_ref, count=TOK):
    codes = jnp.concatenate([codes_ref[...].astype(F32), jnp.zeros((HW - HEADS, count), F32)], axis=0)
    row = lax.broadcasted_iota(jnp.int32, (count, count), 0)
    col = lax.broadcasted_iota(jnp.int32, (count, count), 1)
    return lax.dot_general(
        jnp.where(row >= col, 1.0, 0.0).astype(BF), codes.astype(BF), (((1,), (1,)), ((), ())),
        preferred_element_type=F32,
    )


def scan_in_body(
    rate_ref, x_hbm, bc_hbm, codes_hbm, cx_hbm, bx_hbm, cbc_hbm, bbc_hbm, msg_ref, token_ref,
    x_ref, bc_ref, codes_ref, cx_ref, bx_ref, cbc_ref, bbc_ref, xt_ref, b_ref, sems,
):
    chunks = [slice(r, r + BT) for r in range(0, TOK, BT)]
    pairs = [
        (codes_hbm, codes_ref), (bc_hbm, bc_ref), (cbc_hbm, cbc_ref), (bbc_hbm, bbc_ref), (cx_hbm, cx_ref),
        (bx_hbm, bx_ref),
    ]
    loads = [pltpu.make_async_copy(src, dst, sems.at[1, k]) for k, (src, dst) in enumerate(pairs)]

    def fetch(i):
        return pltpu.make_async_copy(x_hbm.at[chunks[i]], x_ref.at[chunks[i]], sems.at[0, i])

    token_ref[...] = jnp.zeros((8, HW), F32)
    for load in loads:
        load.start()
    for i in range(len(chunks)):
        fetch(i).start()
    for load in loads[:4]:
        load.wait()
    cum = code_sums(codes_ref)
    grow = jnp.exp(head_row(rate_ref, DECAY) * cum)
    for r in range(0, TOK, ROWS):
        part = conv_part(with_rim(bc_ref, r, ROWS, 0, ST), cbc_ref, bbc_ref[:, :ST], 0, ST)
        b_ref[r : r + ROWS, :] = silu(part)
    bt = b_ref[...].T.astype(BF)
    for load in loads[4:]:
        load.wait()
    for i in range(len(chunks)):
        fetch(i).wait()
        for r in range(i * BT, (i + 1) * BT, ROWS):
            for h in range(HEADS):
                lo, hi = h * HW, (h + 1) * HW
                part = conv_part(with_rim(x_ref, r, ROWS, lo, hi), cx_ref, bx_ref[:, lo:hi], lo, hi)
                xc = silu(part).astype(BF)
                scaled = xc.astype(F32) * spread(grow[r : r + ROWS, :], h)
                if r == 0:
                    scaled = jnp.where(row_ids(ROWS, HW) < EDGE, 0.0, scaled)
                xt_ref[r : r + ROWS, lo:hi] = scaled.astype(BF)
    state = mm(bt, xt_ref[...])
    row = row_ids(8, WID)
    last = pltpu.roll(x_ref[TOK - 16 : TOK, :].astype(F32)[8:], EDGE, 0)
    head = pltpu.roll(x_ref[0:16, :].astype(F32)[0:8], EDGE, 0)
    bc_last = bc_ref[TOK - 16 : TOK, :].astype(F32)[8:]
    bc_head = bc_ref[0:16, :].astype(F32)[0:8]
    bc_rows = [bc_last[8 - EDGE + k : 9 - EDGE + k, :] for k in range(EDGE)]
    bc_row = jnp.concatenate(bc_rows + [jnp.zeros((1, WID - EDGE * 2 * ST), F32)], axis=1)
    rows = jnp.where(row < EDGE, last, jnp.where(row < 2 * EDGE, head, 0.0))
    rows = jnp.where(row == 2 * EDGE, jnp.broadcast_to(bc_row, (8, WID)), rows)
    row = row_ids(8, HW)
    total = cum[TOK - 1 : TOK, :]
    high = jnp.floor(total * (1.0 / 256.0))
    low = total - 256.0 * high
    heads = jnp.where(row < 5, pltpu.roll(cum[0:8, :], 2, 0), 0.0)
    heads = jnp.where(row == 0, high, jnp.where(row == 1, low, heads))
    heads = pltpu.roll(heads, HW // 2, 1)
    pad = jnp.zeros((HW - 8, HW), F32)
    none = jnp.zeros((8, ST), F32)
    b_last = conv_part(jnp.concatenate([bc_last[:, :ST], none], axis=0), cbc_ref, none[0:1], 0, ST)
    b_head = conv_part(jnp.concatenate([none, bc_head[:, :ST]], axis=0), cbc_ref, bbc_ref[:, :ST], 0, ST)
    b_last = jnp.concatenate([b_last, pad], axis=0).T
    b_head = jnp.concatenate([b_head, pad], axis=0).T
    for j in range(CTX):
        at = slice(8 * j, 8 * j + 8)
        msg_ref[j, :, 0:WID] = jnp.concatenate([state[at, :], rows], axis=0).astype(BF)
        side = jnp.concatenate([b_last[at, :] + heads, b_head[at, :]], axis=0)
        msg_ref[j, :, WID:MSG] = side.astype(BF)


def prefix_body(rate_ref, cx_ref, bx_ref, r_ref, after_ref, q_ref):
    rate = head_row(rate_ref, DECAY, HW // 2)
    state = jnp.zeros((8, WID), F32)
    before = jnp.zeros((8, WID), F32)
    side_before = jnp.zeros((8, HW), F32)
    edge_row = row_ids(8, WID) < EDGE
    for c in range(CTX):
        main = r_ref[c, :, 0:WID].astype(F32)
        side = r_ref[c, :, WID:MSG].astype(F32)
        rows = jnp.where(edge_row, before, main[8:16, :])
        before = main[8:16, :]
        pre = bx_ref[...] + cx_ref[0:1, :] * rows
        for k in range(1, 4):
            pre = pre + cx_ref[k : k + 1, :] * pltpu.roll(rows, 8 - k, 0)
        edge = silu(pre).astype(BF).astype(F32)
        heads = side[0:8, :]
        grow = jnp.exp(rate * pltpu.roll(heads, 6, 0))
        fade = jnp.exp(-rate * (256.0 * heads[0:1, :] + heads[1:2, :]))
        b_edge = silu(side_before + side[8:16, :]).astype(BF).astype(F32)
        side_before = heads
        parts = []
        for h in range(HEADS):
            lo, hi = h * HW, (h + 1) * HW
            scaled = (edge[:, lo:hi] * spread(grow, HW // 2 + h)).astype(BF).astype(F32)
            part = state[:, lo:hi]
            for k in range(EDGE):
                part = part + spread(b_edge, k) * jnp.broadcast_to(scaled[k : k + 1, :], (8, HW))
            q_ref[c, :, lo:hi] = part.astype(BF)
            parts.append(spread(fade, HW // 2 + h, 8) * (part + main[0:8, lo:hi]))
        state = jnp.concatenate(parts, axis=1)


def local_body(
    rate_ref, skip_ref, x_ref, z_ref, codes_ref, bc_ref, cx_ref, bx_ref, cbc_ref, bbc_ref, after_ref, a1_ref, a2_ref,
    cm_ref, gram, prod, bm, xc_ref, xt_ref,
):
    cum = code_sums(codes_ref)
    grow = jnp.exp(head_row(rate_ref, DECAY) * cum)
    for r in range(0, TOK, ROWS):
        for h in range(HEADS):
            lo, hi = h * HW, (h + 1) * HW
            part = conv_part(with_rim(x_ref, r, ROWS, lo, hi), cx_ref, bx_ref[:, lo:hi], lo, hi)
            xc = silu(part).astype(BF)
            xc_ref[r : r + ROWS, lo:hi] = xc
            scaled = xc.astype(F32) * spread(grow[r : r + ROWS, :], h)
            if r == 0:
                scaled = jnp.where(row_ids(ROWS, HW) < EDGE, 0.0, scaled)
            xt_ref[r : r + ROWS, lo:hi] = scaled.astype(BF)
    for r in range(0, TOK, ROWS):
        for ref, lo in ((bm, 0), (cm_ref, ST)):
            hi = lo + ST
            part = conv_part(with_rim(bc_ref, r, ROWS, lo, hi), cbc_ref, bbc_ref[:, lo:hi], lo, hi)
            ref[r : r + ROWS, :] = silu(part).astype(BF)
    for r in range(0, TOK, BT):
        size = r + BT
        part = lax.dot_general(
            cm_ref[r:size, :], bm[0:size, :], (((1,), (1,)), ((), ())), preferred_element_type=F32
        )
        row = lax.broadcasted_iota(jnp.int32, (BT, size), 0) + r
        col = lax.broadcasted_iota(jnp.int32, (BT, size), 1)
        gram[r:size, 0:size] = jnp.where(row >= col, part, 0.0).astype(BF)
        prod[r:size, :] = mm(gram[r:size, 0:size], xt_ref[0:size, :])
    fades = jnp.exp(head_row(rate_ref, -DECAY) * cum)
    for r in range(0, TOK, ROWS):
        rs = slice(r, r + ROWS)
        for h in range(HEADS):
            lo, hi = h * HW, (h + 1) * HW
            gate = silu(z_ref[rs, lo:hi].astype(F32))
            fade = spread(fades[rs, :], h)
            fade = SCALE * fade
            total = prod[rs, lo:hi] * fade + skip_ref[h] * xc_ref[rs, lo:hi].astype(F32)
            a1_ref[rs, lo:hi] = (total * gate).astype(BF)
            a2_ref[rs, lo:hi] = (fade * gate).astype(BF)


def patch_body(
    place_ref, rate_ref, skip_ref, got_ref, x_ref, bc_ref, z_ref, codes_ref, cx_ref, bx_ref, cbc_ref, bbc_ref,
    after_ref, a1_ref, cm_ref, xe, be,
):
    live = place_ref[0] > 0
    rim = got_ref[0, 8:16, 0:WID].astype(F32)
    xe[0:8, :] = jnp.where(live, pltpu.roll(rim, 8 - EDGE, 0), 0.0)
    xe[8:24, :] = x_ref[...].astype(F32)
    for k in range(EDGE):
        part = rim[2 * EDGE : 2 * EDGE + 1, k * 2 * ST : (k + 1) * 2 * ST]
        be[8 - EDGE + k : 9 - EDGE + k, :] = jnp.where(live, part, 0.0)
    be[8:24, :] = bc_ref[...].astype(F32)
    cum = code_sums(codes_ref, HW)[0:16, :]
    grow = jnp.exp(head_row(rate_ref, DECAY) * cum)
    fades = jnp.exp(head_row(rate_ref, -DECAY) * cum)
    bm = silu(conv_part(be[:, :ST], cbc_ref, bbc_ref[:, :ST], 0, ST)).astype(BF)
    cm = silu(conv_part(be[:, ST:], cbc_ref, bbc_ref[:, ST:], ST, 2 * ST)).astype(BF)
    cm_ref[...] = cm
    part = lax.dot_general(cm, bm, (((1,), (1,)), ((), ())), preferred_element_type=F32)
    row = lax.broadcasted_iota(jnp.int32, (16, 16), 0)
    col = lax.broadcasted_iota(jnp.int32, (16, 16), 1)
    edge = jnp.where(row < col, -part, 0.0)
    gram = jnp.where(col < EDGE, edge, jnp.where(row >= col, part, 0.0)).astype(BF)
    for h in range(HEADS):
        lo, hi = h * HW, (h + 1) * HW
        xc = silu(conv_part(xe[:, lo:hi], cx_ref, bx_ref[:, lo:hi], lo, hi)).astype(BF).astype(F32)
        total = mm(gram, (xc * spread(grow, h)).astype(BF))
        gate = silu(z_ref[:, lo:hi].astype(F32))
        a1_ref[:, lo:hi] = ((total * (SCALE * spread(fades, h)) + skip_ref[h] * xc) * gate).astype(BF)


def norm_body(half, place_ref, q_ref, a1_hbm, a2_hbm, c_hbm, gain_hbm, first_ref, cm_ref, ws_hbm, n_ref, *refs):
    a1_ref, a2_ref, c_ref, gain_ref, prod, sems = refs[-6:]
    if half == 0:
        source = pl.ds(target_column(place_ref, 2, 0), WID)
        weights = pltpu.make_async_copy(ws_hbm.at[:, source], refs[0], sems.at[4])
    tokens = pl.ds(half * HT, HT)
    pairs = [
        (c_hbm.at[tokens], c_ref), (a1_hbm.at[tokens], a1_ref), (a2_hbm.at[tokens], a2_ref), (gain_hbm, gain_ref),
    ]
    loads = [pltpu.make_async_copy(src, dst, sems.at[k]) for k, (src, dst) in enumerate(pairs)]
    for load in loads:
        load.start()
    if half == 0:
        weights.start()
    state = q_ref[...].astype(F32).reshape(ST, WID).astype(BF)
    loads[0].wait()
    prod[...] = mm(c_ref[...], state)
    if half == 0:
        prod[0:16, :] = mm(cm_ref[...], state)
    for load in loads[1:]:
        load.wait()
    for r in range(0, HT, ROWS):
        for h in range(HEADS):
            rs, hs = slice(r, r + ROWS), slice(h * HW, (h + 1) * HW)
            local = a1_ref[rs, hs]
            if half == 0 and r == 0:
                local = jnp.concatenate([first_ref[:, hs], local[16:, :]], axis=0)
            gated = local.astype(F32) + a2_ref[rs, hs].astype(F32) * prod[rs, hs]
            power = jnp.mean(gated * gated, axis=-1, keepdims=True)
            n_ref[rs, hs] = (gated * lax.rsqrt(power + 1e-05) * gain_ref[:, hs]).astype(BF)
    if half == 0:
        weights.wait()


def target_column(place_ref, far, side):
    index = place_ref[0]
    column = ((((index >> 1) + far) & 3) * 2 + (index & 1)) * WID + side * HALF
    return pl.multiple_of(column, HALF)


def fetch_body(place_ref, w_hbm, after_ref, own_ref, token_ref, sem):
    load = pltpu.make_async_copy(w_hbm.at[:, pl.ds(target_column(place_ref, 2, 0), WID)], own_ref, sem.at[0])
    load.start()
    token_ref[...] = jnp.zeros((8, HW), F32)
    load.wait()


def project_far_body(own_ref, sib_ref, w_ref, ws_ref, l_ref, r_ref):
    for i in range(4):
        at = slice(i * QUART, (i + 1) * QUART)
        cols = slice((i & 1) * QUART, (i & 1) * QUART + QUART)
        total = mm(own_ref[...], w_ref[:, at]) + mm(sib_ref[...], ws_ref[:, at])
        (l_ref, r_ref)[i // 2][:, cols] = total.astype(BF)


def project_body(parts, adds, targets, place_ref, *refs):
    owns, sibs = refs[:parts], refs[parts : 2 * parts]
    weights = refs[2 * parts : 2 * parts + 2]
    addends = refs[2 * parts + 2 : 2 * parts + 2 + 2 * adds]
    outs = refs[-4:-2]
    blocks, sems = refs[-2:]

    def load(k, i):
        column = target_column(place_ref, *targets[i // 2]) + (i & 1) * QUART
        source = weights[k].at[:, pl.ds(pl.multiple_of(column, QUART), QUART)]
        return pltpu.make_async_copy(source, blocks.at[k, i], sems.at[k, i])

    for i in range(4):
        for k in range(2):
            load(k, i).start()
    for i in range(4):
        cols = slice((i & 1) * QUART, (i & 1) * QUART + QUART)
        mine = addends[adds * (i // 2) : adds * (i // 2 + 1)]
        for k in range(2):
            load(k, i).wait()
        for p in range(parts):
            rows = slice(p * HT, (p + 1) * HT)
            total = mm(owns[p][...], blocks[0, i]) + mm(sibs[p][...], blocks[1, i])
            if adds == 2:
                total = total + mine[p][:, cols].astype(F32)
            elif adds == 1:
                total = total + mine[0][rows, cols].astype(F32)
            outs[i // 2][rows, cols] = total.astype(outs[i // 2].dtype)


def final_body(m0_ref, m1_ref, a_ref, b_ref, o_ref):
    o_ref[:, :HALF] = (m0_ref[...] + a_ref[...].astype(F32)).astype(BF)
    o_ref[:, HALF:] = (m1_ref[...] + b_ref[...].astype(F32)).astype(BF)


def params(dims=1, room=20):
    return pltpu.CompilerParams(
        dimension_semantics=("arbitrary",) * dims if dims else None, vmem_limit_bytes=room << 20
    )


SMEM = pl.BlockSpec(memory_space=pltpu.SMEM)
VMEM = pl.BlockSpec(memory_space=pltpu.VMEM)
ANY = pl.BlockSpec(memory_space=pl.ANY)


def whole(*shape):
    return pl.BlockSpec(shape, lambda i: (0,) * len(shape))


def in_hbm(a):
    return pltpu.with_memory_space_constraint(a, pltpu.HBM)


QUART = HALF // 2


def project(place, owns, sibs, w, w_sib, targets, addends, kind):
    parts, count = len(owns), len(addends[0])
    return pl.pallas_call(
        functools.partial(project_body, parts, count, targets),
        out_shape=[SD((parts * HT, HALF), kind)] * 2,
        in_specs=[SMEM] + [VMEM] * (2 * parts) + [ANY, ANY] + [VMEM] * (2 * count),
        out_specs=[VMEM, VMEM],
        scratch_shapes=[pltpu.VMEM((2, 4, WID, QUART), BF), pltpu.SemaphoreType.DMA((2, 4))],
        compiler_params=params(0),
        name="project",
    )(place, *owns, *sibs, w, w_sib, *addends[0], *addends[1])


def body(
    x_in, bc_in, z_in, codes, head_rate, conv_x, conv_bc, bias_x, bias_bc, skip, norm_gain, w_out
):
    place = lax.axis_index("tp")
    where = jnp.full((1,), place, jnp.int32)
    x_in, bc_in, z_in, w_out = in_hbm(x_in), in_hbm(bc_in), in_hbm(z_in), in_hbm(w_out)
    codes, conv_x, conv_bc = in_hbm(codes.T), in_hbm(conv_x), in_hbm(conv_bc)
    head_rate, skip = in_hbm(head_rate), in_hbm(skip)
    bias_x, bias_bc, gain = in_hbm(bias_x[None, :]), in_hbm(bias_bc[None, :]), in_hbm(norm_gain[None, :])

    swap = [(s, s ^ 1) for s in range(8)]
    w_sib = in_hbm(lax.ppermute(w_out, "tp", swap))
    taps = (conv_x, bias_x, conv_bc, bias_bc)
    buf = pltpu.VMEM
    msg, begun = pl.pallas_call(
        scan_in_body,
        in_specs=[SMEM] + [ANY] * 7,
        out_specs=[VMEM, VMEM],
        out_shape=[SD((CTX, 16, MSG), BF), SD((8, HW), F32)],
        scratch_shapes=[
            buf((TOK, WID), BF), buf((TOK, 2 * ST), BF), buf((HEADS, TOK), jnp.int32), buf((4, WID), F32),
            buf((1, WID), F32), buf((4, 2 * ST), F32), buf((1, 2 * ST), F32), buf((TOK, WID), BF), buf((TOK, ST), F32),
            pltpu.SemaphoreType.DMA((2, 8)),
        ],
        compiler_params=params(0),
        name="scan_in",
    )(head_rate, x_in, bc_in, codes, *taps)
    got = lax.all_to_all(msg, "ctx", 0, 0, tiled=True)

    a1, a2, c_map = pl.pallas_call(
        local_body,
        grid=(1,),
        in_specs=[
            SMEM, SMEM, whole(TOK, WID), whole(TOK, WID), whole(HEADS, TOK), whole(TOK, 2 * ST), whole(4, WID),
            whole(1, WID), whole(4, 2 * ST), whole(1, 2 * ST), ANY,
        ],
        out_specs=[whole(TOK, WID), whole(TOK, WID), whole(TOK, ST)],
        out_shape=[pltpu.HBM((TOK, WID), BF), pltpu.HBM((TOK, WID), BF), pltpu.HBM((TOK, ST), BF)],
        scratch_shapes=[
            buf((TOK, TOK), BF), buf((TOK, WID), F32), buf((TOK, ST), BF), buf((TOK, WID), BF), buf((TOK, WID), BF),
        ],
        compiler_params=params(),
        name="local",
    )(head_rate, skip, x_in, z_in, codes, bc_in, *taps, begun)
    a1, a2, c_map = in_hbm(a1), in_hbm(a2), in_hbm(c_map)

    prefix = pl.pallas_call(
        prefix_body,
        in_specs=[SMEM, VMEM, VMEM, VMEM, ANY],
        out_specs=VMEM,
        out_shape=SD((CTX, 8, WID), BF),
        compiler_params=params(0),
        name="prefix",
    )(head_rate, conv_x, bias_x, got, a1)
    incoming = lax.all_to_all(prefix, "ctx", 0, 0, tiled=True)

    def fixed(*shape):
        return pl.BlockSpec(shape, lambda i, ix: (0,) * len(shape))

    far_own, token = pl.pallas_call(
        fetch_body,
        in_specs=[SMEM, ANY, ANY],
        out_specs=[VMEM, VMEM],
        out_shape=[SD((WID, WID), BF), SD((8, HW), F32)],
        scratch_shapes=[pltpu.SemaphoreType.DMA((1,))],
        compiler_params=params(0, 2),
        name="fetch",
    )(where, w_out, prefix)

    def project_far(own, sib):
        return pl.pallas_call(
            project_far_body,
            in_specs=[VMEM] * 4,
            out_specs=[VMEM, VMEM],
            out_shape=[SD((HT, HALF), BF)] * 2,
            compiler_params=params(0, 6),
            name="project_far",
        )(own, sib, far_own, far_sib)

    ctx = jnp.full((1,), lax.axis_index("ctx"), jnp.int32)
    a_first, c_first = pl.pallas_call(
        patch_body,
        out_shape=[SD((16, WID), BF), SD((16, ST), BF)],
        grid_spec=pltpu.PrefetchScalarGridSpec(
            num_scalar_prefetch=1,
            grid=(1,),
            in_specs=[
                SMEM, SMEM, pl.BlockSpec((1, 16, MSG), lambda i, ix: (jnp.maximum(ix[0] - 1, 0), 0, 0)),
                fixed(16, WID), fixed(16, 2 * ST), fixed(16, WID), fixed(HEADS, HW), fixed(4, WID), fixed(1, WID),
                fixed(4, 2 * ST), fixed(1, 2 * ST), ANY,
            ],
            out_specs=[fixed(16, WID), fixed(16, ST)],
            scratch_shapes=[buf((24, WID), F32), buf((24, 2 * ST), F32)],
        ),
        compiler_params=params(1, 6),
        name="patch",
    )(ctx, head_rate, skip, got, x_in, bc_in, z_in, codes, *taps, token)

    def norm(half):
        outs = [SD((HT, WID), BF)] + ([] if half else [SD((WID, WID), BF)])
        return pl.pallas_call(
            functools.partial(norm_body, half),
            in_specs=[SMEM, VMEM] + [ANY] * 4 + [VMEM] * 2 + [ANY],
            out_specs=[VMEM] * len(outs),
            out_shape=outs,
            scratch_shapes=[
                buf((HT, WID), BF), buf((HT, WID), BF), buf((HT, ST), BF), buf((1, WID), F32), buf((HT, WID), F32),
                pltpu.SemaphoreType.DMA((5,)),
            ],
            compiler_params=params(0, 6),
            name="norm",
        )(where, incoming, a1, a2, c_map, gain, a_first, c_first, w_sib)

    up = [(s, (s + 2) % 8) for s in range(8)]
    down = [(s, (s + 6) % 8) for s in range(8)]
    n0, far_sib = norm(0)
    s0 = lax.ppermute(n0, "tp", swap)
    (n1,) = norm(1)
    s1 = lax.ppermute(n1, "tp", swap)
    fl0, fr0 = project_far(n0, s0)
    fl0, fr0 = lax.ppermute(fl0, "tp", up), lax.ppermute(fr0, "tp", down)
    fl1, fr1 = project_far(n1, s1)
    fl1, fr1 = lax.ppermute(fl1, "tp", up), lax.ppermute(fr1, "tp", down)
    run = functools.partial(project, where, (n0, n1), (s0, s1), w_out, w_sib)
    above_r, below_l = run(((1, 1), (3, 0)), ((), ()), BF)
    from_r, from_l = lax.ppermute(above_r, "tp", up), lax.ppermute(below_l, "tp", down)
    above_l, below_r = run(((1, 0), (3, 1)), ((fl0, fl1), (fr0, fr1)), BF)
    last_l, last_r = lax.ppermute(above_l, "tp", up), lax.ppermute(below_r, "tp", down)
    here_l, here_r = run(((0, 0), (0, 1)), ((from_l,), (from_r,)), F32)
    return pl.pallas_call(
        final_body,
        in_specs=[VMEM] * 4,
        out_specs=VMEM,
        out_shape=SD((TOK, WID), BF),
        compiler_params=params(0),
        name="final",
    )(here_l, here_r, last_l, last_r)


def solution(mesh):
    in_specs = (
        P("ctx", "tp"),
        P("ctx", None),
        P("ctx", "tp"),
        P("ctx", "tp"),
        P("tp"),
        P(None, "tp"),
        P(),
        P("tp"),
        P(),
        P("tp"),
        P("tp"),
        P("tp", None),
    )
    out_specs = P("ctx", "tp")
    return jax.shard_map(body, mesh=mesh, in_specs=in_specs, out_specs=out_specs, check_vma=False)
```

```python
import functools

import jax
import jax.numpy as jnp
from jax import lax
from jax.experimental import pallas as pl
from jax.experimental.pallas import tpu as pltpu
from jax.sharding import PartitionSpec as P

BF = jnp.bfloat16
F32 = jnp.float32
TOK = 512
HT = TOK // 2
BT = 128
EDGE = 3
WID = 1024
HALF = WID // 2
HEADS = 8
HW = 128
ST = 128
CTX = 16
SEQ = TOK * CTX
DECAY = 12.288 / SEQ / 63.0
SCALE = 1.0 / (ST * SEQ) ** 0.5
ROWS = 64
SD = jax.ShapeDtypeStruct


def silu(v):
    half = 0.5 * v
    return half + half * jnp.tanh(half)


def mm(a, b):
    return jnp.dot(a, b, preferred_element_type=F32)


def head_row(ref, factor, at=0):
    lane = lax.broadcasted_iota(jnp.int32, (1, HW), 1)
    row = jnp.zeros((1, HW), F32)
    for h in range(HEADS):
        row = jnp.where(lane == at + h, ref[h] * factor, row)
    return row


def spread(compact, lane, rows=None):
    column = compact[:, lane : lane + 1]
    return jnp.broadcast_to(column, (rows or compact.shape[0], HW))


def row_ids(rows, width):
    return lax.broadcasted_iota(jnp.int32, (rows, width), 0)


def conv_part(big, w_ref, bias, lo, hi):
    count = big.shape[0] // 8
    row = row_ids(8, hi - lo)
    total = bias + w_ref[3:4, lo:hi] * big[8:]
    for k in range(1, 4):
        rolled = [pltpu.roll(big[8 * t : 8 * t + 8], k, 0) for t in range(count)]
        moved = [jnp.where(row < k, rolled[t], rolled[t + 1]) for t in range(count - 1)]
        total = total + w_ref[3 - k : 4 - k, lo:hi] * jnp.concatenate(moved, axis=0)
    return total


def with_rim(ref, r, rows, lo, hi):
    body = ref[r : r + rows, lo:hi].astype(F32)
    if r == 0:
        return jnp.concatenate([jnp.zeros((8, hi - lo), F32), body], axis=0)
    return jnp.concatenate([ref[r - 16 : r, lo:hi].astype(F32)[8:], body], axis=0)


def code_sums(codes_ref, count=TOK):
    codes = jnp.concatenate([codes_ref[...].astype(F32), jnp.zeros((HW - HEADS, count), F32)], axis=0)
    row = lax.broadcasted_iota(jnp.int32, (count, count), 0)
    col = lax.broadcasted_iota(jnp.int32, (count, count), 1)
    return lax.dot_general(
        jnp.where(row >= col, 1.0, 0.0).astype(BF), codes.astype(BF), (((1,), (1,)), ((), ())),
        preferred_element_type=F32,
    )


def scan_in_body(
    rate_ref, x_hbm, bc_hbm, codes_hbm, cx_hbm, bx_hbm, cbc_hbm, bbc_hbm, msg_ref, token_ref,
    x_ref, bc_ref, codes_ref, cx_ref, bx_ref, cbc_ref, bbc_ref, xt_ref, b_ref, sems,
):
    chunks = [slice(r, r + BT) for r in range(0, TOK, BT)]
    pairs = [
        (codes_hbm, codes_ref), (bc_hbm, bc_ref), (cbc_hbm, cbc_ref), (bbc_hbm, bbc_ref), (cx_hbm, cx_ref),
        (bx_hbm, bx_ref),
    ]
    loads = [pltpu.make_async_copy(src, dst, sems.at[1, k]) for k, (src, dst) in enumerate(pairs)]

    def fetch(i):
        return pltpu.make_async_copy(x_hbm.at[chunks[i]], x_ref.at[chunks[i]], sems.at[0, i])

    token_ref[...] = jnp.zeros((8, HW), F32)
    for load in loads:
        load.start()
    for i in range(len(chunks)):
        fetch(i).start()
    for load in loads[:4]:
        load.wait()
    cum = code_sums(codes_ref)
    grow = jnp.exp(head_row(rate_ref, DECAY) * cum)
    for r in range(0, TOK, ROWS):
        part = conv_part(with_rim(bc_ref, r, ROWS, 0, ST), cbc_ref, bbc_ref[:, :ST], 0, ST)
        b_ref[r : r + ROWS, :] = silu(part)
    bt = b_ref[...].T.astype(BF)
    for load in loads[4:]:
        load.wait()
    for i in range(len(chunks)):
        fetch(i).wait()
        for r in range(i * BT, (i + 1) * BT, ROWS):
            for h in range(HEADS):
                lo, hi = h * HW, (h + 1) * HW
                part = conv_part(with_rim(x_ref, r, ROWS, lo, hi), cx_ref, bx_ref[:, lo:hi], lo, hi)
                xc = silu(part).astype(BF)
                scaled = xc.astype(F32) * spread(grow[r : r + ROWS, :], h)
                if r == 0:
                    scaled = jnp.where(row_ids(ROWS, HW) < EDGE, 0.0, scaled)
                xt_ref[r : r + ROWS, lo:hi] = scaled.astype(BF)
    state = mm(bt, xt_ref[...])
    row = row_ids(8, WID)
    last = pltpu.roll(x_ref[TOK - 16 : TOK, :].astype(F32)[8:], EDGE, 0)
    head = pltpu.roll(x_ref[0:16, :].astype(F32)[0:8], EDGE, 0)
    bc_last = bc_ref[TOK - 16 : TOK, :].astype(F32)[8:]
    bc_head = bc_ref[0:16, :].astype(F32)[0:8]
    bc_rows = [bc_last[8 - EDGE + k : 9 - EDGE + k, :] for k in range(EDGE)]
    bc_row = jnp.concatenate(bc_rows + [jnp.zeros((1, WID - EDGE * 2 * ST), F32)], axis=1)
    rows = jnp.where(row < EDGE, last, jnp.where(row < 2 * EDGE, head, 0.0))
    rows = jnp.where(row == 2 * EDGE, jnp.broadcast_to(bc_row, (8, WID)), rows)
    total = cum[TOK - 1 : TOK, :]
    high = jnp.floor(total * (1.0 / 256.0))
    spare = jnp.zeros((1, HW), F32)
    heads = [high, total - 256.0 * high] + [cum[k : k + 1, :] for k in range(EDGE)] + [spare]
    heads = jnp.broadcast_to(jnp.concatenate([spare, spare] + heads, axis=1), (8, WID))
    rows = jnp.where(row == 7, heads, rows)
    none = jnp.zeros((8, ST), F32)
    b_last = conv_part(jnp.concatenate([bc_last[:, :ST], none], axis=0), cbc_ref, none[0:1], 0, ST)
    b_head = conv_part(jnp.concatenate([none, bc_head[:, :ST]], axis=0), cbc_ref, bbc_ref[:, :ST], 0, ST)
    row = row_ids(8, HW)
    group = lax.broadcasted_iota(jnp.int32, (8, HW), 1) // 8

    def stepped(b):
        return jnp.where(row == 1, pltpu.roll(b, 8, 1), jnp.where(row == 2, pltpu.roll(b, 16, 1), b))

    def slot(b, j):
        mine = pltpu.roll(b, (HW - 8 * j) % HW, 1) if j else b
        mine = jnp.where((row == group) & (row < EDGE), mine, 0.0)
        return jnp.sum(mine, axis=0, keepdims=True)

    b_last, b_head = stepped(b_last), stepped(b_head)
    for j in range(CTX):
        pair = jnp.broadcast_to(jnp.concatenate([slot(b_last, j), slot(b_head, j)], axis=1), (8, 2 * HW))
        front = jnp.where(row_ids(8, 2 * HW) == 7, pair, rows[:, : 2 * HW])
        tail = jnp.concatenate([front, rows[:, 2 * HW :]], axis=1)
        msg_ref[j] = jnp.concatenate([state[8 * j : 8 * j + 8, :], tail], axis=0).astype(BF)


def prefix_body(rate_ref, cx_ref, bx_ref, r_ref, after_ref, q_ref):
    rate = head_row(rate_ref, DECAY)
    state = jnp.zeros((8, WID), F32)
    before = jnp.zeros((8, WID), F32)
    edge_row = row_ids(8, WID) < EDGE
    row = row_ids(8, HW)
    b_rows, b_before = [], jnp.zeros((1, HW), F32)
    for c in range(CTX):
        spare = r_ref[c, 8:16, 0 : 2 * HW].astype(F32)[7:8, :]
        b_rows.append(b_before + spare[:, HW:])
        b_before = spare[:, :HW]
    b_rows = silu(jnp.concatenate(b_rows, axis=0)).astype(BF).astype(F32)
    b_edge = jnp.concatenate([b_rows, jnp.zeros((HW - CTX, HW), F32)], axis=0).T
    for c in range(CTX):
        main = r_ref[c].astype(F32)
        tail = main[8:16, :]
        rows = jnp.where(edge_row, before, tail)
        before = tail
        pre = bx_ref[...] + cx_ref[0:1, :] * rows
        for k in range(1, 4):
            pre = pre + cx_ref[k : k + 1, :] * pltpu.roll(rows, 8 - k, 0)
        edge = silu(pre).astype(BF).astype(F32)
        heads = [tail[7:8, k * HW : (k + 1) * HW] for k in range(2, 4 + EDGE)]
        grow = jnp.where(row == 0, heads[2], jnp.where(row == 1, heads[3], heads[4]))
        grow = jnp.exp(rate * grow)
        fade = jnp.exp(-rate * (256.0 * heads[0] + heads[1]))
        parts = []
        for h in range(HEADS):
            lo, hi = h * HW, (h + 1) * HW
            scaled = (edge[:, lo:hi] * spread(grow, h)).astype(BF).astype(F32)
            part = state[:, lo:hi]
            for k in range(EDGE):
                b_column = spread(b_edge[8 * k : 8 * k + 8, :], c)
                part = part + b_column * jnp.broadcast_to(scaled[k : k + 1, :], (8, HW))
            q_ref[c, :, lo:hi] = part.astype(BF)
            parts.append(spread(fade, h, 8) * (part + main[0:8, lo:hi]))
        state = jnp.concatenate(parts, axis=1)


def local_body(
    rate_ref, skip_ref, x_ref, z_ref, codes_ref, bc_ref, cx_ref, bx_ref, cbc_ref, bbc_ref, after_ref, a1_ref, a2_ref,
    cm_ref, gram, prod, bm, xc_ref, xt_ref,
):
    cum = code_sums(codes_ref)
    grow = jnp.exp(head_row(rate_ref, DECAY) * cum)
    for r in range(0, TOK, ROWS):
        for h in range(HEADS):
            lo, hi = h * HW, (h + 1) * HW
            part = conv_part(with_rim(x_ref, r, ROWS, lo, hi), cx_ref, bx_ref[:, lo:hi], lo, hi)
            xc = silu(part).astype(BF)
            xc_ref[r : r + ROWS, lo:hi] = xc
            scaled = xc.astype(F32) * spread(grow[r : r + ROWS, :], h)
            if r == 0:
                scaled = jnp.where(row_ids(ROWS, HW) < EDGE, 0.0, scaled)
            xt_ref[r : r + ROWS, lo:hi] = scaled.astype(BF)
    for r in range(0, TOK, ROWS):
        for ref, lo in ((bm, 0), (cm_ref, ST)):
            hi = lo + ST
            part = conv_part(with_rim(bc_ref, r, ROWS, lo, hi), cbc_ref, bbc_ref[:, lo:hi], lo, hi)
            ref[r : r + ROWS, :] = silu(part).astype(BF)
    for r in range(0, TOK, BT):
        size = r + BT
        part = lax.dot_general(
            cm_ref[r:size, :], bm[0:size, :], (((1,), (1,)), ((), ())), preferred_element_type=F32
        )
        row = lax.broadcasted_iota(jnp.int32, (BT, size), 0) + r
        col = lax.broadcasted_iota(jnp.int32, (BT, size), 1)
        gram[r:size, 0:size] = jnp.where(row >= col, part, 0.0).astype(BF)
        prod[r:size, :] = mm(gram[r:size, 0:size], xt_ref[0:size, :])
    fades = jnp.exp(head_row(rate_ref, -DECAY) * cum)
    for r in range(0, TOK, ROWS):
        rs = slice(r, r + ROWS)
        for h in range(HEADS):
            lo, hi = h * HW, (h + 1) * HW
            gate = silu(z_ref[rs, lo:hi].astype(F32))
            fade = spread(fades[rs, :], h)
            fade = SCALE * fade
            total = prod[rs, lo:hi] * fade + skip_ref[h] * xc_ref[rs, lo:hi].astype(F32)
            a1_ref[rs, lo:hi] = (total * gate).astype(BF)
            a2_ref[rs, lo:hi] = (fade * gate).astype(BF)


def patch_body(
    place_ref, rate_ref, skip_ref, got_ref, x_ref, bc_ref, z_ref, codes_ref, cx_ref, bx_ref, cbc_ref, bbc_ref,
    after_ref, a1_ref, cm_ref, xe, be,
):
    live = place_ref[0] > 0
    rim = got_ref[0, 8:16, 0:WID].astype(F32)
    xe[0:8, :] = jnp.where(live, pltpu.roll(rim, 8 - EDGE, 0), 0.0)
    xe[8:24, :] = x_ref[...].astype(F32)
    for k in range(EDGE):
        part = rim[2 * EDGE : 2 * EDGE + 1, k * 2 * ST : (k + 1) * 2 * ST]
        be[8 - EDGE + k : 9 - EDGE + k, :] = jnp.where(live, part, 0.0)
    be[8:24, :] = bc_ref[...].astype(F32)
    cum = code_sums(codes_ref, HW)[0:16, :]
    grow = jnp.exp(head_row(rate_ref, DECAY) * cum)
    fades = jnp.exp(head_row(rate_ref, -DECAY) * cum)
    bm = silu(conv_part(be[:, :ST], cbc_ref, bbc_ref[:, :ST], 0, ST)).astype(BF)
    cm = silu(conv_part(be[:, ST:], cbc_ref, bbc_ref[:, ST:], ST, 2 * ST)).astype(BF)
    cm_ref[...] = cm
    part = lax.dot_general(cm, bm, (((1,), (1,)), ((), ())), preferred_element_type=F32)
    row = lax.broadcasted_iota(jnp.int32, (16, 16), 0)
    col = lax.broadcasted_iota(jnp.int32, (16, 16), 1)
    edge = jnp.where(row < col, -part, 0.0)
    gram = jnp.where(col < EDGE, edge, jnp.where(row >= col, part, 0.0)).astype(BF)
    for h in range(HEADS):
        lo, hi = h * HW, (h + 1) * HW
        xc = silu(conv_part(xe[:, lo:hi], cx_ref, bx_ref[:, lo:hi], lo, hi)).astype(BF).astype(F32)
        total = mm(gram, (xc * spread(grow, h)).astype(BF))
        gate = silu(z_ref[:, lo:hi].astype(F32))
        a1_ref[:, lo:hi] = ((total * (SCALE * spread(fades, h)) + skip_ref[h] * xc) * gate).astype(BF)


def norm_body(half, place_ref, q_ref, a1_hbm, a2_hbm, c_hbm, gain_hbm, first_ref, cm_ref, ws_hbm, n_ref, *refs):
    a1_ref, a2_ref, c_ref, gain_ref, prod, sems = refs[-6:]
    if half == 0:
        source = pl.ds(target_column(place_ref, 2, 0), WID)
        weights = pltpu.make_async_copy(ws_hbm.at[:, source], refs[0], sems.at[4])
    tokens = pl.ds(half * HT, HT)
    pairs = [
        (c_hbm.at[tokens], c_ref), (a1_hbm.at[tokens], a1_ref), (a2_hbm.at[tokens], a2_ref), (gain_hbm, gain_ref),
    ]
    loads = [pltpu.make_async_copy(src, dst, sems.at[k]) for k, (src, dst) in enumerate(pairs)]
    for load in loads:
        load.start()
    if half == 0:
        weights.start()
    state = q_ref[...].astype(F32).reshape(ST, WID).astype(BF)
    loads[0].wait()
    prod[...] = mm(c_ref[...], state)
    if half == 0:
        prod[0:16, :] = mm(cm_ref[...], state)
    for load in loads[1:]:
        load.wait()
    for r in range(0, HT, ROWS):
        for h in range(HEADS):
            rs, hs = slice(r, r + ROWS), slice(h * HW, (h + 1) * HW)
            local = a1_ref[rs, hs]
            if half == 0 and r == 0:
                local = jnp.concatenate([first_ref[:, hs], local[16:, :]], axis=0)
            gated = local.astype(F32) + a2_ref[rs, hs].astype(F32) * prod[rs, hs]
            power = jnp.mean(gated * gated, axis=-1, keepdims=True)
            n_ref[rs, hs] = (gated * lax.rsqrt(power + 1e-05) * gain_ref[:, hs]).astype(BF)
    if half == 0:
        weights.wait()


def target_column(place_ref, far, side):
    index = place_ref[0]
    column = ((((index >> 1) + far) & 3) * 2 + (index & 1)) * WID + side * HALF
    return pl.multiple_of(column, HALF)


def fetch_body(place_ref, w_hbm, after_ref, own_ref, token_ref, sem):
    load = pltpu.make_async_copy(w_hbm.at[:, pl.ds(target_column(place_ref, 2, 0), WID)], own_ref, sem.at[0])
    load.start()
    token_ref[...] = jnp.zeros((8, HW), F32)
    load.wait()


def project_far_body(own_ref, sib_ref, w_ref, ws_ref, l_ref, r_ref):
    for i in range(4):
        at = slice(i * QUART, (i + 1) * QUART)
        cols = slice((i & 1) * QUART, (i & 1) * QUART + QUART)
        total = mm(own_ref[...], w_ref[:, at]) + mm(sib_ref[...], ws_ref[:, at])
        (l_ref, r_ref)[i // 2][:, cols] = total.astype(BF)


def project_body(parts, adds, targets, place_ref, *refs):
    owns, sibs = refs[:parts], refs[parts : 2 * parts]
    weights = refs[2 * parts : 2 * parts + 2]
    addends = refs[2 * parts + 2 : 2 * parts + 2 + 2 * adds]
    outs = refs[-4:-2]
    blocks, sems = refs[-2:]

    def load(k, i):
        column = target_column(place_ref, *targets[i // 2]) + (i & 1) * QUART
        source = weights[k].at[:, pl.ds(pl.multiple_of(column, QUART), QUART)]
        return pltpu.make_async_copy(source, blocks.at[k, i], sems.at[k, i])

    for i in range(4):
        for k in range(2):
            load(k, i).start()
    for i in range(4):
        cols = slice((i & 1) * QUART, (i & 1) * QUART + QUART)
        mine = addends[adds * (i // 2) : adds * (i // 2 + 1)]
        for k in range(2):
            load(k, i).wait()
        for p in range(parts):
            rows = slice(p * HT, (p + 1) * HT)
            total = mm(owns[p][...], blocks[0, i]) + mm(sibs[p][...], blocks[1, i])
            if adds == 2:
                total = total + mine[p][:, cols].astype(F32)
            elif adds == 1:
                total = total + mine[0][rows, cols].astype(F32)
            outs[i // 2][rows, cols] = total.astype(outs[i // 2].dtype)


def final_body(side, m_ref, a_ref, *refs):
    o_hbm, half_ref, sem = refs[-3:]
    half_ref[...] = (m_ref[...] + a_ref[...].astype(F32)).astype(BF)
    store = pltpu.make_async_copy(half_ref, o_hbm.at[:, side * HALF : (side + 1) * HALF], sem.at[0])
    store.start()
    store.wait()


def params(dims=1, room=20):
    return pltpu.CompilerParams(
        dimension_semantics=("arbitrary",) * dims if dims else None, vmem_limit_bytes=room << 20
    )


SMEM = pl.BlockSpec(memory_space=pltpu.SMEM)
VMEM = pl.BlockSpec(memory_space=pltpu.VMEM)
ANY = pl.BlockSpec(memory_space=pl.ANY)


def whole(*shape):
    return pl.BlockSpec(shape, lambda i: (0,) * len(shape))


def in_hbm(a):
    return pltpu.with_memory_space_constraint(a, pltpu.HBM)


QUART = HALF // 2


def project(place, owns, sibs, w, w_sib, targets, addends, kind):
    parts, count = len(owns), len(addends[0])
    return pl.pallas_call(
        functools.partial(project_body, parts, count, targets),
        out_shape=[SD((parts * HT, HALF), kind)] * 2,
        in_specs=[SMEM] + [VMEM] * (2 * parts) + [ANY, ANY] + [VMEM] * (2 * count),
        out_specs=[VMEM, VMEM],
        scratch_shapes=[pltpu.VMEM((2, 4, WID, QUART), BF), pltpu.SemaphoreType.DMA((2, 4))],
        compiler_params=params(0),
        name="project",
    )(place, *owns, *sibs, w, w_sib, *addends[0], *addends[1])


def body(
    x_in, bc_in, z_in, codes, head_rate, conv_x, conv_bc, bias_x, bias_bc, skip, norm_gain, w_out
):
    place = lax.axis_index("tp")
    where = jnp.full((1,), place, jnp.int32)
    x_in, bc_in, z_in, w_out = in_hbm(x_in), in_hbm(bc_in), in_hbm(z_in), in_hbm(w_out)
    codes, conv_x, conv_bc = in_hbm(codes.T), in_hbm(conv_x), in_hbm(conv_bc)
    head_rate, skip = in_hbm(head_rate), in_hbm(skip)
    bias_x, bias_bc, gain = in_hbm(bias_x[None, :]), in_hbm(bias_bc[None, :]), in_hbm(norm_gain[None, :])

    swap = [(s, s ^ 1) for s in range(8)]
    w_sib = in_hbm(lax.ppermute(w_out, "tp", swap))
    taps = (conv_x, bias_x, conv_bc, bias_bc)
    buf = pltpu.VMEM
    msg, begun = pl.pallas_call(
        scan_in_body,
        in_specs=[SMEM] + [ANY] * 7,
        out_specs=[VMEM, VMEM],
        out_shape=[SD((CTX, 16, WID), BF), SD((8, HW), F32)],
        scratch_shapes=[
            buf((TOK, WID), BF), buf((TOK, 2 * ST), BF), buf((HEADS, TOK), jnp.int32), buf((4, WID), F32),
            buf((1, WID), F32), buf((4, 2 * ST), F32), buf((1, 2 * ST), F32), buf((TOK, WID), BF), buf((TOK, ST), F32),
            pltpu.SemaphoreType.DMA((2, 8)),
        ],
        compiler_params=params(0),
        name="scan_in",
    )(head_rate, x_in, bc_in, codes, *taps)
    got = lax.all_to_all(msg, "ctx", 0, 0, tiled=True)

    a1, a2, c_map = pl.pallas_call(
        local_body,
        grid=(1,),
        in_specs=[
            SMEM, SMEM, whole(TOK, WID), whole(TOK, WID), whole(HEADS, TOK), whole(TOK, 2 * ST), whole(4, WID),
            whole(1, WID), whole(4, 2 * ST), whole(1, 2 * ST), ANY,
        ],
        out_specs=[whole(TOK, WID), whole(TOK, WID), whole(TOK, ST)],
        out_shape=[pltpu.HBM((TOK, WID), BF), pltpu.HBM((TOK, WID), BF), pltpu.HBM((TOK, ST), BF)],
        scratch_shapes=[
            buf((TOK, TOK), BF), buf((TOK, WID), F32), buf((TOK, ST), BF), buf((TOK, WID), BF), buf((TOK, WID), BF),
        ],
        compiler_params=params(),
        name="local",
    )(head_rate, skip, x_in, z_in, codes, bc_in, *taps, begun)
    a1, a2, c_map = in_hbm(a1), in_hbm(a2), in_hbm(c_map)

    prefix = pl.pallas_call(
        prefix_body,
        in_specs=[SMEM, VMEM, VMEM, VMEM, ANY],
        out_specs=VMEM,
        out_shape=SD((CTX, 8, WID), BF),
        compiler_params=params(0),
        name="prefix",
    )(head_rate, conv_x, bias_x, got, a1)
    incoming = lax.all_to_all(prefix, "ctx", 0, 0, tiled=True)

    def fixed(*shape):
        return pl.BlockSpec(shape, lambda i, ix: (0,) * len(shape))

    far_own, token = pl.pallas_call(
        fetch_body,
        in_specs=[SMEM, ANY, ANY],
        out_specs=[VMEM, VMEM],
        out_shape=[SD((WID, WID), BF), SD((8, HW), F32)],
        scratch_shapes=[pltpu.SemaphoreType.DMA((1,))],
        compiler_params=params(0, 2),
        name="fetch",
    )(where, w_out, prefix)

    def project_far(own, sib):
        return pl.pallas_call(
            project_far_body,
            in_specs=[VMEM] * 4,
            out_specs=[VMEM, VMEM],
            out_shape=[SD((HT, HALF), BF)] * 2,
            compiler_params=params(0, 6),
            name="project_far",
        )(own, sib, far_own, far_sib)

    ctx = jnp.full((1,), lax.axis_index("ctx"), jnp.int32)
    a_first, c_first = pl.pallas_call(
        patch_body,
        out_shape=[SD((16, WID), BF), SD((16, ST), BF)],
        grid_spec=pltpu.PrefetchScalarGridSpec(
            num_scalar_prefetch=1,
            grid=(1,),
            in_specs=[
                SMEM, SMEM, pl.BlockSpec((1, 16, WID), lambda i, ix: (jnp.maximum(ix[0] - 1, 0), 0, 0)),
                fixed(16, WID), fixed(16, 2 * ST), fixed(16, WID), fixed(HEADS, HW), fixed(4, WID), fixed(1, WID),
                fixed(4, 2 * ST), fixed(1, 2 * ST), ANY,
            ],
            out_specs=[fixed(16, WID), fixed(16, ST)],
            scratch_shapes=[buf((24, WID), F32), buf((24, 2 * ST), F32)],
        ),
        compiler_params=params(1, 6),
        name="patch",
    )(ctx, head_rate, skip, got, x_in, bc_in, z_in, codes, *taps, token)

    def norm(half):
        outs = [SD((HT, WID), BF)] + ([] if half else [SD((WID, WID), BF)])
        return pl.pallas_call(
            functools.partial(norm_body, half),
            in_specs=[SMEM, VMEM] + [ANY] * 4 + [VMEM] * 2 + [ANY],
            out_specs=[VMEM] * len(outs),
            out_shape=outs,
            scratch_shapes=[
                buf((HT, WID), BF), buf((HT, WID), BF), buf((HT, ST), BF), buf((1, WID), F32), buf((HT, WID), F32),
                pltpu.SemaphoreType.DMA((5,)),
            ],
            compiler_params=params(0, 6),
            name="norm",
        )(where, incoming, a1, a2, c_map, gain, a_first, c_first, w_sib)

    up = [(s, (s + 2) % 8) for s in range(8)]
    down = [(s, (s + 6) % 8) for s in range(8)]
    n0, far_sib = norm(0)
    s0 = lax.ppermute(n0, "tp", swap)
    (n1,) = norm(1)
    s1 = lax.ppermute(n1, "tp", swap)
    fl0, fr0 = project_far(n0, s0)
    fl0, fr0 = lax.ppermute(fl0, "tp", up), lax.ppermute(fr0, "tp", down)
    fl1, fr1 = project_far(n1, s1)
    fl1, fr1 = lax.ppermute(fl1, "tp", up), lax.ppermute(fr1, "tp", down)
    run = functools.partial(project, where, (n0, n1), (s0, s1), w_out, w_sib)
    above_r, below_l = run(((1, 1), (3, 0)), ((), ()), BF)
    from_r, from_l = lax.ppermute(above_r, "tp", up), lax.ppermute(below_l, "tp", down)
    above_l, below_r = run(((1, 0), (3, 1)), ((fl0, fl1), (fr0, fr1)), BF)
    last_l, last_r = lax.ppermute(above_l, "tp", up), lax.ppermute(below_r, "tp", down)
    here_l, here_r = run(((0, 0), (0, 1)), ((from_l,), (from_r,)), F32)

    def final(side, here, last, *carry):
        return pl.pallas_call(
            functools.partial(final_body, side),
            in_specs=[VMEM, VMEM] + [ANY] * len(carry),
            out_specs=ANY,
            out_shape=SD((TOK, WID), BF),
            scratch_shapes=[buf((TOK, HALF), BF), pltpu.SemaphoreType.DMA((1,))],
            input_output_aliases={2: 0} if carry else {},
            compiler_params=params(0, 4),
            name="final",
        )(here, last, *carry)

    return final(1, here_r, last_r, final(0, here_l, last_l))


def solution(mesh):
    in_specs = (
        P("ctx", "tp"),
        P("ctx", None),
        P("ctx", "tp"),
        P("ctx", "tp"),
        P("tp"),
        P(None, "tp"),
        P(),
        P("tp"),
        P(),
        P("tp"),
        P("tp"),
        P("tp", None),
    )
    out_specs = P("ctx", "tp")
    return jax.shard_map(body, mesh=mesh, in_specs=in_specs, out_specs=out_specs, check_vma=False)
```

```python
import functools

import jax
import jax.numpy as jnp
from jax import lax
from jax.experimental import pallas as pl
from jax.experimental.pallas import tpu as pltpu
from jax.sharding import PartitionSpec as P

BF = jnp.bfloat16
F32 = jnp.float32
TOK = 512
HT = TOK // 2
BT = 128
EDGE = 3
WID = 1024
HALF = WID // 2
HEADS = 8
HW = 128
ST = 128
CTX = 16
SEQ = TOK * CTX
DECAY = 12.288 / SEQ / 63.0
SCALE = 1.0 / (ST * SEQ) ** 0.5
ROWS = 32
SD = jax.ShapeDtypeStruct


def silu(v):
    half = 0.5 * v
    return half + half * jnp.tanh(half)


def mm(a, b):
    return jnp.dot(a, b, preferred_element_type=F32)


def head_row(ref, factor, at=0):
    lane = lax.broadcasted_iota(jnp.int32, (1, HW), 1)
    row = jnp.zeros((1, HW), F32)
    for h in range(HEADS):
        row = jnp.where(lane == at + h, ref[h] * factor, row)
    return row


def spread(compact, lane, rows=None):
    column = compact[:, lane : lane + 1]
    return jnp.broadcast_to(column, (rows or compact.shape[0], HW))


def row_ids(rows, width):
    return lax.broadcasted_iota(jnp.int32, (rows, width), 0)


def conv_part(big, w_ref, bias, lo, hi):
    count = big.shape[0] // 8
    row = row_ids(8, hi - lo)
    total = bias + w_ref[3:4, lo:hi] * big[8:]
    for k in range(1, 4):
        rolled = [pltpu.roll(big[8 * t : 8 * t + 8], k, 0) for t in range(count)]
        moved = [jnp.where(row < k, rolled[t], rolled[t + 1]) for t in range(count - 1)]
        total = total + w_ref[3 - k : 4 - k, lo:hi] * jnp.concatenate(moved, axis=0)
    return total


def with_rim(ref, r, rows, lo, hi):
    body = ref[r : r + rows, lo:hi].astype(F32)
    if r == 0:
        return jnp.concatenate([jnp.zeros((8, hi - lo), F32), body], axis=0)
    return jnp.concatenate([ref[r - 16 : r, lo:hi].astype(F32)[8:], body], axis=0)


def code_sums(codes_ref, count=TOK):
    codes = jnp.concatenate([codes_ref[...].astype(F32), jnp.zeros((HW - HEADS, count), F32)], axis=0)
    row = lax.broadcasted_iota(jnp.int32, (count, count), 0)
    col = lax.broadcasted_iota(jnp.int32, (count, count), 1)
    return lax.dot_general(
        jnp.where(row >= col, 1.0, 0.0).astype(BF), codes.astype(BF), (((1,), (1,)), ((), ())),
        preferred_element_type=F32,
    )


def scan_in_body(
    rate_ref, x_hbm, bc_hbm, codes_hbm, cx_hbm, bx_hbm, cbc_hbm, bbc_hbm, msg_ref, token_ref,
    x_ref, bc_ref, codes_ref, cx_ref, bx_ref, cbc_ref, bbc_ref, xt_ref, b_ref, sems,
):
    chunks = [slice(r, r + BT) for r in range(0, TOK, BT)]
    pairs = [
        (codes_hbm, codes_ref), (bc_hbm, bc_ref), (cbc_hbm, cbc_ref), (bbc_hbm, bbc_ref), (cx_hbm, cx_ref),
        (bx_hbm, bx_ref),
    ]
    loads = [pltpu.make_async_copy(src, dst, sems.at[1, k]) for k, (src, dst) in enumerate(pairs)]

    def fetch(i):
        return pltpu.make_async_copy(x_hbm.at[chunks[i]], x_ref.at[chunks[i]], sems.at[0, i])

    token_ref[...] = jnp.zeros((8, HW), F32)
    for load in loads:
        load.start()
    for i in range(len(chunks)):
        fetch(i).start()
    for load in loads[:4]:
        load.wait()
    cum = code_sums(codes_ref)
    grow = jnp.exp(head_row(rate_ref, DECAY) * cum)
    for r in range(0, TOK, ROWS):
        part = conv_part(with_rim(bc_ref, r, ROWS, 0, ST), cbc_ref, bbc_ref[:, :ST], 0, ST)
        b_ref[r : r + ROWS, :] = silu(part)
    bt = b_ref[...].T.astype(BF)
    for load in loads[4:]:
        load.wait()
    for i in range(len(chunks)):
        fetch(i).wait()
        for r in range(i * BT, (i + 1) * BT, ROWS):
            for h in range(HEADS):
                lo, hi = h * HW, (h + 1) * HW
                part = conv_part(with_rim(x_ref, r, ROWS, lo, hi), cx_ref, bx_ref[:, lo:hi], lo, hi)
                xc = silu(part).astype(BF)
                scaled = xc.astype(F32) * spread(grow[r : r + ROWS, :], h)
                if r == 0:
                    scaled = jnp.where(row_ids(ROWS, HW) < EDGE, 0.0, scaled)
                xt_ref[r : r + ROWS, lo:hi] = scaled.astype(BF)
    state = mm(bt, xt_ref[...])
    row = row_ids(8, WID)
    last = pltpu.roll(x_ref[TOK - 16 : TOK, :].astype(F32)[8:], EDGE, 0)
    head = pltpu.roll(x_ref[0:16, :].astype(F32)[0:8], EDGE, 0)
    bc_last = bc_ref[TOK - 16 : TOK, :].astype(F32)[8:]
    bc_head = bc_ref[0:16, :].astype(F32)[0:8]
    bc_rows = [bc_last[8 - EDGE + k : 9 - EDGE + k, :] for k in range(EDGE)]
    bc_row = jnp.concatenate(bc_rows + [jnp.zeros((1, WID - EDGE * 2 * ST), F32)], axis=1)
    rows = jnp.where(row < EDGE, last, jnp.where(row < 2 * EDGE, head, 0.0))
    rows = jnp.where(row == 2 * EDGE, jnp.broadcast_to(bc_row, (8, WID)), rows)
    total = cum[TOK - 1 : TOK, :]
    high = jnp.floor(total * (1.0 / 256.0))
    spare = jnp.zeros((1, HW), F32)
    heads = [high, total - 256.0 * high] + [cum[k : k + 1, :] for k in range(EDGE)] + [spare]
    heads = jnp.broadcast_to(jnp.concatenate([spare, spare] + heads, axis=1), (8, WID))
    rows = jnp.where(row == 7, heads, rows)
    none = jnp.zeros((8, ST), F32)
    b_last = conv_part(jnp.concatenate([bc_last[:, :ST], none], axis=0), cbc_ref, none[0:1], 0, ST)
    b_head = conv_part(jnp.concatenate([none, bc_head[:, :ST]], axis=0), cbc_ref, bbc_ref[:, :ST], 0, ST)
    row = row_ids(8, HW)
    group = lax.broadcasted_iota(jnp.int32, (8, HW), 1) // 8

    def stepped(b):
        return jnp.where(row == 1, pltpu.roll(b, 8, 1), jnp.where(row == 2, pltpu.roll(b, 16, 1), b))

    def slot(b, j):
        mine = pltpu.roll(b, (HW - 8 * j) % HW, 1) if j else b
        mine = jnp.where((row == group) & (row < EDGE), mine, 0.0)
        return jnp.sum(mine, axis=0, keepdims=True)

    b_last, b_head = stepped(b_last), stepped(b_head)
    for j in range(CTX):
        pair = jnp.broadcast_to(jnp.concatenate([slot(b_last, j), slot(b_head, j)], axis=1), (8, 2 * HW))
        front = jnp.where(row_ids(8, 2 * HW) == 7, pair, rows[:, : 2 * HW])
        tail = jnp.concatenate([front, rows[:, 2 * HW :]], axis=1)
        msg_ref[j] = jnp.concatenate([state[8 * j : 8 * j + 8, :], tail], axis=0).astype(BF)


def prefix_body(rate_ref, cx_ref, bx_ref, r_ref, after_ref, q_ref):
    rate = head_row(rate_ref, DECAY)
    state = jnp.zeros((8, WID), F32)
    before = jnp.zeros((8, WID), F32)
    edge_row = row_ids(8, WID) < EDGE
    row = row_ids(8, HW)
    b_rows, b_before = [], jnp.zeros((1, HW), F32)
    for c in range(CTX):
        spare = r_ref[c, 8:16, 0 : 2 * HW].astype(F32)[7:8, :]
        b_rows.append(b_before + spare[:, HW:])
        b_before = spare[:, :HW]
    b_rows = silu(jnp.concatenate(b_rows, axis=0)).astype(BF).astype(F32)
    b_edge = jnp.concatenate([b_rows, jnp.zeros((HW - CTX, HW), F32)], axis=0).T
    for c in range(CTX):
        main = r_ref[c].astype(F32)
        tail = main[8:16, :]
        rows = jnp.where(edge_row, before, tail)
        before = tail
        pre = bx_ref[...] + cx_ref[0:1, :] * rows
        for k in range(1, 4):
            pre = pre + cx_ref[k : k + 1, :] * pltpu.roll(rows, 8 - k, 0)
        edge = silu(pre).astype(BF).astype(F32)
        heads = [tail[7:8, k * HW : (k + 1) * HW] for k in range(2, 4 + EDGE)]
        grow = jnp.where(row == 0, heads[2], jnp.where(row == 1, heads[3], heads[4]))
        grow = jnp.exp(rate * grow)
        fade = jnp.exp(-rate * (256.0 * heads[0] + heads[1]))
        parts = []
        for h in range(HEADS):
            lo, hi = h * HW, (h + 1) * HW
            scaled = (edge[:, lo:hi] * spread(grow, h)).astype(BF).astype(F32)
            part = state[:, lo:hi]
            for k in range(EDGE):
                b_column = spread(b_edge[8 * k : 8 * k + 8, :], c)
                part = part + b_column * jnp.broadcast_to(scaled[k : k + 1, :], (8, HW))
            q_ref[c, :, lo:hi] = part.astype(BF)
            parts.append(spread(fade, h, 8) * (part + main[0:8, lo:hi]))
        state = jnp.concatenate(parts, axis=1)


def local_body(
    rate_ref, skip_ref, x_ref, z_ref, codes_ref, bc_ref, cx_ref, bx_ref, cbc_ref, bbc_ref, after_ref, a1_ref, a2_ref,
    cm_ref, gram, prod, bm, xc_ref, xt_ref,
):
    cum = code_sums(codes_ref)
    grow = jnp.exp(head_row(rate_ref, DECAY) * cum)
    for r in range(0, TOK, ROWS):
        for h in range(HEADS):
            lo, hi = h * HW, (h + 1) * HW
            part = conv_part(with_rim(x_ref, r, ROWS, lo, hi), cx_ref, bx_ref[:, lo:hi], lo, hi)
            xc = silu(part).astype(BF)
            xc_ref[r : r + ROWS, lo:hi] = xc
            scaled = xc.astype(F32) * spread(grow[r : r + ROWS, :], h)
            if r == 0:
                scaled = jnp.where(row_ids(ROWS, HW) < EDGE, 0.0, scaled)
            xt_ref[r : r + ROWS, lo:hi] = scaled.astype(BF)
    for r in range(0, TOK, ROWS):
        for ref, lo in ((bm, 0), (cm_ref, ST)):
            hi = lo + ST
            part = conv_part(with_rim(bc_ref, r, ROWS, lo, hi), cbc_ref, bbc_ref[:, lo:hi], lo, hi)
            ref[r : r + ROWS, :] = silu(part).astype(BF)
    for r in range(0, TOK, BT):
        size = r + BT
        part = lax.dot_general(
            cm_ref[r:size, :], bm[0:size, :], (((1,), (1,)), ((), ())), preferred_element_type=F32
        )
        row = lax.broadcasted_iota(jnp.int32, (BT, size), 0) + r
        col = lax.broadcasted_iota(jnp.int32, (BT, size), 1)
        gram[r:size, 0:size] = jnp.where(row >= col, part, 0.0).astype(BF)
        prod[r:size, :] = mm(gram[r:size, 0:size], xt_ref[0:size, :])
    fades = jnp.exp(head_row(rate_ref, -DECAY) * cum)
    for r in range(0, TOK, ROWS):
        rs = slice(r, r + ROWS)
        for h in range(HEADS):
            lo, hi = h * HW, (h + 1) * HW
            gate = silu(z_ref[rs, lo:hi].astype(F32))
            fade = spread(fades[rs, :], h)
            fade = SCALE * fade
            total = prod[rs, lo:hi] * fade + skip_ref[h] * xc_ref[rs, lo:hi].astype(F32)
            a1_ref[rs, lo:hi] = (total * gate).astype(BF)
            a2_ref[rs, lo:hi] = (fade * gate).astype(BF)


def patch_body(
    place_ref, rate_ref, skip_ref, got_ref, x_ref, bc_ref, z_ref, codes_ref, cx_ref, bx_ref, cbc_ref, bbc_ref,
    after_ref, a1_ref, cm_ref, xe, be,
):
    live = place_ref[0] > 0
    rim = got_ref[0, 8:16, 0:WID].astype(F32)
    xe[0:8, :] = jnp.where(live, pltpu.roll(rim, 8 - EDGE, 0), 0.0)
    xe[8:24, :] = x_ref[...].astype(F32)
    for k in range(EDGE):
        part = rim[2 * EDGE : 2 * EDGE + 1, k * 2 * ST : (k + 1) * 2 * ST]
        be[8 - EDGE + k : 9 - EDGE + k, :] = jnp.where(live, part, 0.0)
    be[8:24, :] = bc_ref[...].astype(F32)
    cum = code_sums(codes_ref, HW)[0:16, :]
    grow = jnp.exp(head_row(rate_ref, DECAY) * cum)
    fades = jnp.exp(head_row(rate_ref, -DECAY) * cum)
    bm = silu(conv_part(be[:, :ST], cbc_ref, bbc_ref[:, :ST], 0, ST)).astype(BF)
    cm = silu(conv_part(be[:, ST:], cbc_ref, bbc_ref[:, ST:], ST, 2 * ST)).astype(BF)
    cm_ref[...] = cm
    part = lax.dot_general(cm, bm, (((1,), (1,)), ((), ())), preferred_element_type=F32)
    row = lax.broadcasted_iota(jnp.int32, (16, 16), 0)
    col = lax.broadcasted_iota(jnp.int32, (16, 16), 1)
    edge = jnp.where(row < col, -part, 0.0)
    gram = jnp.where(col < EDGE, edge, jnp.where(row >= col, part, 0.0)).astype(BF)
    for h in range(HEADS):
        lo, hi = h * HW, (h + 1) * HW
        xc = silu(conv_part(xe[:, lo:hi], cx_ref, bx_ref[:, lo:hi], lo, hi)).astype(BF).astype(F32)
        total = mm(gram, (xc * spread(grow, h)).astype(BF))
        gate = silu(z_ref[:, lo:hi].astype(F32))
        a1_ref[:, lo:hi] = ((total * (SCALE * spread(fades, h)) + skip_ref[h] * xc) * gate).astype(BF)


def norm_body(half, place_ref, q_ref, a1_hbm, a2_hbm, c_hbm, gain_hbm, first_ref, cm_ref, ws_hbm, n_ref, *refs):
    a1_ref, a2_ref, c_ref, gain_ref, prod, sems = refs[-6:]
    if half == 0:
        source = pl.ds(target_column(place_ref, 2, 0), WID)
        weights = pltpu.make_async_copy(ws_hbm.at[:, source], refs[0], sems.at[4])
    tokens = pl.ds(half * HT, HT)
    pairs = [
        (c_hbm.at[tokens], c_ref), (a1_hbm.at[tokens], a1_ref), (a2_hbm.at[tokens], a2_ref), (gain_hbm, gain_ref),
    ]
    loads = [pltpu.make_async_copy(src, dst, sems.at[k]) for k, (src, dst) in enumerate(pairs)]
    for load in loads:
        load.start()
    if half == 0:
        weights.start()
    state = q_ref[...].astype(F32).reshape(ST, WID).astype(BF)
    loads[0].wait()
    prod[...] = mm(c_ref[...], state)
    if half == 0:
        prod[0:16, :] = mm(cm_ref[...], state)
    for load in loads[1:]:
        load.wait()
    for r in range(0, HT, ROWS):
        for h in range(HEADS):
            rs, hs = slice(r, r + ROWS), slice(h * HW, (h + 1) * HW)
            local = a1_ref[rs, hs]
            if half == 0 and r == 0:
                local = jnp.concatenate([first_ref[:, hs], local[16:, :]], axis=0)
            gated = local.astype(F32) + a2_ref[rs, hs].astype(F32) * prod[rs, hs]
            power = jnp.mean(gated * gated, axis=-1, keepdims=True)
            n_ref[rs, hs] = (gated * lax.rsqrt(power + 1e-05) * gain_ref[:, hs]).astype(BF)
    if half == 0:
        weights.wait()


def target_column(place_ref, far, side):
    index = place_ref[0]
    column = ((((index >> 1) + far) & 3) * 2 + (index & 1)) * WID + side * HALF
    return pl.multiple_of(column, HALF)


def fetch_body(place_ref, w_hbm, after_ref, own_ref, token_ref, sem):
    load = pltpu.make_async_copy(w_hbm.at[:, pl.ds(target_column(place_ref, 2, 0), WID)], own_ref, sem.at[0])
    load.start()
    token_ref[...] = jnp.zeros((8, HW), F32)
    load.wait()


def project_far_body(own_ref, sib_ref, w_ref, ws_ref, l_ref, r_ref):
    for i in range(4):
        at = slice(i * QUART, (i + 1) * QUART)
        cols = slice((i & 1) * QUART, (i & 1) * QUART + QUART)
        total = mm(own_ref[...], w_ref[:, at]) + mm(sib_ref[...], ws_ref[:, at])
        (l_ref, r_ref)[i // 2][:, cols] = total.astype(BF)


def project_body(parts, adds, targets, place_ref, *refs):
    owns, sibs = refs[:parts], refs[parts : 2 * parts]
    weights = refs[2 * parts : 2 * parts + 2]
    addends = refs[2 * parts + 2 : 2 * parts + 2 + 2 * adds]
    outs = refs[-4:-2]
    blocks, sems = refs[-2:]

    def load(k, i):
        column = target_column(place_ref, *targets[i // 2]) + (i & 1) * QUART
        source = weights[k].at[:, pl.ds(pl.multiple_of(column, QUART), QUART)]
        return pltpu.make_async_copy(source, blocks.at[k, i], sems.at[k, i])

    for i in range(4):
        for k in range(2):
            load(k, i).start()
    for i in range(4):
        cols = slice((i & 1) * QUART, (i & 1) * QUART + QUART)
        mine = addends[adds * (i // 2) : adds * (i // 2 + 1)]
        for k in range(2):
            load(k, i).wait()
        for p in range(parts):
            rows = slice(p * HT, (p + 1) * HT)
            total = mm(owns[p][...], blocks[0, i]) + mm(sibs[p][...], blocks[1, i])
            if adds == 2:
                total = total + mine[p][:, cols].astype(F32)
            elif adds == 1:
                total = total + mine[0][rows, cols].astype(F32)
            outs[i // 2][rows, cols] = total.astype(outs[i // 2].dtype)


def final_body(side, m_ref, a_ref, *refs):
    o_hbm, half_ref, sem = refs[-3:]
    half_ref[...] = (m_ref[...] + a_ref[...].astype(F32)).astype(BF)
    store = pltpu.make_async_copy(half_ref, o_hbm.at[:, side * HALF : (side + 1) * HALF], sem.at[0])
    store.start()
    store.wait()


def params(dims=1, room=20):
    return pltpu.CompilerParams(
        dimension_semantics=("arbitrary",) * dims if dims else None, vmem_limit_bytes=room << 20
    )


SMEM = pl.BlockSpec(memory_space=pltpu.SMEM)
VMEM = pl.BlockSpec(memory_space=pltpu.VMEM)
ANY = pl.BlockSpec(memory_space=pl.ANY)


def whole(*shape):
    return pl.BlockSpec(shape, lambda i: (0,) * len(shape))


def in_hbm(a):
    return pltpu.with_memory_space_constraint(a, pltpu.HBM)


QUART = HALF // 2


def project(place, owns, sibs, w, w_sib, targets, addends, kind):
    parts, count = len(owns), len(addends[0])
    return pl.pallas_call(
        functools.partial(project_body, parts, count, targets),
        out_shape=[SD((parts * HT, HALF), kind)] * 2,
        in_specs=[SMEM] + [VMEM] * (2 * parts) + [ANY, ANY] + [VMEM] * (2 * count),
        out_specs=[VMEM, VMEM],
        scratch_shapes=[pltpu.VMEM((2, 4, WID, QUART), BF), pltpu.SemaphoreType.DMA((2, 4))],
        compiler_params=params(0),
        name="project",
    )(place, *owns, *sibs, w, w_sib, *addends[0], *addends[1])


def body(
    x_in, bc_in, z_in, codes, head_rate, conv_x, conv_bc, bias_x, bias_bc, skip, norm_gain, w_out
):
    place = lax.axis_index("tp")
    where = jnp.full((1,), place, jnp.int32)
    x_in, bc_in, z_in, w_out = in_hbm(x_in), in_hbm(bc_in), in_hbm(z_in), in_hbm(w_out)
    codes, conv_x, conv_bc = in_hbm(codes.T), in_hbm(conv_x), in_hbm(conv_bc)
    head_rate, skip = in_hbm(head_rate), in_hbm(skip)
    bias_x, bias_bc, gain = in_hbm(bias_x[None, :]), in_hbm(bias_bc[None, :]), in_hbm(norm_gain[None, :])

    swap = [(s, s ^ 1) for s in range(8)]
    w_sib = in_hbm(lax.ppermute(w_out, "tp", swap))
    taps = (conv_x, bias_x, conv_bc, bias_bc)
    buf = pltpu.VMEM
    msg, begun = pl.pallas_call(
        scan_in_body,
        in_specs=[SMEM] + [ANY] * 7,
        out_specs=[VMEM, VMEM],
        out_shape=[SD((CTX, 16, WID), BF), SD((8, HW), F32)],
        scratch_shapes=[
            buf((TOK, WID), BF), buf((TOK, 2 * ST), BF), buf((HEADS, TOK), jnp.int32), buf((4, WID), F32),
            buf((1, WID), F32), buf((4, 2 * ST), F32), buf((1, 2 * ST), F32), buf((TOK, WID), BF), buf((TOK, ST), F32),
            pltpu.SemaphoreType.DMA((2, 8)),
        ],
        compiler_params=params(0),
        name="scan_in",
    )(head_rate, x_in, bc_in, codes, *taps)
    got = lax.all_to_all(msg, "ctx", 0, 0, tiled=True)

    a1, a2, c_map = pl.pallas_call(
        local_body,
        grid=(1,),
        in_specs=[
            SMEM, SMEM, whole(TOK, WID), whole(TOK, WID), whole(HEADS, TOK), whole(TOK, 2 * ST), whole(4, WID),
            whole(1, WID), whole(4, 2 * ST), whole(1, 2 * ST), ANY,
        ],
        out_specs=[whole(TOK, WID), whole(TOK, WID), whole(TOK, ST)],
        out_shape=[pltpu.HBM((TOK, WID), BF), pltpu.HBM((TOK, WID), BF), pltpu.HBM((TOK, ST), BF)],
        scratch_shapes=[
            buf((TOK, TOK), BF), buf((TOK, WID), F32), buf((TOK, ST), BF), buf((TOK, WID), BF), buf((TOK, WID), BF),
        ],
        compiler_params=params(),
        name="local",
    )(head_rate, skip, x_in, z_in, codes, bc_in, *taps, begun)
    a1, a2, c_map = in_hbm(a1), in_hbm(a2), in_hbm(c_map)

    prefix = pl.pallas_call(
        prefix_body,
        in_specs=[SMEM, VMEM, VMEM, VMEM, ANY],
        out_specs=VMEM,
        out_shape=SD((CTX, 8, WID), BF),
        compiler_params=params(0),
        name="prefix",
    )(head_rate, conv_x, bias_x, got, a1)
    incoming = lax.all_to_all(prefix, "ctx", 0, 0, tiled=True)

    def fixed(*shape):
        return pl.BlockSpec(shape, lambda i, ix: (0,) * len(shape))

    far_own, token = pl.pallas_call(
        fetch_body,
        in_specs=[SMEM, ANY, ANY],
        out_specs=[VMEM, VMEM],
        out_shape=[SD((WID, WID), BF), SD((8, HW), F32)],
        scratch_shapes=[pltpu.SemaphoreType.DMA((1,))],
        compiler_params=params(0, 2),
        name="fetch",
    )(where, w_out, prefix)

    def project_far(own, sib):
        return pl.pallas_call(
            project_far_body,
            in_specs=[VMEM] * 4,
            out_specs=[VMEM, VMEM],
            out_shape=[SD((HT, HALF), BF)] * 2,
            compiler_params=params(0, 6),
            name="project_far",
        )(own, sib, far_own, far_sib)

    ctx = jnp.full((1,), lax.axis_index("ctx"), jnp.int32)
    a_first, c_first = pl.pallas_call(
        patch_body,
        out_shape=[SD((16, WID), BF), SD((16, ST), BF)],
        grid_spec=pltpu.PrefetchScalarGridSpec(
            num_scalar_prefetch=1,
            grid=(1,),
            in_specs=[
                SMEM, SMEM, pl.BlockSpec((1, 16, WID), lambda i, ix: (jnp.maximum(ix[0] - 1, 0), 0, 0)),
                fixed(16, WID), fixed(16, 2 * ST), fixed(16, WID), fixed(HEADS, HW), fixed(4, WID), fixed(1, WID),
                fixed(4, 2 * ST), fixed(1, 2 * ST), ANY,
            ],
            out_specs=[fixed(16, WID), fixed(16, ST)],
            scratch_shapes=[buf((24, WID), F32), buf((24, 2 * ST), F32)],
        ),
        compiler_params=params(1, 6),
        name="patch",
    )(ctx, head_rate, skip, got, x_in, bc_in, z_in, codes, *taps, token)

    def norm(half):
        outs = [SD((HT, WID), BF)] + ([] if half else [SD((WID, WID), BF)])
        return pl.pallas_call(
            functools.partial(norm_body, half),
            in_specs=[SMEM, VMEM] + [ANY] * 4 + [VMEM] * 2 + [ANY],
            out_specs=[VMEM] * len(outs),
            out_shape=outs,
            scratch_shapes=[
                buf((HT, WID), BF), buf((HT, WID), BF), buf((HT, ST), BF), buf((1, WID), F32), buf((HT, WID), F32),
                pltpu.SemaphoreType.DMA((5,)),
            ],
            compiler_params=params(0, 6),
            name="norm",
        )(where, incoming, a1, a2, c_map, gain, a_first, c_first, w_sib)

    up = [(s, (s + 2) % 8) for s in range(8)]
    down = [(s, (s + 6) % 8) for s in range(8)]
    n0, far_sib = norm(0)
    s0 = lax.ppermute(n0, "tp", swap)
    (n1,) = norm(1)
    s1 = lax.ppermute(n1, "tp", swap)
    fl0, fr0 = project_far(n0, s0)
    fl0, fr0 = lax.ppermute(fl0, "tp", up), lax.ppermute(fr0, "tp", down)
    fl1, fr1 = project_far(n1, s1)
    fl1, fr1 = lax.ppermute(fl1, "tp", up), lax.ppermute(fr1, "tp", down)
    run = functools.partial(project, where, (n0, n1), (s0, s1), w_out, w_sib)
    above_r, below_l = run(((1, 1), (3, 0)), ((), ()), BF)
    from_r, from_l = lax.ppermute(above_r, "tp", up), lax.ppermute(below_l, "tp", down)
    above_l, below_r = run(((1, 0), (3, 1)), ((fl0, fl1), (fr0, fr1)), BF)
    last_l, last_r = lax.ppermute(above_l, "tp", up), lax.ppermute(below_r, "tp", down)
    here_l, here_r = run(((0, 0), (0, 1)), ((from_l,), (from_r,)), F32)

    def final(side, here, last, *carry):
        return pl.pallas_call(
            functools.partial(final_body, side),
            in_specs=[VMEM, VMEM] + [ANY] * len(carry),
            out_specs=ANY,
            out_shape=SD((TOK, WID), BF),
            scratch_shapes=[buf((TOK, HALF), BF), pltpu.SemaphoreType.DMA((1,))],
            input_output_aliases={2: 0} if carry else {},
            compiler_params=params(0, 4),
            name="final",
        )(here, last, *carry)

    return final(1, here_r, last_r, final(0, here_l, last_l))


def solution(mesh):
    in_specs = (
        P("ctx", "tp"),
        P("ctx", None),
        P("ctx", "tp"),
        P("ctx", "tp"),
        P("tp"),
        P(None, "tp"),
        P(),
        P("tp"),
        P(),
        P("tp"),
        P("tp"),
        P("tp", None),
    )
    out_specs = P("ctx", "tp")
    return jax.shard_map(body, mesh=mesh, in_specs=in_specs, out_specs=out_specs, check_vma=False)
```
